32 devices in a mesh: dp: 2 (over x), seq: 4 (over z), mp: 4 (over y, core).
Axes of the slice: x: 2, y: 2, z: 4, core: 2. Of those that a mesh axis runs over, the one named last changes fastest.
Arguments:
- tokens: bfloat16 [2, 4096, 2048], P(None, ('dp', 'seq', 'mp')), may hold values from -6 to 6
- lengths: int32 [2, 2], P(None, 'dp'), may hold values from 256 to 2048, as said below
- cotangent: bfloat16 [2, 4096, 2048], P(None, ('dp', 'seq', 'mp')), may hold values from -6 to 6
- q_weight: bfloat16 [2048, 2048], P(None, 'mp'), may hold values from -0.125 to 0.125
- k_weight: bfloat16 [2048, 2048], P(None, 'mp'), may hold values from -0.125 to 0.125
- v_weight: bfloat16 [2048, 2048], P(None, 'mp'), may hold values from -0.125 to 0.125
- o_weight: bfloat16 [2048, 2048], P('mp'), may hold values from -0.125 to 0.125
- q_gain: float32 [2048], replicated, may hold values from 0.25 to 1.75
- k_gain: float32 [2048], replicated, may hold values from 0.25 to 1.75
- attn_gain: float32 [2048], replicated, may hold values from 0.25 to 1.75
- gate_weight: bfloat16 [2048, 8192], P(None, 'mp'), may hold values from -0.125 to 0.125
- up_weight: bfloat16 [2048, 8192], P(None, 'mp'), may hold values from -0.125 to 0.125
- down_weight: bfloat16 [8192, 2048], P('mp'), may hold values from -0.0625 to 0.0625
- mlp_gain: float32 [2048], replicated, may hold values from 0.25 to 1.75
Outputs:
- layer_out: bfloat16 [2, 4096, 2048], P(None, ('dp', 'seq', 'mp'))
- input_grad: float32 [2, 4096, 2048], P(None, ('dp', 'seq', 'mp'))
- q_weight_grad: float32 [2048, 2048], P(None, 'mp')
- k_weight_grad: float32 [2048, 2048], P(None, 'mp')
- v_weight_grad: float32 [2048, 2048], P(None, 'mp')
- o_weight_grad: float32 [2048, 2048], P('mp')
- q_gain_grad: float32 [2048], replicated
- k_gain_grad: float32 [2048], replicated
- attn_gain_grad: float32 [2048], replicated
- gate_weight_grad: float32 [2048, 8192], P(None, 'mp')
- up_weight_grad: float32 [2048, 8192], P(None, 'mp')
- down_weight_grad: float32 [8192, 2048], P('mp')
- mlp_gain_grad: float32 [2048], replicated
The draws below stay inside these ranges and needn't reach their ends.
Inputs may be any that keep to these rules, and one draw needn't show every extreme that they name: Each sequence has its live tokens first and padding after; lengths lean toward the short end, and in every draw one sequence is live in all 2048 positions.
All inputs are finite; a program needn't handle non-finite values.
Results may differ from the reference program's by a relative error of at most 0.038.
Values may be sent and summed in bfloat16 or wider, within the bound.
No kernel may reach another device: no remote copies, remote signals or barrier semaphores. Data moves between devices by JAX's collectives and lax.ppermute only.
A program may use at most 320 MiB of HBM per device.

```python
import jax
import jax.numpy as jnp
from jax import lax

D = 2048
HEADS = 16
HEAD_DIM = 128
FF = 8192
MICRO = 2
SEQ_LEN = 2048
TOKENS_MB = 4096
N_DP = 2


def draw_lengths(key, part):
    key_one, key_two, key_three, key_four = jax.random.split(key, 4)
    shortest = SEQ_LEN // 8
    pair_shape = (MICRO, N_DP)
    draw_one = jax.random.randint(key_one, pair_shape, shortest, SEQ_LEN + 1)
    draw_two = jax.random.randint(key_two, pair_shape, shortest, SEQ_LEN + 1)
    draw_three = jax.random.randint(key_three, pair_shape, shortest, SEQ_LEN + 1)
    lengths_base = jnp.minimum(jnp.minimum(draw_one, draw_two), draw_three)
    chosen = jax.random.randint(key_four, (), 0, MICRO * N_DP)
    slots = jnp.arange(MICRO * N_DP, dtype=jnp.int32).reshape(pair_shape)
    return jnp.where(slots == chosen, SEQ_LEN, lengths_base).astype(jnp.int32)


def levels(rng, dims, shards, smallest, top_value):
    gain, own = 1.0, jax.random.fold_in(rng, 6)
    for axis_at, blocks in shards:
        heights = jnp.exp(jax.random.uniform(jax.random.fold_in(own, axis_at), (blocks,), jnp.float32, smallest / len(shards), top_value / len(shards)))
        gain = gain * jnp.repeat(heights, dims[axis_at] // blocks).reshape([-1 if axis == axis_at else 1 for axis in range(len(dims))])
    return gain


def gaussian(own_key, extent, width, reach, cuts=(), kind=jnp.bfloat16):
    result = width * jax.random.normal(own_key, extent, jnp.float32)
    if cuts:
        result = result * levels(own_key, extent, cuts, -0.22, 0.18)
    return jnp.clip(result, -reach, reach).astype(kind)


def setup_inputs(seed: int = 0) -> dict:
    arg_keys = jax.random.split(jax.random.key(seed), 15)
    tokens = gaussian(arg_keys[0], (MICRO, TOKENS_MB, D), 1.0, 6.0, ((1, 32),))
    lengths = draw_lengths(jax.random.fold_in(arg_keys[14], 71), 0)
    cotangent = gaussian(arg_keys[2], (MICRO, TOKENS_MB, D), 1.0, 6.0, ((1, 32),))
    q_weight = gaussian(arg_keys[3], (D, D), D ** -0.5, 0.125, ((1, 4),))
    k_weight = gaussian(arg_keys[4], (D, D), D ** -0.5, 0.125, ((1, 4),))
    v_weight = gaussian(arg_keys[5], (D, D), D ** -0.5, 0.125, ((1, 4),))
    o_weight = gaussian(arg_keys[6], (D, D), D ** -0.5, 0.125, ((0, 4),))
    q_gain = jnp.clip(1.0 + 0.15 * jax.random.normal(arg_keys[7], (D,), jnp.float32), 0.25, 1.75)
    k_gain = jnp.clip(1.0 + 0.15 * jax.random.normal(arg_keys[8], (D,), jnp.float32), 0.25, 1.75)
    attn_gain = jnp.clip(1.0 + 0.15 * jax.random.normal(arg_keys[9], (D,), jnp.float32), 0.25, 1.75)
    gate_weight = gaussian(arg_keys[10], (D, FF), D ** -0.5, 0.125, ((1, 4),))
    up_weight = gaussian(arg_keys[11], (D, FF), D ** -0.5, 0.125, ((1, 4),))
    down_weight = gaussian(arg_keys[12], (FF, D), FF ** -0.5, 0.0625, ((0, 4),))
    mlp_gain = jnp.clip(1.0 + 0.15 * jax.random.normal(arg_keys[13], (D,), jnp.float32), 0.25, 1.75)
    return dict(tokens=tokens, lengths=lengths, cotangent=cotangent, q_weight=q_weight, k_weight=k_weight, v_weight=v_weight, o_weight=o_weight, q_gain=q_gain, k_gain=k_gain, attn_gain=attn_gain, gate_weight=gate_weight, up_weight=up_weight, down_weight=down_weight, mlp_gain=mlp_gain)


epsilon = 1e-06
rope_base = 500000.0

@jax.custom_vjp
def low(v):
    return lax.optimization_barrier(v.astype(jnp.bfloat16)).astype(jnp.float32)

@jax.custom_vjp
def low_back(v):
    return v

def low_keep(v):
    return (low(v), None)

def low_pass(kept, grad):
    return (grad,)

def back_keep(v):
    return (v, None)

def back_low(kept, grad):
    return (low(grad),)
low.defvjp(low_keep, low_pass)
low_back.defvjp(back_keep, back_low)

def rope_tables(seq_count, head_width):
    half_width = head_width // 2
    frequency = rope_base ** (-(jnp.arange(half_width, dtype=jnp.float32) * 2.0 / head_width))
    angles = jnp.arange(seq_count, dtype=jnp.float32)[:, None] * frequency[None, :]
    angles = jnp.concatenate([angles, angles], axis=1)
    return (jnp.cos(angles)[:, None, :], jnp.sin(angles)[:, None, :])

def rotate(vectors, rot_cos, rot_sin):
    half_width = vectors.shape[-1] // 2
    turned = jnp.concatenate([-vectors[..., half_width:], vectors[..., :half_width]], axis=-1)
    return vectors * rot_cos + turned * rot_sin

def rms_norm(vectors, gain_vec):
    return vectors * lax.rsqrt(lax.optimization_barrier(jnp.mean(vectors * vectors, axis=-1, keepdims=True)) + epsilon) * gain_vec

def matmul(left, right):
    return jnp.dot(left, right, precision=lax.Precision.HIGHEST, preferred_element_type=jnp.float32)

def sequence_forward(params, sequence, length):
    q_weight, k_weight, v_weight, o_weight, q_gain, k_gain, attn_gain, gate_weight, up_weight, down_weight, mlp_gain = params
    seq_count = sequence.shape[0]
    queries = rms_norm(low_back(matmul(sequence, q_weight)), q_gain)
    key_proj = rms_norm(low_back(matmul(sequence, k_weight)), k_gain)
    value_proj = low_back(low(matmul(sequence, v_weight)))
    rot_cos, rot_sin = rope_tables(seq_count, HEAD_DIM)
    queries = low_back(low(rotate(queries.reshape(seq_count, HEADS, HEAD_DIM), rot_cos, rot_sin)))
    key_proj = low_back(low(rotate(key_proj.reshape(seq_count, HEADS, HEAD_DIM), rot_cos, rot_sin)))
    value_proj = value_proj.reshape(seq_count, HEADS, HEAD_DIM)
    places = jnp.arange(seq_count, dtype=jnp.int32)
    allowed = (places[None, :] <= places[:, None]) & (places[None, :] < length)
    scaling = HEAD_DIM ** (-0.5)

    def one_head(operands):
        head_q, head_k, head_v = operands
        scores = low_back(jnp.dot(head_q, head_k.T, precision=lax.Precision.HIGHEST) * scaling)
        scores = jnp.where(allowed, scores, -1e+30)
        shifted = scores - lax.optimization_barrier(jnp.max(scores, axis=-1, keepdims=True))
        raised = jnp.where(allowed, jnp.exp(shifted), 0.0)
        probabilities = raised / lax.optimization_barrier(jnp.sum(raised, axis=-1, keepdims=True))
        return jnp.dot(low(probabilities), head_v, precision=lax.Precision.HIGHEST)
    mixed_heads = lax.map(jax.checkpoint(one_head), (jnp.swapaxes(queries, 0, 1), jnp.swapaxes(key_proj, 0, 1), jnp.swapaxes(value_proj, 0, 1)))
    mixed_heads = low_back(low(jnp.swapaxes(mixed_heads, 0, 1).reshape(seq_count, HEADS * HEAD_DIM)))
    attended = low_back(matmul(mixed_heads, o_weight))
    hidden = sequence + rms_norm(attended, attn_gain)
    hidden_low = low(hidden)
    gate_proj = low_back(matmul(hidden_low, gate_weight))
    up_proj = low_back(matmul(hidden_low, up_weight))
    activated = low(gate_proj * jax.nn.sigmoid(gate_proj) * up_proj)
    mlp_out = low_back(matmul(activated, down_weight))
    return hidden + rms_norm(mlp_out, mlp_gain)

def reference(tokens, lengths, cotangent, q_weight, k_weight, v_weight, o_weight, q_gain, k_gain, attn_gain, gate_weight, up_weight, down_weight, mlp_gain):
    params = (q_weight.astype(jnp.float32), k_weight.astype(jnp.float32), v_weight.astype(jnp.float32), o_weight.astype(jnp.float32), q_gain.astype(jnp.float32), k_gain.astype(jnp.float32), attn_gain.astype(jnp.float32), gate_weight.astype(jnp.float32), up_weight.astype(jnp.float32), down_weight.astype(jnp.float32), mlp_gain.astype(jnp.float32))
    group_count = MICRO * N_DP
    sequences = tokens.astype(jnp.float32).reshape(group_count, SEQ_LEN, D)
    group_lengths = lengths.reshape(group_count).astype(jnp.int32)

    def forward(weight_set, inputs):
        return lax.map(lambda operand_pair: sequence_forward(weight_set, operand_pair[0], operand_pair[1]), (inputs, group_lengths))
    outputs, pullback = jax.vjp(forward, params, sequences)
    places = jnp.arange(SEQ_LEN, dtype=jnp.int32)
    live_rows = (places[None, :] < group_lengths[:, None]).astype(jnp.float32)
    seeds = cotangent.astype(jnp.float32).reshape(group_count, SEQ_LEN, D) * live_rows[:, :, None]
    weight_grads, input_grads = pullback(seeds)
    return (outputs.reshape(MICRO, N_DP * SEQ_LEN, D).astype(jnp.bfloat16), input_grads.reshape(MICRO, N_DP * SEQ_LEN, D), weight_grads[0], weight_grads[1], weight_grads[2], weight_grads[3], weight_grads[4], weight_grads[5], weight_grads[6], weight_grads[7], weight_grads[8], weight_grads[9], weight_grads[10])
```

```python
import functools

import jax
import jax.numpy as jnp
from jax import lax
from jax.experimental import pallas as pl
from jax.experimental.pallas import tpu as pltpu
from jax.sharding import PartitionSpec as P

HEAD_DIM = 128
HALF = HEAD_DIM // 2
epsilon = 1e-06
rope_base = 500000.0
masked_score = -1e30
LOG2E = 1.4426950408889634
TILE = 256

f32 = jnp.float32
bf16 = jnp.bfloat16


def add_low(a, b):
    return (a.astype(f32) + b.astype(f32)).astype(bf16)


def bits_of(n):
    out = []
    b = 1
    while b < n:
        out.append(b)
        b *= 2
    return out


def xor_perm(n, b):
    return [(i, i ^ b) for i in range(n)]


def row_masks(n):
    masks = [0]
    for b in reversed(bits_of(n)):
        masks = masks + [m | b for m in masks]
    return masks


def inv_rms(v):
    return lax.rsqrt(jnp.mean(v * v, axis=-1, keepdims=True) + epsilon)


def norm_backward(source, inverse, gain_vec, upstream):
    normed = source * inverse
    weighted = upstream * gain_vec
    back = inverse * (weighted - normed * jnp.mean(weighted * normed, axis=-1, keepdims=True))
    return back, upstream * normed


def dot_t(a, b):
    return lax.dot_general(a, b, (((0,), (0,)), ((), ())), preferred_element_type=f32)


def dot_nt(a, b):
    return lax.dot_general(a, b, (((1,), (1,)), ((), ())), preferred_element_type=f32)


def dot(a, b):
    return jnp.dot(a, b, preferred_element_type=f32)


def rope_kernel(slots, width, local, z_ref, proj, inv, cos, sin, qg, kg, *outs):
    z = z_ref[0]
    c, s = cos[...], sin[...]
    for j in range(slots):
        base = (z ^ j) * width if slots > 1 else 0
        for h in range(width // HEAD_DIM):
            at = base + h * HEAD_DIM
            at = pl.multiple_of(at, HEAD_DIM) if slots > 1 else at
            for part, gain in ((0, qg), (1, kg)):
                raw = proj[:, pl.ds(part * local + at, HEAD_DIM)]
                v = raw * inv[:, part : part + 1] * gain[:, pl.ds(at, HEAD_DIM)]
                v = v * c + pltpu.roll(v, HALF, 1) * s
                lo = part * width + h * HEAD_DIM
                outs[j][:, lo : lo + HEAD_DIM] = v.astype(bf16)
            lo = 2 * width + h * HEAD_DIM
            outs[j][:, lo : lo + HEAD_DIM] = proj[:, pl.ds(2 * local + at, HEAD_DIM)].astype(bf16)


def rope_call(slots, z, proj, inv, cos, sin, qg, kg):
    rows, local = proj.shape[0], proj.shape[1] // 3
    width = local // slots
    blk = min(rows, 256)
    row = lambda n: pl.BlockSpec((blk, n), lambda i, *_: (i, 0))
    vec = pl.BlockSpec((1, local), lambda i, *_: (0, 0))
    return pl.pallas_call(
        functools.partial(rope_kernel, slots, width, local),
        out_shape=[jax.ShapeDtypeStruct((rows, 3 * width), bf16)] * slots,
        grid_spec=pltpu.PrefetchScalarGridSpec(
            num_scalar_prefetch=1,
            grid=(rows // blk,),
            in_specs=[row(3 * local), row(2), row(HEAD_DIM), row(HEAD_DIM), vec, vec],
            out_specs=[row(3 * width)] * slots,
        ),
        cost_estimate=pl.CostEstimate(
            flops=rows * local * 12, bytes_accessed=rows * local * 18, transcendentals=0
        ),
        name="rope_rows",
    )(z, proj, inv, cos, sin, qg, kg)


def unrope(grad, c, s):
    g = grad.astype(f32)
    return g * c - pltpu.roll(g, HALF, 1) * s


def cross_kernel(slots, width, local, z_ref, *refs):
    grads = refs[:slots]
    proj, inv, cos, sin, qg, kg, cross, gains = refs[slots:]
    z = z_ref[0]
    c, s = cos[...], sin[...]

    @pl.when(pl.program_id(0) == 0)
    def _():
        gains[...] = jnp.zeros_like(gains)

    for part, gain in ((0, qg), (1, kg)):
        total = None
        for j in range(slots):
            base = (z ^ j) * width if slots > 1 else 0
            for h in range(width // HEAD_DIM):
                at = base + h * HEAD_DIM
                at = pl.multiple_of(at, HEAD_DIM) if slots > 1 else at
                lo = part * width + h * HEAD_DIM
                g = unrope(grads[j][:, lo : lo + HEAD_DIM], c, s)
                gr = g * proj[:, pl.ds(part * local + at, HEAD_DIM)]
                w = gr * gain[:, pl.ds(at, HEAD_DIM)]
                total = w if total is None else total + w
                col = jnp.sum(gr * inv[:, part : part + 1], axis=0, keepdims=True)
                gains[part : part + 1, pl.ds(at, HEAD_DIM)] += col
        cross[:, part : part + 1] = jnp.sum(total, axis=1, keepdims=True)


def raw_kernel(slots, width, local, d, z_ref, *refs):
    grads = refs[:slots]
    proj, inv, cross, cos, sin, qg, kg, out = refs[slots:]
    z = z_ref[0]
    c, s = cos[...], sin[...]
    for j in range(slots):
        base = (z ^ j) * width if slots > 1 else 0
        for h in range(width // HEAD_DIM):
            at = base + h * HEAD_DIM
            at = pl.multiple_of(at, HEAD_DIM) if slots > 1 else at
            for part, gain in ((0, qg), (1, kg)):
                lo = part * width + h * HEAD_DIM
                g = unrope(grads[j][:, lo : lo + HEAD_DIM], c, s)
                r = inv[:, part : part + 1]
                w = g * gain[:, pl.ds(at, HEAD_DIM)] * r
                k = r * r * r * (cross[:, part : part + 1] * (1.0 / d))
                w = w - proj[:, pl.ds(part * local + at, HEAD_DIM)] * k
                out[:, pl.ds(part * local + at, HEAD_DIM)] = w.astype(bf16)
            lo = 2 * width + h * HEAD_DIM
            out[:, pl.ds(2 * local + at, HEAD_DIM)] = grads[j][:, lo : lo + HEAD_DIM]


def cross_call(slots, m, z, grads, proj, inv, cos, sin, qg, kg):
    rows, local = proj.shape[0], proj.shape[1] // 3
    width = local // slots
    blk = min(rows, 256)
    far = lambda n: pl.BlockSpec((blk, n), lambda i, *_: (i + m * (rows // blk), 0))
    row = lambda n: pl.BlockSpec((blk, n), lambda i, *_: (i, 0))
    vec = pl.BlockSpec((1, local), lambda i, *_: (0, 0))
    return pl.pallas_call(
        functools.partial(cross_kernel, slots, width, local),
        out_shape=[
            jax.ShapeDtypeStruct((rows, 2), f32),
            jax.ShapeDtypeStruct((2, local), f32),
        ],
        grid_spec=pltpu.PrefetchScalarGridSpec(
            num_scalar_prefetch=1,
            grid=(rows // blk,),
            in_specs=[far(3 * width)] * slots
            + [row(3 * local), row(2), row(HEAD_DIM), row(HEAD_DIM), vec, vec],
            out_specs=[row(2), pl.BlockSpec((2, local), lambda i, *_: (0, 0))],
        ),
        cost_estimate=pl.CostEstimate(
            flops=rows * local * 20, bytes_accessed=rows * local * 18, transcendentals=0
        ),
        name="norm_cross",
    )(z, *grads, proj, inv, cos, sin, qg, kg)


def raw_call(slots, d, m, z, grads, proj, inv, cross, cos, sin, qg, kg):
    rows, local = proj.shape[0], proj.shape[1] // 3
    width = local // slots
    blk = min(rows, 256)
    far = lambda n: pl.BlockSpec((blk, n), lambda i, *_: (i + m * (rows // blk), 0))
    row = lambda n: pl.BlockSpec((blk, n), lambda i, *_: (i, 0))
    vec = pl.BlockSpec((1, local), lambda i, *_: (0, 0))
    return pl.pallas_call(
        functools.partial(raw_kernel, slots, width, local, d),
        out_shape=jax.ShapeDtypeStruct((rows, 3 * local), bf16),
        grid_spec=pltpu.PrefetchScalarGridSpec(
            num_scalar_prefetch=1,
            grid=(rows // blk,),
            in_specs=[far(3 * width)] * slots
            + [row(3 * local), row(2), row(2), row(HEAD_DIM), row(HEAD_DIM), vec, vec],
            out_specs=row(3 * local),
        ),
        cost_estimate=pl.CostEstimate(
            flops=rows * local * 20, bytes_accessed=rows * local * 24, transcendentals=0
        ),
        name="raw_grads",
    )(z, *grads, proj, inv, cross, cos, sin, qg, kg)


def join_kernel(slots, width, z_ref, *refs):
    z = z_ref[0]
    out = refs[slots]
    for j in range(slots):
        out[:, pl.ds(pl.multiple_of((z ^ j) * width, HEAD_DIM), width)] = refs[j][...]


def join_heads(z, pieces):
    rows, width = pieces[0].shape
    slots = len(pieces)
    blk = min(rows, 256)
    return pl.pallas_call(
        functools.partial(join_kernel, slots, width),
        out_shape=jax.ShapeDtypeStruct((rows, slots * width), bf16),
        grid_spec=pltpu.PrefetchScalarGridSpec(
            num_scalar_prefetch=1,
            grid=(rows // blk,),
            in_specs=[pl.BlockSpec((blk, width), lambda i, *_: (i, 0))] * slots,
            out_specs=pl.BlockSpec((blk, slots * width), lambda i, *_: (i, 0)),
        ),
        name="join_heads",
    )(z, *pieces)


def split_kernel(slots, width, z_ref, x, *outs):
    z = z_ref[0]
    for j in range(slots):
        outs[j][...] = x[:, pl.ds(pl.multiple_of((z ^ j) * width, HEAD_DIM), width)]


def split_heads(z, x, slots):
    rows, local = x.shape
    width = local // slots
    blk = min(rows, 256)
    return pl.pallas_call(
        functools.partial(split_kernel, slots, width),
        out_shape=[jax.ShapeDtypeStruct((rows, width), bf16)] * slots,
        grid_spec=pltpu.PrefetchScalarGridSpec(
            num_scalar_prefetch=1,
            grid=(rows // blk,),
            in_specs=[pl.BlockSpec((blk, local), lambda i, *_: (i, 0))],
            out_specs=[pl.BlockSpec((blk, width), lambda i, *_: (i, 0))] * slots,
        ),
        name="split_heads",
    )(z, x)


def exchange(pieces, n):
    return [p if j == 0 else lax.ppermute(p, "seq", xor_perm(n, j)) for j, p in enumerate(pieces)]


def row_places(slots, masks, rows, z, me):
    count = rows // len(masks)
    for j in range(slots):
        for k, m in enumerate(masks):
            yield j, k * count, pl.multiple_of((z ^ j) * rows + (me ^ m) * count, count), count


def key_bias(total, length):
    pos = lax.broadcasted_iota(jnp.int32, (1, total), 1)
    return jnp.where(pos < length, 0.0, masked_score).astype(f32)


def diag_mask(size):
    r = lax.broadcasted_iota(jnp.int32, (size, size), 0)
    c = lax.broadcasted_iota(jnp.int32, (size, size), 1)
    return c <= r


def attend_kernel(slots, masks, rows, blk, scal, *refs):
    pieces, outs = refs[:slots], refs[slots : 2 * slots]
    o32, lse, qkv, o16, sem = refs[2 * slots :]
    z, me, length = scal[0], scal[1], scal[2]
    total = slots * rows
    copies = []
    for t, (j, at, to, n) in enumerate(row_places(slots, masks, rows, z, me)):
        cp = pltpu.make_async_copy(pieces[j].at[pl.ds(at, n)], qkv.at[pl.ds(to, n)], sem.at[t])
        cp.start()
        copies.append(cp)
    bias = key_bias(total, length)
    causal = diag_mask(blk)
    for cp in copies:
        cp.wait()
    factor = HEAD_DIM**-0.5 * LOG2E
    for i in range(total // blk):
        lo = i * blk
        q = qkv[lo : lo + blk, :HEAD_DIM]
        s = dot_nt(q, qkv[lo : lo + blk, HEAD_DIM : 2 * HEAD_DIM]) * factor
        s = jnp.where(causal, s + bias[:, lo : lo + blk], masked_score)
        top = jnp.max(s, axis=1, keepdims=True)
        if i:
            before = dot_nt(q, qkv[:lo, HEAD_DIM : 2 * HEAD_DIM]) * factor + bias[:, :lo]
            top = jnp.maximum(top, jnp.max(before, axis=1, keepdims=True))
        p = jnp.exp2(s - top)
        mass = jnp.sum(p, axis=1, keepdims=True)
        acc = dot(p.astype(bf16), qkv[lo : lo + blk, 2 * HEAD_DIM :])
        if i:
            p = jnp.exp2(before - top)
            mass = mass + jnp.sum(p, axis=1, keepdims=True)
            acc = acc + dot(p.astype(bf16), qkv[:lo, 2 * HEAD_DIM :])
        acc = acc / mass
        o32[lo : lo + blk, :] = acc
        o16[lo : lo + blk, :] = acc.astype(bf16)
        lse[lo : lo + blk, :] = top + jnp.log(mass) * LOG2E
    copies = []
    for t, (j, at, to, n) in enumerate(row_places(slots, masks, rows, z, me)):
        cp = pltpu.make_async_copy(o16.at[pl.ds(to, n)], outs[j].at[pl.ds(at, n)], sem.at[t])
        cp.start()
        copies.append(cp)
    for cp in copies:
        cp.wait()


def attend(scal, pieces, masks):
    slots = len(pieces)
    rows = pieces[0].shape[0]
    total = slots * rows
    hbm = pl.BlockSpec(memory_space=pl.ANY)
    vmem = pl.BlockSpec(memory_space=pltpu.VMEM)
    out = pl.pallas_call(
        functools.partial(attend_kernel, slots, masks, rows, 256),
        out_shape=[jax.ShapeDtypeStruct((rows, HEAD_DIM), bf16)] * slots
        + [
            jax.ShapeDtypeStruct((total, HEAD_DIM), f32),
            jax.ShapeDtypeStruct((total, 1), f32),
        ],
        in_specs=[pl.BlockSpec(memory_space=pltpu.SMEM)] + [hbm] * slots,
        out_specs=[hbm] * slots + [vmem, vmem],
        scratch_shapes=[
            pltpu.VMEM((total, 3 * HEAD_DIM), bf16),
            pltpu.VMEM((total, HEAD_DIM), bf16),
            pltpu.SemaphoreType.DMA((slots * len(masks),)),
        ],
        cost_estimate=pl.CostEstimate(
            flops=total * total * HEAD_DIM * 4,
            bytes_accessed=total * HEAD_DIM * 12,
            transcendentals=total * total // 2,
        ),
        name="attend",
    )(scal, *pieces)
    return out[:slots], (out[slots], out[slots + 1])


def attend_back_kernel(slots, masks, rows, blk, micros, scal, *refs):
    pieces = [refs[m * slots : (m + 1) * slots] for m in range(micros)]
    refs = refs[micros * slots :]
    kept = [refs[2 * m : 2 * m + 2] for m in range(micros)]
    dos, outs = refs[2 * micros : 2 * micros + slots], refs[2 * micros + slots :][:slots]
    qkv, do, o32, lse, dkv, grad, sem = refs[2 * micros + 2 * slots :]
    micro = pl.program_id(0)
    z, me, length = scal[0], scal[1], scal[2 + micro]
    total = slots * rows
    runs = slots * len(masks)
    places = list(row_places(slots, masks, rows, z, me))
    base = micro * rows

    def incoming(m):
        out = []
        for t, (j, at, to, n) in enumerate(places):
            from_, to_ = pl.ds(at, n), pl.ds(to, n)
            out.append(pltpu.make_async_copy(pieces[m][j].at[from_], qkv.at[to_], sem.at[t]))
            far = pl.ds(pl.multiple_of(base + at, n), n)
            out.append(pltpu.make_async_copy(dos[j].at[far], do.at[to_], sem.at[runs + t]))
        out.append(pltpu.make_async_copy(kept[m][0], o32, sem.at[2 * runs]))
        out.append(pltpu.make_async_copy(kept[m][1], lse, sem.at[2 * runs + 1]))
        return out

    for m in range(micros):

        @pl.when(micro == m)
        def _(m=m):
            copies = incoming(m)
            for cp in copies:
                cp.start()
            for cp in copies:
                cp.wait()

    bias = key_bias(total, length)
    causal = diag_mask(blk)
    dkv[...] = jnp.zeros_like(dkv)
    scale = HEAD_DIM**-0.5
    factor = scale * LOG2E
    D = HEAD_DIM
    for i in range(total // blk):
        lo = i * blk
        q, dy = qkv[lo : lo + blk, :D], do[lo : lo + blk, :]
        delta = jnp.sum(dy.astype(f32) * o32[lo : lo + blk, :], axis=1, keepdims=True)
        level = lse[lo : lo + blk, :]
        dq = None
        for start, stop in ((lo, lo + blk), (0, lo)):
            if start == stop:
                continue
            keys, vals = qkv[start:stop, D : 2 * D], qkv[start:stop, 2 * D :]
            s = dot_nt(q, keys) * factor + bias[:, start:stop]
            if start == lo:
                s = jnp.where(causal, s, masked_score)
            p = jnp.exp2(s - level)
            ds = (p * (dot_nt(dy, vals) - delta)).astype(bf16)
            part = dot(ds, keys)
            dq = part if dq is None else dq + part
            dkv[start:stop, :D] += dot_t(ds, q)
            dkv[start:stop, D:] += dot_t(p.astype(bf16), dy)
        grad[lo : lo + blk, :D] = (dq * scale).astype(bf16)
    grad[:, D : 2 * D] = (dkv[:, :D] * scale).astype(bf16)
    grad[:, 2 * D :] = dkv[:, D:].astype(bf16)
    copies = []
    for t, (j, at, to, n) in enumerate(places):
        far = pl.ds(pl.multiple_of(base + at, n), n)
        cp = pltpu.make_async_copy(grad.at[pl.ds(to, n)], outs[j].at[far], sem.at[t])
        cp.start()
        copies.append(cp)
    for cp in copies:
        cp.wait()


def attend_back(scal, pieces, kept, dos, masks):
    micros, slots = len(pieces), len(dos)
    rows = dos[0].shape[0] // micros
    total = slots * rows
    hbm = pl.BlockSpec(memory_space=pl.ANY)
    return pl.pallas_call(
        functools.partial(attend_back_kernel, slots, masks, rows, 256, micros),
        out_shape=[jax.ShapeDtypeStruct((micros * rows, 3 * HEAD_DIM), bf16)] * slots,
        grid=(micros,),
        in_specs=[pl.BlockSpec(memory_space=pltpu.SMEM)] + [hbm] * ((micros + 1) * slots + 2 * micros),
        out_specs=[hbm] * slots,
        scratch_shapes=[
            pltpu.VMEM((total, 3 * HEAD_DIM), bf16),
            pltpu.VMEM((total, HEAD_DIM), bf16),
            pltpu.VMEM((total, HEAD_DIM), f32),
            pltpu.VMEM((total, 1), f32),
            pltpu.VMEM((total, 2 * HEAD_DIM), f32),
            pltpu.VMEM((total, 3 * HEAD_DIM), bf16),
            pltpu.SemaphoreType.DMA((2 * slots * len(masks) + 2,)),
        ],
        cost_estimate=pl.CostEstimate(
            flops=micros * total * total * HEAD_DIM * 10,
            bytes_accessed=micros * total * HEAD_DIM * 24,
            transcendentals=micros * total * total // 2,
        ),
        name="attend_back",
    )(scal, *[p for ps in pieces for p in ps], *[k for ks in kept for k in ks], *dos)


def mlp_back_kernel(n, *refs):
    grads, dw, gates, ups = refs[: 2 * n], refs[2 * n], refs[2 * n + 1 :][:n], refs[3 * n + 1 :][:n]
    tok, outs, tok_out = refs[4 * n + 1], refs[4 * n + 2 : 6 * n + 2], refs[6 * n + 2]
    w = dw[...]
    half = grads[0].shape[0]
    for i, x in enumerate(grads):
        m, t = i // 2, slice(i % 2 * half, (i % 2 + 1) * half)
        a = dot_nt(x[...], w)
        g, u = gates[m][t, :], ups[m][t, :]
        s = jax.nn.sigmoid(g)
        outs[m][t, :] = (a * u * s * (1.0 + g * (1.0 - s))).astype(bf16)
        outs[n + m][t, :] = (a * g * s).astype(bf16)
    tok_out[0] = tok[0]


def mlp_back(line, grads, down_weight, gates, ups):
    n = len(gates)
    half, width = grads[0].shape
    rows = 2 * half
    ff = down_weight.shape[0]
    t = min(ff, 256)
    tall = pl.BlockSpec((rows, t), lambda i: (0, i))
    smem = pl.BlockSpec(memory_space=pltpu.SMEM)
    full = jax.ShapeDtypeStruct((rows, ff), bf16)
    *out, line.token = pl.pallas_call(
        functools.partial(mlp_back_kernel, n),
        out_shape=[full] * (2 * n) + [jax.ShapeDtypeStruct((1,), jnp.int32)],
        grid=(ff // t,),
        in_specs=[pl.BlockSpec((half, width), lambda i: (0, 0))] * (2 * n)
        + [pl.BlockSpec((t, width), lambda i: (i, 0))]
        + [tall] * (2 * n)
        + [smem],
        out_specs=[tall] * (2 * n) + [smem],
        cost_estimate=pl.CostEstimate(
            flops=2 * n * rows * width * ff,
            bytes_accessed=2 * width * ff + n * (2 * rows * width + 12 * rows * ff),
            transcendentals=n * rows * ff,
        ),
        name="mlp_back",
    )(*grads, down_weight, *gates, *ups, line.token)
    return out[:n], out[n:]


def hidden_back_kernel(n, *refs):
    gate_grads, gw, up_grads, uw = refs[:n], refs[n], refs[n + 1 : 2 * n + 1], refs[2 * n + 1]
    tok, outs, tok_out = refs[2 * n + 2], refs[2 * n + 3 : 3 * n + 3], refs[3 * n + 3]
    g, u = gw[...], uw[...]
    for m in range(n):
        outs[m][...] = (dot_nt(gate_grads[m][...], g) + dot_nt(up_grads[m][...], u)).astype(bf16)
    tok_out[0] = tok[0]


def hidden_back(line, gate_grads, gate_weight, up_grads, up_weight):
    n = len(gate_grads)
    rows, ff = gate_grads[0].shape
    width = gate_weight.shape[0]
    t = min(width, 256)
    all_ = pl.BlockSpec((rows, ff), lambda i: (0, 0), pipeline_mode=pl.Buffered(1))
    tile = pl.BlockSpec((t, ff), lambda i: (i, 0))
    smem = pl.BlockSpec(memory_space=pltpu.SMEM)
    *out, line.token = pl.pallas_call(
        functools.partial(hidden_back_kernel, n),
        out_shape=[jax.ShapeDtypeStruct((rows, width), bf16)] * n
        + [jax.ShapeDtypeStruct((1,), jnp.int32)],
        grid=(width // t,),
        in_specs=[all_] * n + [tile] + [all_] * n + [tile, smem],
        out_specs=[pl.BlockSpec((rows, t), lambda i: (0, i))] * n + [smem],
        cost_estimate=pl.CostEstimate(
            flops=4 * n * rows * width * ff,
            bytes_accessed=4 * width * ff + n * (4 * rows * ff + 2 * rows * width),
            transcendentals=0,
        ),
        name="hidden_back",
    )(*gate_grads, gate_weight, *up_grads, up_weight, line.token)
    return out


def turn_kernel(n, *refs):
    out, tok_out = refs[n + 1 :]
    at = 0
    for x in refs[:n]:
        out[:, at : at + x.shape[0]] = x[...].T
        at += x.shape[0]
    tok_out[0] = refs[n][0]


def turn(line, pieces, m=0, count=1):
    counts = [x.shape[0] // count for x in pieces]
    rows, cols = sum(counts), pieces[0].shape[1]
    t = min(cols, 512)
    smem = pl.BlockSpec(memory_space=pltpu.SMEM)
    out, line.token = pl.pallas_call(
        functools.partial(turn_kernel, len(pieces)),
        out_shape=[
            jax.ShapeDtypeStruct((cols, rows), pieces[0].dtype),
            jax.ShapeDtypeStruct((1,), jnp.int32),
        ],
        grid=(cols // t,),
        in_specs=[pl.BlockSpec((n, t), lambda i: (m, i)) for n in counts] + [smem],
        out_specs=[pl.BlockSpec((t, rows), lambda i: (i, 0)), smem],
        cost_estimate=pl.CostEstimate(flops=0, bytes_accessed=4 * rows * cols, transcendentals=0),
        name="turn",
    )(*pieces, line.token)
    return out


def gathered_attend(piece, pos, length):
    rows, local = piece.shape[0], piece.shape[1] // 3
    heads = local // HEAD_DIM
    q = piece[:, :local].reshape(rows, heads, HEAD_DIM)
    kv = lax.all_gather(piece[:, local:], "seq", axis=0, tiled=True)
    n = kv.shape[0]
    k = kv[:, :local].reshape(n, heads, HEAD_DIM)
    v = kv[:, local:].reshape(n, heads, HEAD_DIM)
    base = jnp.arange(n // rows, dtype=jnp.int32) * rows
    own = pos - lax.axis_index("seq") * rows
    key_pos = (base[:, None] + own[None, :]).reshape(n)
    allowed = (key_pos[None, :] <= pos[:, None]) & (key_pos[None, :] < length)
    allowed = allowed[:, None, :]
    s = jnp.einsum("shd,khd->shk", q, k, preferred_element_type=f32) * HEAD_DIM**-0.5
    s = jnp.where(allowed, s, masked_score)
    top = jnp.max(s, axis=-1, keepdims=True)
    w = jnp.where(allowed, jnp.exp(s - top), 0.0)
    mass = jnp.sum(w, axis=-1, keepdims=True)
    mixed = jnp.einsum("shk,khd->shd", w.astype(bf16), v, preferred_element_type=f32) / mass
    return mixed.reshape(rows, local).astype(bf16), (q, k, v, allowed, mixed, top + jnp.log(mass))


def gathered_back(kept, dy):
    q, k, v, allowed, mixed, level = kept
    rows, heads, _ = q.shape
    n = k.shape[0]
    dy = dy.reshape(rows, heads, HEAD_DIM)
    scale = HEAD_DIM**-0.5
    delta = jnp.sum(dy.astype(f32) * mixed, axis=-1, keepdims=True)
    s = jnp.einsum("shd,khd->shk", q, k, preferred_element_type=f32) * scale
    p = jnp.where(allowed, jnp.exp(s - level), 0.0)
    dp = jnp.einsum("shd,khd->shk", dy, v, preferred_element_type=f32)
    ds = (p * (dp - delta)).astype(bf16)
    dq = jnp.einsum("shk,khd->shd", ds, k, preferred_element_type=f32) * scale
    dk = jnp.einsum("shk,shd->khd", ds, q, preferred_element_type=f32) * scale
    dv = jnp.einsum("shk,shd->khd", p.astype(bf16), dy, preferred_element_type=f32)
    local = heads * HEAD_DIM
    dkv = jnp.concatenate([dk.reshape(n, local), dv.reshape(n, local)], axis=1).astype(bf16)
    dkv = lax.psum_scatter(dkv, "seq", scatter_dimension=0, tiled=True)
    return jnp.concatenate([dq.reshape(rows, local).astype(bf16), dkv.astype(bf16)], axis=1)


class Line:
    def __init__(self, token):
        self.token = token
        self.waits = {}

    def add(self, *tasks):
        for t in tasks:
            self.waits[t] = next(t)[0]

    def mark(self, *arrays):
        for x in arrays:
            x = lax.slice(x, (0,) * x.ndim, (1,) * x.ndim).reshape(1)
            self.token = self.token + (x.astype(f32) > 3.4e38).astype(jnp.int32)

    def step(self, *tasks):
        tasks = [t for t in tasks if t in self.waits]
        if not tasks:
            return []
        held = [self.waits.pop(t) for t in tasks]
        if jax.tree.leaves(held):
            held, self.token = lax.optimization_barrier((held, self.token))
        for t, v in zip(tasks, held):
            try:
                self.waits[t], out = t.send(v)
            except StopIteration as end:
                out = end.value
            self.mark(*jax.tree.leaves(out)[:1])
        return [t for t in tasks if t in self.waits]


def idle(n):
    for _ in range(n):
        yield (), ()


class Place:
    def __init__(self, n_seq):
        self.n = n_seq
        self.dp, self.z = lax.axis_index("dp"), lax.axis_index("seq")
        self.swap = [(0, 1), (1, 0)]
        self.lo, self.hi = n_seq // 2 - 1, n_seq // 2
        self.mid = [(self.lo, self.hi), (self.hi, self.lo)]
        self.inward = [
            [(i, i + 1), (n_seq - 1 - i, n_seq - 2 - i)] for i in range(n_seq // 2 - 1)
        ]

    def ends(self, pairs):
        return functools.reduce(jnp.logical_or, [self.z == b for _, b in pairs])


def take_half(x, dp, own):
    half = x.shape[1] // 2
    return lax.dynamic_slice_in_dim(x, (dp if own else 1 - dp) * half, half, 1)


def task_a(at, outs, which, x_send, x_keep, grad, cols, out_col):
    half = x_keep.shape[1]
    g = (yield grad, ())[:, cols]
    send = dot_t(x_send, g).astype(bf16)
    got = yield lax.ppermute(send, "dp", at.swap), send
    s = (dot_t(x_keep, g) + got.astype(f32)).astype(bf16)
    for pairs in at.inward:
        got = yield lax.ppermute(s, "seq", pairs), s
        s = add_low(s, got)
    got = yield lax.ppermute(s, "seq", at.mid), s
    s = add_low(s, got)
    for pairs in reversed(at.inward):
        pairs = [(b, a) for a, b in pairs]
        got = yield lax.ppermute(s, "seq", pairs), s
        s = jnp.where(at.ends(pairs), got, s)
    outs[which] = lax.dynamic_update_slice(outs[which], s.astype(f32), (at.dp * half, out_col))
    got = yield lax.ppermute(s, "dp", at.swap), s
    outs[which] = lax.dynamic_update_slice(
        outs[which], got.astype(f32), ((1 - at.dp) * half, out_col)
    )
    return ()


def task_b(at, outs, which, x, grad, cols, out_col):
    g = (yield grad, ())[:, cols]
    s = dot_t(x, g).astype(bf16)
    for pairs in at.inward:
        got = yield lax.ppermute(s, "seq", pairs), s
        s = add_low(s, got)
    h = s.shape[1] // 2
    first = at.z == at.lo
    send = jnp.where(first, s[:, h:], s[:, :h])
    keep = jnp.where(first, s[:, :h], s[:, h:])
    got = yield lax.ppermute(send, "seq", at.mid), (send, keep)
    keep = add_low(keep, got)
    n = at.n
    pairs = [(d * n + k, (1 - d) * n + k) for d in (0, 1) for k in (at.lo, at.hi)]
    got = yield lax.ppermute(keep, ("dp", "seq"), pairs), keep
    keep = add_low(keep, got)
    got = yield lax.ppermute(keep, "seq", at.mid), keep
    s = jnp.concatenate([jnp.where(first, keep, got), jnp.where(first, got, keep)], axis=1)
    for pairs in reversed(at.inward):
        pairs = [(b, a) for a, b in pairs]
        got = yield lax.ppermute(s, "seq", pairs), s
        s = jnp.where(at.ends(pairs), got, s)
    outs[which] = lax.dynamic_update_slice(outs[which], s.astype(f32), (0, out_col))
    return None


class Round:
    def __init__(self):
        self.refs, self.loads, self.keys = [], {}, {}

    def ref(self, array):
        for i, r in enumerate(self.refs):
            if r is array:
                return i
        self.refs.append(array)
        return len(self.refs) - 1

    def load(self, name, array, rows, cols=None):
        cols = (0, array.shape[1]) if cols is None else cols
        self.loads[name] = ((rows[1], cols[1]), ((self.ref(array), rows, cols, 0, 0),))

    def load_down(self, name, arrays, cols):
        n = arrays[0].shape[0]
        parts = tuple((self.ref(x), (0, n), cols, i * n, 0) for i, x in enumerate(arrays))
        self.loads[name] = ((n * len(arrays), cols[1]), parts)

    def load_across(self, name, arrays, rows):
        n = arrays[0].shape[1]
        parts = tuple((self.ref(x), rows, (0, n), 0, i * n) for i, x in enumerate(arrays))
        self.loads[name] = ((rows[1], n * len(arrays)), parts)


def first_row(first, count, dp):
    if isinstance(first, int):
        return first
    return pl.multiple_of((dp if first == "own" else 1 - dp) * count, count)


def round_kernel(kind, loads, n_in, pieces, extras, stores, scal, tok, *refs):
    ins = refs[:n_in]
    outs = refs[n_in + 1 : n_in + 1 + bool(pieces) + bool(extras) + len(stores)]
    refs[n_in][0] = tok[0]
    scratch = refs[n_in + 1 + len(outs) :]
    bufs = dict(zip([l[0] for l in loads], scratch))
    rest = list(scratch[len(loads) :])
    out_bufs = {}
    for name, _ in pieces + extras:
        out_bufs[name] = rest.pop(0)
    f_bufs = [rest.pop(0) for _ in stores]
    in_sem, out_sem = rest
    dp, z, n = scal[0], scal[1], scal[2]
    outer = (z == 0) | (z == n - 1)
    first = z == n // 2 - 1
    waits = {}
    t = 0
    for name, _, parts in loads:
        for i, (r0, rows), (c0, cols), to_row, to_col in parts:
            for k in range(0, rows, TILE):
                n = min(TILE, rows - k)
                at = first_row(r0, rows, dp) + k
                at = at if isinstance(at, int) else pl.multiple_of(at, n)
                src = ins[i].at[pl.ds(at, n), pl.ds(c0, cols)]
                dst = bufs[name].at[pl.ds(to_row + k, n), pl.ds(to_col, cols)]
                cp = pltpu.make_async_copy(src, dst, in_sem.at[t])
                cp.start()
                waits.setdefault(name, []).append((to_row + k, cp))
                t += 1

    def get(name, upto=None):
        rest = []
        for row, cp in waits.pop(name, ()):
            if upto is None or row < upto:
                cp.wait()
            else:
                rest.append((row, cp))
        if rest:
            waits[name] = rest
        return bufs[name]

    done = []
    slot = [0]

    def ship(src, dst):
        cp = pltpu.make_async_copy(src, dst, out_sem.at[slot[0]])
        slot[0] += 1
        cp.start()
        done.append(cp)

    where_out = {}
    k = 0
    for group in (pieces, extras):
        if group:
            at = 0
            for name, rows in group:
                where_out[name] = (outs[k], at)
                at += rows
            k += 1

    def emit(name, t):
        if name in where_out:
            ref, at = where_out[name]
            n = t.stop - t.start
            ship(out_bufs[name].at[pl.ds(t.start, n)], ref.at[pl.ds(at + t.start, n)])

    def store(name, t, value):
        for i, (key, r0, rows, col) in enumerate(stores):
            if key == name:
                f_bufs[i][t, :] = value.astype(f32)
                at = first_row(r0, rows, dp) + t.start
                n = t.stop - t.start
                at = at if isinstance(at, int) else pl.multiple_of(at, n)
                dst = outs[len(outs) - len(stores) + i]
                dst = dst.at[pl.ds(at, n), pl.ds(col, f_bufs[i].shape[1])]
                ship(f_bufs[i].at[pl.ds(t.start, n)], dst)

    def tiles(rows):
        t = min(rows, TILE)
        return [slice(i, i + t) for i in range(0, rows, t)]

    have = lambda *names: all(n in bufs for n in names)
    low = lambda a, b: (a.astype(f32) + b.astype(f32)).astype(bf16)
    if kind == "X":
        if have("a4_got"):
            out = out_bufs["a4"]
            for t in tiles(out.shape[0]):
                got, own = get("a4_got", t.stop), get("a4_own", t.stop)
                v = jnp.where(outer, got[t, :], own[t, :])
                out[t, :] = v
                emit("a4", t)
                store("a4", t, v)
        if have("b2_got"):
            out = out_bufs["b2"]
            for t in tiles(out.shape[0]):
                out[t, :] = low(get("b2_own", t.stop)[t, :], get("b2_got", t.stop)[t, :])
                emit("b2", t)
        if have("a0_g"):
            g, out = get("a0_g")[...], out_bufs["a0"]
            for t in tiles(out.shape[0]):
                out[t, :] = dot(get("a0_x", t.stop)[t, :], g).astype(bf16)
                emit("a0", t)
    if kind == "O":
        if have("a4_fin"):
            for t in tiles(bufs["a4_fin"].shape[0]):
                store("a4_fin", t, get("a4_fin", t.stop)[t, :])
        a_in, a_out = have("s1_g"), have("s3_got")
        if a_in or a_out:
            out = out_bufs["a"]
            g = get("s1_g")[...] if a_in else None
            for t in tiles(out.shape[0]):
                if a_in:
                    v = dot(get("s1_x", t.stop)[t, :], g)
                    v = (v + get("s1_got", t.stop)[t, :].astype(f32)).astype(bf16)
                    out_bufs["s1"][t, :] = v
                    emit("s1", t)
                if a_out:
                    u = low(get("s3_own", t.stop)[t, :], get("s3_got", t.stop)[t, :])
                    v = jnp.where(outer, v, u) if a_in else u
                out[t, :] = v
                emit("a", t)
        b_in, b_out = have("t0_g"), have("t4_got")
        if b_in or b_out:
            out = out_bufs["b"]
            h = out.shape[0] // 2
            g = get("t0_g")[...] if b_in else None
            for half in (0, 1):
                mine = first if half == 0 else jnp.logical_not(first)
                for t in tiles(h):
                    o = slice(half * h + t.start, half * h + t.stop)
                    if b_in:
                        v = dot(get("t0_x", o.stop)[o, :], g).astype(bf16)
                        out_bufs["t0"][o, :] = v
                        emit("t0", o)
                    if b_out:
                        own, got = get("t4_own", t.stop), get("t4_got", t.stop)
                        u = jnp.where(mine, own[t, :], got[t, :])
                        v = jnp.where(outer, v, u) if b_in else u
                    out[o, :] = v
                    emit("b", o)
    if kind == "M":
        for name in ("a2", "b3"):
            if have(name + "_got"):
                out = out_bufs[name]
                for t in tiles(out.shape[0]):
                    own, got = get(name + "_own", t.stop), get(name + "_got", t.stop)
                    out[t, :] = low(own[t, :], got[t, :])
                    emit(name, t)
        if have("b1_own"):
            own, got, out, keep = get("b1_own"), get("or_b"), out_bufs["b1"], out_bufs["keep"]
            h = out.shape[0]
            for t in tiles(h):
                o = slice(h + t.start, h + t.stop)
                top, bottom = low(own[t, :], got[t, :]), low(own[o, :], got[o, :])
                out[t, :] = jnp.where(first, bottom, top)
                keep[t, :] = jnp.where(first, top, bottom)
                emit("b1", t)
                emit("keep", t)
        if have("fin_own"):
            for t in tiles(bufs["fin_own"].shape[0]):
                own, got = get("fin_own", t.stop), get("or_b", t.stop)
                store("fin", t, jnp.where(outer, got[t, :], own[t, :]))
    for cp in done:
        cp.wait()


class Rounds:
    def __init__(self, at, outs, line):
        self.at, self.outs, self.line = at, outs, line
        self.a, self.b = {}, {}
        self.got = {}
        self.r = 0
        self.swap_outer = [(0, 1), (1, 0), (2, 3), (3, 2)]
        self.scal = jnp.stack([at.dp, at.z, jnp.int32(at.n)]).astype(jnp.int32)

    def piece(self, kind, r, name, own=False):
        sent, got, table = self.got[kind, r]
        at = 0
        for k, rows in table:
            if k == name:
                return (sent if own else got), (at, rows)
            at += rows

    def run(self, kind, b, pieces, extras, stores, flops):
        rows = {n: r for n, r in pieces + extras}
        w = self.width
        loads = tuple((k,) + v for k, v in b.loads.items())
        any_ = pl.BlockSpec(memory_space=pl.ANY)
        smem = pl.BlockSpec(memory_space=pltpu.SMEM)
        shapes, aliases = [jax.ShapeDtypeStruct((1,), jnp.int32)], {}
        if pieces:
            shapes.append(jax.ShapeDtypeStruct((sum(r for _, r in pieces), w), bf16))
        if extras:
            shapes.append(jax.ShapeDtypeStruct((sum(r for _, r in extras), w), bf16))
        for which, *_ in stores:
            aliases[2 + len(b.refs) + len(aliases)] = len(shapes)
            shapes.append(jax.ShapeDtypeStruct(self.outs[which].shape, f32))
        scratch = [pltpu.VMEM(shape, bf16) for _, shape, _ in loads]
        scratch += [pltpu.VMEM((rows[n], w), bf16) for n, _ in pieces + extras]
        scratch += [pltpu.VMEM((r, w), f32) for _, _, _, r, _ in stores]
        count = lambda rows: -(-rows // TILE)
        n_out = sum(count(r) for _, r in pieces + extras) + sum(count(r) for _, _, _, r, _ in stores)
        n_load = sum(count(p[1][1]) for _, _, parts in loads for p in parts)
        scratch += [pltpu.SemaphoreType.DMA((n_load,)), pltpu.SemaphoreType.DMA((n_out,))]
        moved = sum(m * n * 2 for _, (m, n), _ in loads) + sum(rows.values()) * w * 2
        moved += sum(r * w * 4 for _, _, _, r, _ in stores)
        n_in = len(b.refs) + len(stores)
        out = pl.pallas_call(
            functools.partial(
                round_kernel, kind, loads, n_in, tuple(pieces), tuple(extras),
                tuple(s[1:] for s in stores),
            ),
            out_shape=shapes,
            in_specs=[smem, smem] + [any_] * n_in,
            out_specs=[smem] + [any_] * (len(shapes) - 1),
            input_output_aliases=aliases,
            scratch_shapes=scratch,
            cost_estimate=pl.CostEstimate(flops=flops, bytes_accessed=moved, transcendentals=0),
            name="round_" + kind.lower(),
        )(self.scal, self.line.token, *b.refs, *[self.outs[s[0]] for s in stores])
        self.line.token, *out = out
        for which, *_ in reversed(stores):
            self.outs[which] = out.pop()
        extra = out.pop() if extras else None
        if pieces:
            axis, pairs = {
                "X": ("dp", self.at.swap), "O": ("seq", self.swap_outer), "M": ("seq", self.at.mid),
            }[kind]
            self.got[kind, self.r] = (out[0], lax.ppermute(out[0], axis, pairs), pieces)
        return extra

    def step_x(self):
        r, A, B = self.r, self.a, self.b
        b, pieces, stores, flops = Round(), [], [], 0
        if r in A:
            c = A[r]
            half, tok = c["x"][0].shape[0] // 2, sum(x.shape[1] for x in c["x"])
            b.load_down("a0_g", c["grad"], c["cols"])
            b.load_across("a0_x", c["x"], ("other", half))
            pieces.append(("a0", half))
            flops += 2 * half * tok * c["cols"][1]
        if r - 6 in A:
            c = A[r - 6]
            b.load("a4_got", *self.piece("O", r - 2, "a"))
            b.load("a4_own", *self.piece("O", r - 2, "a", True))
            rows = b.loads["a4_own"][0][0]
            pieces.append(("a4", rows))
            stores.append((c["which"], "a4", "own", rows, c["col"]))
        if r - 3 in B:
            c = B[r - 3]
            b.load("b2_got", *self.piece("M", r - 2, "b1"))
            b.load("b2_own", *c["keep"])
            pieces.append(("b2", b.loads["b2_got"][0][0]))
        if pieces:
            self.run("X", b, pieces, [], stores, flops)

    def step_o(self):
        r, A, B = self.r, self.a, self.b
        b, pieces, extras, stores, flops = Round(), [], [], [], 0
        if r - 1 in A:
            c = A[r - 1]
            half, tok = c["x"][0].shape[0] // 2, sum(x.shape[1] for x in c["x"])
            b.load_down("s1_g", c["grad"], c["cols"])
            b.load_across("s1_x", c["x"], ("own", half))
            b.load("s1_got", *self.piece("X", r - 1, "a0"))
            extras.append(("s1", half))
            flops += 2 * half * tok * c["cols"][1]
        if r - 4 in A:
            b.load("s3_own", *self.piece("M", r - 2, "a2", True))
            b.load("s3_got", *self.piece("M", r - 2, "a2"))
        if r - 1 in A or r - 4 in A:
            pieces.append(("a", half if r - 1 in A else b.loads["s3_got"][0][0]))
        if r in B:
            c = B[r]
            rows, tok = c["x"][0].shape[0], sum(x.shape[1] for x in c["x"])
            b.load_down("t0_g", c["grad"], c["cols"])
            b.load_across("t0_x", c["x"], (0, rows))
            extras.append(("t0", rows))
            flops += 2 * rows * tok * c["cols"][1]
        if r - 6 in B:
            b.load("t4_own", *self.piece("M", r - 2, "b3", True))
            b.load("t4_got", *self.piece("M", r - 2, "b3"))
        if r in B or r - 6 in B:
            pieces.append(("b", rows if r in B else 2 * b.loads["t4_got"][0][0]))
        if r - 7 in A:
            c = A.pop(r - 7)
            b.load("a4_fin", *self.piece("X", r - 1, "a4"))
            stores.append((c["which"], "a4_fin", "other", b.loads["a4_fin"][0][0], c["col"]))
        if pieces or stores:
            extra = self.run("O", b, pieces, extras, stores, flops)
            at = 0
            for name, n in extras:
                (A[r - 1] if name == "s1" else B[r])[name] = (extra, (at, n))
                at += n

    def step_m(self):
        r, A, B = self.r, self.a, self.b
        b, pieces, extras, stores = Round(), [], [], []
        if r - 2 in A:
            b.load("a2_own", *A[r - 2]["s1"])
            b.load("a2_got", *self.piece("O", r - 1, "a"))
            pieces.append(("a2", b.loads["a2_got"][0][0]))
        if r - 1 in B or r - 7 in B:
            b.load("or_b", *self.piece("O", r - 1, "b"))
            rows = b.loads["or_b"][0][0]
        if r - 1 in B:
            b.load("b1_own", *B[r - 1]["t0"])
            pieces.append(("b1", rows // 2))
            extras.append(("keep", rows // 2))
        if r - 4 in B:
            b.load("b3_own", *self.piece("X", r - 1, "b2", True))
            b.load("b3_got", *self.piece("X", r - 1, "b2"))
            pieces.append(("b3", b.loads["b3_got"][0][0]))
        if r - 7 in B:
            c = B.pop(r - 7)
            b.load("fin_own", *self.piece("O", r - 1, "b", True))
            stores.append((c["which"], "fin", 0, rows, c["col"]))
        if pieces or stores:
            extra = self.run("M", b, pieces, extras, stores, 0)
            if extras:
                B[r - 1]["keep"] = (extra, (0, rows // 2))


def blank_kernel(*outs):
    pass


def blanks(shapes):
    return pl.pallas_call(
        blank_kernel,
        out_shape=[jax.ShapeDtypeStruct(s, f32) for s in shapes],
        out_specs=[pl.BlockSpec(memory_space=pl.ANY)] * len(shapes),
        name="blanks",
    )()


def gather_steps(x, n, axis=0, wait=0):
    got = None
    for b in reversed(bits_of(n)):
        if got is not None:
            x = jnp.concatenate([x, got], axis=axis)
        got = lax.ppermute(x, "mp", xor_perm(n, b))
        if wait:
            yield (), x
            yield from idle(wait - 1)
            got = yield got, ()
        else:
            got = yield got, x
    return [x, got]


def joined(pieces, axis=0):
    return jnp.concatenate(pieces, axis=axis)


def scatter_steps(x, n, axis=0, wait=0):
    for b in bits_of(n):
        half = x.shape[axis] // 2
        keep = lax.slice_in_dim(x, 0, half, axis=axis)
        send = lax.slice_in_dim(x, half, 2 * half, axis=axis)
        got = lax.ppermute(send, "mp", xor_perm(n, b))
        if wait:
            yield (), (send, keep)
            yield from idle(wait - 1)
            got = yield got, ()
        else:
            got = yield got, (send, keep)
        x = keep.astype(f32) + got.astype(f32)
        if 2 * b < n:
            x = x.astype(bf16)
    return x.astype(f32)


def sum_rows_steps(x, n):
    masks = row_masks(n)
    for b in bits_of(n):
        got = yield lax.ppermute(x, "mp", xor_perm(n, b)), x
        got = got.reshape(x.shape[:-1] + (n, -1))
        order = [masks.index(m ^ b) for m in masks]
        got = jnp.stack([got[..., k, :] for k in order], axis=-2)
        x = x + got.reshape(x.shape)
    return x


def exchange_steps(pieces, n):
    got = yield exchange(pieces, n)[1:], pieces[1:]
    return [pieces[0]] + list(got)


class Layer:
    pass


def forward_task(c, m):
    f = c.fwd[m]
    own = c.tokens[m]
    length = c.lengths[m, 0]
    x = f.x = yield from gather_steps(own, c.n_mp)
    proj = dot(joined(x), c.qkv_weight)
    local = c.local
    squares = jnp.stack(
        [jnp.sum(jnp.square(proj[:, t * local : (t + 1) * local]), axis=1) for t in (0, 1)], axis=0
    )
    squares = yield from sum_rows_steps(squares, c.n_mp)
    inv = lax.rsqrt(squares / c.width + epsilon).T
    pieces = rope_call(c.slots, c.z_arr, proj, inv, c.cos, c.sin, c.qg, c.kg)
    if c.by_heads:
        scal = jnp.stack([c.z, c.me, length]).astype(jnp.int32)
        f.pieces = yield from exchange_steps(pieces, c.n_seq)
        mixed, f.kept = attend(scal, f.pieces, c.masks)
        mixed = yield from exchange_steps(mixed, c.n_seq)
        mixed = join_heads(c.z_arr, mixed)
    else:
        mixed, f.kept = gathered_attend(pieces[0], c.pos, length)
    attended = yield from scatter_steps(dot(mixed, c.o_weight).astype(bf16), c.n_mp)
    attn_inv = inv_rms(attended)
    hidden = own.astype(f32) + attended * attn_inv * c.attn_gain
    mlp_in = yield from gather_steps(hidden.astype(bf16), c.n_mp)
    f.mlp_in = mlp_in
    rows_in = joined(mlp_in)
    f.gate, f.up = dot(rows_in, c.gate_weight), dot(rows_in, c.up_weight)
    f.act = (f.gate * jax.nn.sigmoid(f.gate) * f.up).astype(bf16)
    mlp_out = yield from scatter_steps(dot(f.act, c.down_weight).astype(bf16), c.n_mp)
    mlp_inv = inv_rms(mlp_out)
    f.layer = (hidden + mlp_out * mlp_inv * c.mlp_gain).astype(bf16)
    f.seeds = c.cotangent[m].astype(f32) * (c.own_pos < length).astype(f32)[:, None]
    mlp_grad, gain_rows = norm_backward(mlp_out, mlp_inv, c.mlp_gain, f.seeds)
    f.mlp_gain = jnp.sum(gain_rows, axis=0)
    f.mlp_grad = yield from gather_steps(mlp_grad.astype(bf16), c.n_mp)
    f.proj, f.inv, f.mixed, f.attended, f.attn_inv = proj, inv, mixed, attended, attn_inv
    return ()


def backward_task(c):
    n, rows, fwd = len(c.fwd), c.rows, c.fwd
    yield (), ()
    gates = mlp_back(
        c.line, [x for f in fwd for x in f.mlp_grad], c.down_weight, [f.gate for f in fwd], [f.up for f in fwd]
    )
    for f, f.gate_grad, f.up_grad in zip(fwd, *gates):
        pass
    yield (), ()
    back = hidden_back(c.line, gates[0], c.gate_weight, gates[1], c.up_weight)
    back = yield from scatter_steps(jnp.stack(back), c.n_mp, 1, c.far)
    hidden_grad, attn_grad = [], []
    for m, f in enumerate(fwd):
        hidden_grad.append(f.seeds + back[m])
        e, gain_rows = norm_backward(f.attended, f.attn_inv, c.attn_gain, hidden_grad[m])
        f.attn_gain = jnp.sum(gain_rows, axis=0)
        attn_grad.append(e.astype(bf16))
    attn_grad = yield from gather_steps(jnp.stack(attn_grad), c.n_mp, 1, c.far)
    c.attn_grad = [x.reshape(-1, c.width) for x in attn_grad]
    c.attn_grad_all = attn_grad = joined(attn_grad, 1).reshape(n * rows, c.width)
    dy = dot_nt(attn_grad, c.o_weight).astype(bf16)
    if c.by_heads:
        dys = split_heads(c.z_arr, dy, c.slots)
        dys = yield from exchange_steps(dys, c.n_seq)
        scal = jnp.concatenate([jnp.stack([c.z, c.me]), c.lengths[:, 0]]).astype(jnp.int32)
        grads = attend_back(scal, [f.pieces for f in fwd], [f.kept for f in fwd], dys, c.masks)
        grads = yield from exchange_steps(grads, c.n_seq)
    else:
        grads = [gathered_back(f.kept, dy[m * rows : (m + 1) * rows]) for m, f in enumerate(fwd)]
        grads = [jnp.concatenate(grads, axis=0)]
    tables = (c.cos, c.sin, c.qg, c.kg)
    cross = []
    for m, f in enumerate(fwd):
        e, f.gains = cross_call(c.slots, m, c.z_arr, grads, f.proj, f.inv, *tables)
        cross.append(e.T)
    cross = yield from sum_rows_steps(jnp.concatenate(cross, axis=0), c.n_mp)
    for m, f in enumerate(fwd):
        e = cross[2 * m : 2 * m + 2].T
        f.qkv_grad = raw_call(
            c.slots, c.width, m, c.z_arr, grads, f.proj, f.inv, e, *tables
        )
    yield (), [f.qkv_grad for f in fwd]
    back = jnp.stack([dot_nt(f.qkv_grad, c.qkv_weight).astype(bf16) for f in fwd])
    back = yield from scatter_steps(back, c.n_mp, 1, c.far)
    c.input_grad = jnp.stack(hidden_grad) + back
    return c.input_grad


def turning_task(c):
    yield (), ()
    c.attn_grad_t = []
    for m in range(len(c.fwd)):
        c.attn_grad_t.append(turn(c.line, c.attn_grad, m, len(c.fwd)))
        yield (), ()


def gains_task(c):
    yield (), ()
    gains = sum(f.gains for f in c.fwd)
    gains = lax.dynamic_update_slice(jnp.zeros((2, c.width), f32), gains, (0, c.me * c.local))
    gains = jnp.concatenate(
        [gains, sum(f.attn_gain for f in c.fwd)[None], sum(f.mlp_gain for f in c.fwd)[None]], axis=0
    )
    for name, n in (("mp", c.n_mp), ("seq", c.n_seq), ("dp", c.n_dp)):
        for b in bits_of(n):
            got = lax.ppermute(gains, name, xor_perm(n, b))
            yield (), gains
            if c.rounds:
                yield from idle(5)
            got = yield got, ()
            gains = gains + got
    c.gains = gains
    return gains


def per_device(
    n_dp, n_seq, n_mp,
    tokens, lengths, cotangent, q_weight, k_weight, v_weight, o_weight, q_gain, k_gain,
    attn_gain, gate_weight, up_weight, down_weight, mlp_gain,
):
    c = Layer()
    micros, own_rows, width = tokens.shape
    rows = own_rows * n_mp
    local = q_weight.shape[1]
    heads = local // HEAD_DIM
    ff = gate_weight.shape[1]
    me, z = lax.axis_index("mp"), lax.axis_index("seq")
    c.tokens, c.lengths, c.cotangent, c.o_weight = tokens, lengths, cotangent, o_weight
    c.gate_weight, c.up_weight, c.down_weight = gate_weight, up_weight, down_weight
    c.attn_gain, c.mlp_gain = attn_gain, mlp_gain
    c.n_dp, c.n_seq, c.n_mp, c.rows, c.width, c.local = n_dp, n_seq, n_mp, rows, width, local
    c.me, c.z, c.masks = me, z, row_masks(n_mp)
    c.by_heads = heads == n_seq
    c.slots = n_seq if c.by_heads else 1
    c.z_arr = z.astype(jnp.int32).reshape(1)
    c.qkv_weight = jnp.concatenate([q_weight, k_weight, v_weight], axis=1)
    c.qg = lax.dynamic_slice_in_dim(q_gain, me * local, local)[None]
    c.kg = lax.dynamic_slice_in_dim(k_gain, me * local, local)[None]
    block = jnp.asarray(c.masks, jnp.int32) ^ me
    steps = jnp.arange(own_rows, dtype=jnp.int32)
    c.pos = z * rows + (block[:, None] * own_rows + steps).reshape(-1)
    c.own_pos = z * rows + me * own_rows + steps
    frequency = rope_base ** (-(jnp.arange(HALF, dtype=f32) * 2.0 / HEAD_DIM))
    angles = c.pos.astype(f32)[:, None] * frequency[None, :]
    cos, sin = jnp.cos(angles), jnp.sin(angles)
    c.cos = jnp.concatenate([cos, cos], axis=1)
    c.sin = jnp.concatenate([-sin, sin], axis=1)
    c.fwd = [Layer() for _ in range(micros)]

    at = Place(n_seq)
    c.rounds = rounds = n_seq == 4
    line = c.line = Line(jnp.zeros((1,), jnp.int32))
    fw = [forward_task(c, m) for m in range(micros)]
    line.add(*fw)
    def turned(m, name):
        f = c.fwd[m]
        rows_ = getattr(f, name)
        setattr(f, name + "_t", turn(line, rows_ if isinstance(rows_, list) else [rows_]))

    extra = {"a": (0, "x"), "b": (1, "x"), "c": (0, "act"), "d": (1, "act"), "e": (0, "mlp_in"), "f": (1, "mlp_in")}
    order = ORDER if (micros, n_mp, c.by_heads) == (2, 4, True) and rounds else ""
    for act in order:
        if act in extra:
            turned(*extra[act])
        else:
            line.step(fw[int(act)])
    while any(t in line.waits for t in fw):
        for t in fw:
            line.step(t)

    c.far = 0
    each = lambda name: [getattr(f, name) for f in c.fwd]
    outs = list(blanks(
        [(ff, width), (width, ff), (width, ff)]
        + [(width, local)] * 3
        + [(width, local) if rounds else (local, width)]
    ))
    back, gains = backward_task(c), gains_task(c)
    side = []
    line.add(back)

    stack = lambda lists: [x for pieces in lists for x in pieces]
    both = lambda name: jnp.concatenate(each(name), axis=0)
    both2 = lambda name: jnp.concatenate(stack(each(name)), axis=0)

    def work(key):
        if rounds:
            return {
                "down": lambda: (each("act_t"), stack(each("mlp_grad"))),
                "gate": lambda: (each("mlp_in_t"), each("gate_grad")),
                "up": lambda: (each("mlp_in_t"), each("up_grad")),
                "o": lambda: (c.attn_grad_t, each("mixed")),
                "qkv": lambda: (each("x_t"), each("qkv_grad")),
            }[key]()
        return {
            "down": lambda: (both("act"), both2("mlp_grad")),
            "gate": lambda: (both2("mlp_in"), both("gate_grad")),
            "up": lambda: (both2("mlp_in"), both("up_grad")),
            "o": lambda: (both("mixed"), c.attn_grad_all),
            "qkv": lambda: (both2("x"), both("qkv_grad")),
        }[key]()

    done, live = {}, []
    if rounds:
        reducer = Rounds(at, outs, line)
        reducer.width = local // 2

    def rows_of(key):
        if key not in done:
            done[key] = work(key)
        return done[key]

    def one_round(new_a, new_b, script=""):
        if rounds:
            for new, table in ((new_a, reducer.a), (new_b, reducer.b)):
                if new is not None:
                    key, which, first, n, col = new
                    x, grad = rows_of(key)
                    table[reducer.r] = dict(x=x, grad=grad, cols=(first, n), which=which, col=col)
            for act in script:
                if act in "XOM":
                    getattr(reducer, "step_" + act.lower())()
                else:
                    line.step({"c": back, "t": turning, "g": gains}[act])
            reducer.r += 1
            return
        for new, kind in ((new_a, "a"), (new_b, "b")):
            if new is not None:
                key, which, first, n, col = new
                x, grad = rows_of(key)
                if kind == "a":
                    if key + "/" not in done:
                        done[key + "/"] = (take_half(x, at.dp, False), take_half(x, at.dp, True))
                    t = task_a(at, outs, which, *done[key + "/"], grad, slice(first, first + n), col)
                else:
                    t = task_b(at, outs, which, x, grad, slice(first, first + n), col)
                line.add(t)
                live.append(t)
        live[:] = line.step(*live)
        for t in side:
            line.step(t)

    unit = local // 2
    cut = lambda key, which, n, u=unit, first=0: [
        (key, which, first + t, u, t) for t in range(0, n, u)
    ]
    ready = {
        "down": lambda: True,
        "gate": lambda: all(hasattr(f, "up_grad") for f in c.fwd),
        "o": lambda: len(c.attn_grad_t) == micros if rounds else hasattr(c, "attn_grad_all"),
        "qkv": lambda: all(hasattr(f, "qkv_grad") for f in c.fwd),
    }
    ready["up"] = ready["gate"]
    todo = cut("down", 0, width) + cut("gate", 1, ff) + cut("up", 2, ff)
    todo += cut("o", 6, local) if rounds else cut("o", 6, width, width // 2)
    for t in range(3):
        todo += cut("qkv", 3 + t, local, first=t * local)
    c.attn_grad_t = []
    if rounds:
        for m in range(micros):
            for name in ("x", "act", "mlp_in"):
                if not hasattr(c.fwd[m], name + "_t"):
                    turned(m, name)
        turning = turning_task(c)
        line.add(turning)
    else:
        side = [back]
    count_a = (len(todo) * 5) // 8

    def take():
        for i, chunk in enumerate(todo):
            if ready[chunk[0]]():
                return todo.pop(i)
        return None

    gains_on = False
    r = taken_a = 0
    while todo or any(t in line.waits for t in (back, gains)) or (
        reducer.a or reducer.b if rounds else live
    ):
        late = ready["qkv"]()
        if late and not gains_on:
            gains_on = True
            side.append(gains)
            line.add(gains)
        new_a = take() if taken_a < count_a else None
        taken_a += new_a is not None
        script = SCRIPT[r] if r < len(SCRIPT) else "XgOcMg"
        lone = rounds and r < len(SCRIPT) and script[-1:] == "-"
        new_b = None if lone else take()
        one_round(new_a, new_b, script.strip("-") if rounds else "")
        r += 1
    return (
        jnp.stack(each("layer")),
        c.input_grad,
        outs[3],
        outs[4],
        outs[5],
        outs[6].T if rounds else outs[6],
        c.gains[0],
        c.gains[1],
        c.gains[2],
        outs[1],
        outs[2],
        outs[0],
        c.gains[3],
    )


SCRIPT = (
    "XOc",
    "XcOM",
    "XcOM",
    "XcOM",
    "XOcM",
    "XOcM",
    "XOMc",
    "XOtMtc",
    "XOcM",
    "XcOMc",
    "XOMc",
)

ORDER = "001010" "11" "ab" "000" "1" "0" "1" "0" "1" "0" "1" "0" "ce" "11" "0" "1" "d" "0" "f" "1" "0" "1" "1"


def solution(mesh):
    n_dp, n_seq, n_mp = (mesh.shape[a] for a in ("dp", "seq", "mp"))
    assert n_dp == 2
    rows = P(None, ("dp", "seq", "mp"), None)
    cols, flat, all_ = P(None, "mp"), P("mp", None), P()
    return jax.shard_map(
        functools.partial(per_device, n_dp, n_seq, n_mp),
        mesh=mesh,
        in_specs=(rows, P(None, "dp"), rows, cols, cols, cols, flat, all_, all_, all_, cols, cols, flat, all_),
        out_specs=(rows, rows, cols, cols, cols, flat, all_, all_, all_, cols, cols, flat, all_),
        check_vma=False,
    )
```

```python
import functools

import jax
import jax.numpy as jnp
from jax import lax
from jax.experimental import pallas as pl
from jax.experimental.pallas import tpu as pltpu
from jax.sharding import PartitionSpec as P

HEAD_DIM = 128
HALF = HEAD_DIM // 2
DP, SEQ, MP = "dp", "seq", "mp"
TO_KEYS, TO_ROWS, TO_HEADS = "shd,khd->shk", "shk,khd->shd", "shk,shd->khd"
epsilon = 1e-06
rope_base = 500000.0
masked_score = -1e30
LOG2E = 1.4426950408889634

f32 = jnp.float32
bf16 = jnp.bfloat16


def add_low(a, b):
    return (a.astype(f32) + b.astype(f32)).astype(bf16)


def bits_of(n):
    out = []
    b = 1
    while b < n:
        out.append(b)
        b *= 2
    return out


def xor_perm(n, b):
    return [(i, i ^ b) for i in range(n)]


def row_masks(n):
    masks = [0]
    for b in reversed(bits_of(n)):
        masks = masks + [m | b for m in masks]
    return masks


def inv_rms(v):
    return lax.rsqrt(jnp.mean(v * v, axis=-1, keepdims=True) + epsilon)


def norm_backward(source, inverse, gain_vec, upstream):
    normed = source * inverse
    weighted = upstream * gain_vec
    back = inverse * (weighted - normed * jnp.mean(weighted * normed, axis=-1, keepdims=True))
    return back, upstream * normed


def dot_t(a, b):
    return lax.dot_general(a, b, (((0,), (0,)), ((), ())), preferred_element_type=f32)


def dot_nt(a, b):
    return lax.dot_general(a, b, (((1,), (1,)), ((), ())), preferred_element_type=f32)


def dot(a, b):
    return jnp.dot(a, b, preferred_element_type=f32)


def rope_kernel(slots, width, local, z_ref, proj, inv, cos, sin, qg, kg, *outs):
    z = z_ref[0]
    c, s = cos[...], sin[...]
    for j in range(slots):
        base = (z ^ j) * width if slots > 1 else 0
        for h in range(width // HEAD_DIM):
            at = base + h * HEAD_DIM
            at = pl.multiple_of(at, HEAD_DIM) if slots > 1 else at
            for part, gain in ((0, qg), (1, kg)):
                raw = proj[:, pl.ds(part * local + at, HEAD_DIM)]
                v = raw * inv[:, part : part + 1] * gain[:, pl.ds(at, HEAD_DIM)]
                v = v * c + pltpu.roll(v, HALF, 1) * s
                lo = part * width + h * HEAD_DIM
                outs[j][:, lo : lo + HEAD_DIM] = v.astype(bf16)
            lo = 2 * width + h * HEAD_DIM
            outs[j][:, lo : lo + HEAD_DIM] = proj[:, pl.ds(2 * local + at, HEAD_DIM)].astype(bf16)


def rope_call(slots, z, proj, inv, cos, sin, qg, kg):
    rows, local = proj.shape[0], proj.shape[1] // 3
    width = local // slots
    blk = min(rows, 256)
    row = lambda n: pl.BlockSpec((blk, n), lambda i, *_: (i, 0))
    vec = pl.BlockSpec((1, local), lambda i, *_: (0, 0))
    return pl.pallas_call(
        functools.partial(rope_kernel, slots, width, local),
        out_shape=[jax.ShapeDtypeStruct((rows, 3 * width), bf16)] * slots,
        grid_spec=pltpu.PrefetchScalarGridSpec(
            num_scalar_prefetch=1,
            grid=(rows // blk,),
            in_specs=[row(3 * local), row(2), row(HEAD_DIM), row(HEAD_DIM), vec, vec],
            out_specs=[row(3 * width)] * slots,
        ),
        cost_estimate=pl.CostEstimate(
            flops=rows * local * 12, bytes_accessed=rows * local * 18, transcendentals=0
        ),
    )(z, proj, inv, cos, sin, qg, kg)


def unrope(grad, c, s):
    g = grad.astype(f32)
    return g * c - pltpu.roll(g, HALF, 1) * s


def cross_kernel(slots, width, local, z_ref, *refs):
    grads = refs[:slots]
    proj, inv, cos, sin, qg, kg, cross, gains = refs[slots:]
    z = z_ref[0]
    c, s = cos[...], sin[...]

    @pl.when(pl.program_id(0) == 0)
    def _():
        gains[...] = jnp.zeros_like(gains)

    for part, gain in ((0, qg), (1, kg)):
        total = None
        for j in range(slots):
            base = (z ^ j) * width if slots > 1 else 0
            for h in range(width // HEAD_DIM):
                at = base + h * HEAD_DIM
                at = pl.multiple_of(at, HEAD_DIM) if slots > 1 else at
                lo = part * width + h * HEAD_DIM
                g = unrope(grads[j][:, lo : lo + HEAD_DIM], c, s)
                gr = g * proj[:, pl.ds(part * local + at, HEAD_DIM)]
                w = gr * gain[:, pl.ds(at, HEAD_DIM)]
                total = w if total is None else total + w
                col = jnp.sum(gr * inv[:, part : part + 1], axis=0, keepdims=True)
                gains[part : part + 1, pl.ds(at, HEAD_DIM)] += col
        cross[:, part : part + 1] = jnp.sum(total, axis=1, keepdims=True)


def raw_kernel(slots, width, local, d, z_ref, *refs):
    grads = refs[:slots]
    proj, inv, cross, cos, sin, qg, kg, out = refs[slots:]
    z = z_ref[0]
    c, s = cos[...], sin[...]
    for j in range(slots):
        base = (z ^ j) * width if slots > 1 else 0
        for h in range(width // HEAD_DIM):
            at = base + h * HEAD_DIM
            at = pl.multiple_of(at, HEAD_DIM) if slots > 1 else at
            for part, gain in ((0, qg), (1, kg)):
                lo = part * width + h * HEAD_DIM
                g = unrope(grads[j][:, lo : lo + HEAD_DIM], c, s)
                r = inv[:, part : part + 1]
                w = g * gain[:, pl.ds(at, HEAD_DIM)] * r
                k = r * r * r * (cross[:, part : part + 1] * (1.0 / d))
                w = w - proj[:, pl.ds(part * local + at, HEAD_DIM)] * k
                out[:, pl.ds(part * local + at, HEAD_DIM)] = w.astype(bf16)
            lo = 2 * width + h * HEAD_DIM
            out[:, pl.ds(2 * local + at, HEAD_DIM)] = grads[j][:, lo : lo + HEAD_DIM]


def cross_call(slots, m, z, grads, proj, inv, cos, sin, qg, kg):
    rows, local = proj.shape[0], proj.shape[1] // 3
    width = local // slots
    blk = min(rows, 256)
    far = lambda n: pl.BlockSpec((blk, n), lambda i, *_: (i + m * (rows // blk), 0))
    row = lambda n: pl.BlockSpec((blk, n), lambda i, *_: (i, 0))
    vec = pl.BlockSpec((1, local), lambda i, *_: (0, 0))
    return pl.pallas_call(
        functools.partial(cross_kernel, slots, width, local),
        out_shape=[
            jax.ShapeDtypeStruct((rows, 2), f32),
            jax.ShapeDtypeStruct((2, local), f32),
        ],
        grid_spec=pltpu.PrefetchScalarGridSpec(
            num_scalar_prefetch=1,
            grid=(rows // blk,),
            in_specs=[far(3 * width)] * slots
            + [row(3 * local), row(2), row(HEAD_DIM), row(HEAD_DIM), vec, vec],
            out_specs=[row(2), pl.BlockSpec((2, local), lambda i, *_: (0, 0))],
        ),
        cost_estimate=pl.CostEstimate(
            flops=rows * local * 20, bytes_accessed=rows * local * 18, transcendentals=0
        ),
    )(z, *grads, proj, inv, cos, sin, qg, kg)


def raw_call(slots, d, m, z, grads, proj, inv, cross, cos, sin, qg, kg):
    rows, local = proj.shape[0], proj.shape[1] // 3
    width = local // slots
    blk = min(rows, 256)
    far = lambda n: pl.BlockSpec((blk, n), lambda i, *_: (i + m * (rows // blk), 0))
    row = lambda n: pl.BlockSpec((blk, n), lambda i, *_: (i, 0))
    vec = pl.BlockSpec((1, local), lambda i, *_: (0, 0))
    return pl.pallas_call(
        functools.partial(raw_kernel, slots, width, local, d),
        out_shape=jax.ShapeDtypeStruct((rows, 3 * local), bf16),
        grid_spec=pltpu.PrefetchScalarGridSpec(
            num_scalar_prefetch=1,
            grid=(rows // blk,),
            in_specs=[far(3 * width)] * slots
            + [row(3 * local), row(2), row(2), row(HEAD_DIM), row(HEAD_DIM), vec, vec],
            out_specs=row(3 * local),
        ),
        cost_estimate=pl.CostEstimate(
            flops=rows * local * 20, bytes_accessed=rows * local * 24, transcendentals=0
        ),
    )(z, *grads, proj, inv, cross, cos, sin, qg, kg)


def join_kernel(slots, width, z_ref, *refs):
    z = z_ref[0]
    out = refs[slots]
    for j in range(slots):
        out[:, pl.ds(pl.multiple_of((z ^ j) * width, HEAD_DIM), width)] = refs[j][...]


def join_heads(z, pieces):
    rows, width = pieces[0].shape
    slots = len(pieces)
    blk = min(rows, 256)
    return pl.pallas_call(
        functools.partial(join_kernel, slots, width),
        out_shape=jax.ShapeDtypeStruct((rows, slots * width), bf16),
        grid_spec=pltpu.PrefetchScalarGridSpec(
            num_scalar_prefetch=1,
            grid=(rows // blk,),
            in_specs=[pl.BlockSpec((blk, width), lambda i, *_: (i, 0))] * slots,
            out_specs=pl.BlockSpec((blk, slots * width), lambda i, *_: (i, 0)),
        ),
    )(z, *pieces)


def split_kernel(slots, width, z_ref, x, *outs):
    z = z_ref[0]
    for j in range(slots):
        outs[j][...] = x[:, pl.ds(pl.multiple_of((z ^ j) * width, HEAD_DIM), width)]


def split_heads(z, x, slots):
    rows, local = x.shape
    width = local // slots
    blk = min(rows, 256)
    return pl.pallas_call(
        functools.partial(split_kernel, slots, width),
        out_shape=[jax.ShapeDtypeStruct((rows, width), bf16)] * slots,
        grid_spec=pltpu.PrefetchScalarGridSpec(
            num_scalar_prefetch=1,
            grid=(rows // blk,),
            in_specs=[pl.BlockSpec((blk, local), lambda i, *_: (i, 0))],
            out_specs=[pl.BlockSpec((blk, width), lambda i, *_: (i, 0))] * slots,
        ),
    )(z, x)


def exchange(pieces, n):
    return [p if j == 0 else lax.ppermute(p, SEQ, xor_perm(n, j)) for j, p in enumerate(pieces)]


def row_places(slots, masks, rows, z, me):
    count = rows // len(masks)
    for j in range(slots):
        for k, m in enumerate(masks):
            yield j, k * count, pl.multiple_of((z ^ j) * rows + (me ^ m) * count, count), count


def key_bias(total, length):
    pos = lax.broadcasted_iota(jnp.int32, (1, total), 1)
    return jnp.where(pos < length, 0.0, masked_score).astype(f32)


def diag_mask(size):
    r = lax.broadcasted_iota(jnp.int32, (size, size), 0)
    c = lax.broadcasted_iota(jnp.int32, (size, size), 1)
    return c <= r


def attend_kernel(slots, masks, rows, blk, scal, *refs):
    pieces, outs = refs[:slots], refs[slots : 2 * slots]
    o32, lse, qkv, o16, sem = refs[2 * slots :]
    z, me, length = scal[0], scal[1], scal[2]
    total = slots * rows
    copies = []
    for t, (j, at, to, n) in enumerate(row_places(slots, masks, rows, z, me)):
        cp = pltpu.make_async_copy(pieces[j].at[pl.ds(at, n)], qkv.at[pl.ds(to, n)], sem.at[t])
        cp.start()
        copies.append(cp)
    bias = key_bias(total, length)
    causal = diag_mask(blk)
    for cp in copies:
        cp.wait()
    factor = HEAD_DIM**-0.5 * LOG2E
    for i in range(total // blk):
        lo = i * blk
        q = qkv[lo : lo + blk, :HEAD_DIM]
        s = dot_nt(q, qkv[lo : lo + blk, HEAD_DIM : 2 * HEAD_DIM]) * factor
        s = jnp.where(causal, s + bias[:, lo : lo + blk], masked_score)
        top = jnp.max(s, axis=1, keepdims=True)
        if i:
            before = dot_nt(q, qkv[:lo, HEAD_DIM : 2 * HEAD_DIM]) * factor + bias[:, :lo]
            top = jnp.maximum(top, jnp.max(before, axis=1, keepdims=True))
        p = jnp.exp2(s - top)
        mass = jnp.sum(p, axis=1, keepdims=True)
        acc = dot(p.astype(bf16), qkv[lo : lo + blk, 2 * HEAD_DIM :])
        if i:
            p = jnp.exp2(before - top)
            mass = mass + jnp.sum(p, axis=1, keepdims=True)
            acc = acc + dot(p.astype(bf16), qkv[:lo, 2 * HEAD_DIM :])
        acc = acc / mass
        o32[lo : lo + blk, :] = acc
        o16[lo : lo + blk, :] = acc.astype(bf16)
        lse[lo : lo + blk, :] = top + jnp.log(mass) * LOG2E
    copies = []
    for t, (j, at, to, n) in enumerate(row_places(slots, masks, rows, z, me)):
        cp = pltpu.make_async_copy(o16.at[pl.ds(to, n)], outs[j].at[pl.ds(at, n)], sem.at[t])
        cp.start()
        copies.append(cp)
    for cp in copies:
        cp.wait()


def attend(scal, pieces, masks):
    slots = len(pieces)
    rows = pieces[0].shape[0]
    total = slots * rows
    hbm = pl.BlockSpec(memory_space=pl.ANY)
    vmem = pl.BlockSpec(memory_space=pltpu.VMEM)
    out = pl.pallas_call(
        functools.partial(attend_kernel, slots, masks, rows, 256),
        out_shape=[jax.ShapeDtypeStruct((rows, HEAD_DIM), bf16)] * slots
        + [
            jax.ShapeDtypeStruct((total, HEAD_DIM), f32),
            jax.ShapeDtypeStruct((total, 1), f32),
        ],
        in_specs=[pl.BlockSpec(memory_space=pltpu.SMEM)] + [hbm] * slots,
        out_specs=[hbm] * slots + [vmem, vmem],
        scratch_shapes=[
            pltpu.VMEM((total, 3 * HEAD_DIM), bf16),
            pltpu.VMEM((total, HEAD_DIM), bf16),
            pltpu.SemaphoreType.DMA((slots * len(masks),)),
        ],
        cost_estimate=pl.CostEstimate(
            flops=total * total * HEAD_DIM * 4,
            bytes_accessed=total * HEAD_DIM * 12,
            transcendentals=total * total // 2,
        ),
        name="attend",
    )(scal, *pieces)
    return out[:slots], (out[slots], out[slots + 1])


def attend_back_kernel(slots, masks, rows, blk, micros, scal, *refs):
    pieces = [refs[m * slots : (m + 1) * slots] for m in range(micros)]
    refs = refs[micros * slots :]
    kept = [refs[2 * m : 2 * m + 2] for m in range(micros)]
    dos, outs = refs[2 * micros : 2 * micros + slots], refs[2 * micros + slots :][:slots]
    qkv, do, o32, lse, dkv, grad, sem = refs[2 * micros + 2 * slots :]
    micro = pl.program_id(0)
    z, me, length = scal[0], scal[1], scal[2 + micro]
    total = slots * rows
    runs = slots * len(masks)
    places = list(row_places(slots, masks, rows, z, me))
    base = micro * rows

    def incoming(m):
        out = []
        for t, (j, at, to, n) in enumerate(places):
            from_, to_ = pl.ds(at, n), pl.ds(to, n)
            out.append(pltpu.make_async_copy(pieces[m][j].at[from_], qkv.at[to_], sem.at[t]))
            far = pl.ds(pl.multiple_of(base + at, n), n)
            out.append(pltpu.make_async_copy(dos[j].at[far], do.at[to_], sem.at[runs + t]))
        out.append(pltpu.make_async_copy(kept[m][0], o32, sem.at[2 * runs]))
        out.append(pltpu.make_async_copy(kept[m][1], lse, sem.at[2 * runs + 1]))
        return out

    for m in range(micros):

        @pl.when(micro == m)
        def _(m=m):
            copies = incoming(m)
            for cp in copies:
                cp.start()
            for cp in copies:
                cp.wait()

    bias = key_bias(total, length)
    causal = diag_mask(blk)
    dkv[...] = jnp.zeros_like(dkv)
    scale = HEAD_DIM**-0.5
    factor = scale * LOG2E
    D = HEAD_DIM
    for i in range(total // blk):
        lo = i * blk
        q, dy = qkv[lo : lo + blk, :D], do[lo : lo + blk, :]
        delta = jnp.sum(dy.astype(f32) * o32[lo : lo + blk, :], axis=1, keepdims=True)
        level = lse[lo : lo + blk, :]
        dq = None
        for start, stop in ((lo, lo + blk), (0, lo)):
            if start == stop:
                continue
            keys, vals = qkv[start:stop, D : 2 * D], qkv[start:stop, 2 * D :]
            s = dot_nt(q, keys) * factor + bias[:, start:stop]
            if start == lo:
                s = jnp.where(causal, s, masked_score)
            p = jnp.exp2(s - level)
            ds = (p * (dot_nt(dy, vals) - delta)).astype(bf16)
            part = dot(ds, keys)
            dq = part if dq is None else dq + part
            dkv[start:stop, :D] += dot_t(ds, q)
            dkv[start:stop, D:] += dot_t(p.astype(bf16), dy)
        grad[lo : lo + blk, :D] = (dq * scale).astype(bf16)
    grad[:, D : 2 * D] = (dkv[:, :D] * scale).astype(bf16)
    grad[:, 2 * D :] = dkv[:, D:].astype(bf16)
    copies = []
    for t, (j, at, to, n) in enumerate(places):
        far = pl.ds(pl.multiple_of(base + at, n), n)
        cp = pltpu.make_async_copy(grad.at[pl.ds(to, n)], outs[j].at[far], sem.at[t])
        cp.start()
        copies.append(cp)
    for cp in copies:
        cp.wait()


def attend_back(scal, pieces, kept, dos, masks):
    micros, slots = len(pieces), len(dos)
    rows = dos[0].shape[0] // micros
    total = slots * rows
    hbm = pl.BlockSpec(memory_space=pl.ANY)
    return pl.pallas_call(
        functools.partial(attend_back_kernel, slots, masks, rows, 256, micros),
        out_shape=[jax.ShapeDtypeStruct((micros * rows, 3 * HEAD_DIM), bf16)] * slots,
        grid=(micros,),
        in_specs=[pl.BlockSpec(memory_space=pltpu.SMEM)] + [hbm] * ((micros + 1) * slots + 2 * micros),
        out_specs=[hbm] * slots,
        scratch_shapes=[
            pltpu.VMEM((total, 3 * HEAD_DIM), bf16),
            pltpu.VMEM((total, HEAD_DIM), bf16),
            pltpu.VMEM((total, HEAD_DIM), f32),
            pltpu.VMEM((total, 1), f32),
            pltpu.VMEM((total, 2 * HEAD_DIM), f32),
            pltpu.VMEM((total, 3 * HEAD_DIM), bf16),
            pltpu.SemaphoreType.DMA((2 * slots * len(masks) + 2,)),
        ],
        cost_estimate=pl.CostEstimate(
            flops=micros * total * total * HEAD_DIM * 10,
            bytes_accessed=micros * total * HEAD_DIM * 24,
            transcendentals=micros * total * total // 2,
        ),
        name="attend_back",
    )(scal, *[p for ps in pieces for p in ps], *[k for ks in kept for k in ks], *dos)


def mlp_back_kernel(n, *refs):
    grads, dw, gates, ups = refs[: 2 * n], refs[2 * n], refs[2 * n + 1 :][:n], refs[3 * n + 1 :][:n]
    tok, outs, tok_out = refs[4 * n + 1], refs[4 * n + 2 : 6 * n + 2], refs[6 * n + 2]
    w = dw[...]
    half = grads[0].shape[0]
    for i, x in enumerate(grads):
        m, t = i // 2, slice(i % 2 * half, (i % 2 + 1) * half)
        a = dot_nt(x[...], w)
        g, u = gates[m][t, :], ups[m][t, :]
        s = jax.nn.sigmoid(g)
        outs[m][t, :] = (a * u * s * (1.0 + g * (1.0 - s))).astype(bf16)
        outs[n + m][t, :] = (a * g * s).astype(bf16)
    tok_out[0] = tok[0]


def mlp_back(line, grads, down_weight, gates, ups):
    n = len(gates)
    half, width = grads[0].shape
    rows = 2 * half
    ff = down_weight.shape[0]
    t = min(ff, 256)
    tall = pl.BlockSpec((rows, t), lambda i: (0, i))
    smem = pl.BlockSpec(memory_space=pltpu.SMEM)
    full = jax.ShapeDtypeStruct((rows, ff), bf16)
    *out, line.token = pl.pallas_call(
        functools.partial(mlp_back_kernel, n),
        out_shape=[full] * (2 * n) + [jax.ShapeDtypeStruct((1,), jnp.int32)],
        grid=(ff // t,),
        in_specs=[pl.BlockSpec((half, width), lambda i: (0, 0))] * (2 * n)
        + [pl.BlockSpec((t, width), lambda i: (i, 0))]
        + [tall] * (2 * n)
        + [smem],
        out_specs=[tall] * (2 * n) + [smem],
        cost_estimate=pl.CostEstimate(
            flops=2 * n * rows * width * ff,
            bytes_accessed=2 * width * ff + n * (2 * rows * width + 12 * rows * ff),
            transcendentals=n * rows * ff,
        ),
        name="mlp_back",
    )(*grads, down_weight, *gates, *ups, line.token)
    return out[:n], out[n:]


def hidden_back_kernel(n, *refs):
    gate_grads, gw, up_grads, uw = refs[:n], refs[n], refs[n + 1 : 2 * n + 1], refs[2 * n + 1]
    tok, out, tok_out = refs[2 * n + 2 :]
    g, u = gw[...], uw[...]
    for m in range(n):
        out[m] = (dot_nt(gate_grads[m][...], g) + dot_nt(up_grads[m][...], u)).astype(bf16)
    tok_out[0] = tok[0]


def hidden_back(line, gate_grads, gate_weight, up_grads, up_weight):
    n = len(gate_grads)
    rows, ff = gate_grads[0].shape
    width = gate_weight.shape[0]
    t = min(width, 256)
    all_ = pl.BlockSpec((rows, ff), lambda i: (0, 0), pipeline_mode=pl.Buffered(1))
    tile = pl.BlockSpec((t, ff), lambda i: (i, 0))
    smem = pl.BlockSpec(memory_space=pltpu.SMEM)
    out, line.token = pl.pallas_call(
        functools.partial(hidden_back_kernel, n),
        out_shape=[
            jax.ShapeDtypeStruct((n, rows, width), bf16),
            jax.ShapeDtypeStruct((1,), jnp.int32),
        ],
        grid=(width // t,),
        in_specs=[all_] * n + [tile] + [all_] * n + [tile, smem],
        out_specs=[pl.BlockSpec((n, rows, t), lambda i: (0, 0, i)), smem],
        cost_estimate=pl.CostEstimate(
            flops=4 * n * rows * width * ff,
            bytes_accessed=4 * width * ff + n * (4 * rows * ff + 2 * rows * width),
            transcendentals=0,
        ),
        name="hidden_back",
    )(*gate_grads, gate_weight, *up_grads, up_weight, line.token)
    return out


def turn_kernel(n, *refs):
    out, tok_out = refs[n + 1 :]
    at = 0
    for x in refs[:n]:
        out[:, at : at + x.shape[0]] = x[...].T
        at += x.shape[0]
    tok_out[0] = refs[n][0]


def turn(line, pieces, m=0, count=1):
    counts = [x.shape[0] // count for x in pieces]
    rows, cols = sum(counts), pieces[0].shape[1]
    t = min(cols, 512)
    smem = pl.BlockSpec(memory_space=pltpu.SMEM)
    out, line.token = pl.pallas_call(
        functools.partial(turn_kernel, len(pieces)),
        out_shape=[
            jax.ShapeDtypeStruct((cols, rows), pieces[0].dtype),
            jax.ShapeDtypeStruct((1,), jnp.int32),
        ],
        grid=(cols // t,),
        in_specs=[pl.BlockSpec((n, t), lambda i: (m, i)) for n in counts] + [smem],
        out_specs=[pl.BlockSpec((t, rows), lambda i: (i, 0)), smem],
        cost_estimate=pl.CostEstimate(flops=0, bytes_accessed=4 * rows * cols, transcendentals=0),
        name="turn",
    )(*pieces, line.token)
    return out


def gathered_attend(piece, pos, length):
    rows, local = piece.shape[0], piece.shape[1] // 3
    heads = local // HEAD_DIM
    q = piece[:, :local].reshape(rows, heads, HEAD_DIM)
    kv = lax.all_gather(piece[:, local:], SEQ, axis=0, tiled=True)
    n = kv.shape[0]
    k = kv[:, :local].reshape(n, heads, HEAD_DIM)
    v = kv[:, local:].reshape(n, heads, HEAD_DIM)
    base = jnp.arange(n // rows, dtype=jnp.int32) * rows
    own = pos - lax.axis_index(SEQ) * rows
    key_pos = (base[:, None] + own[None, :]).reshape(n)
    allowed = (key_pos[None, :] <= pos[:, None]) & (key_pos[None, :] < length)
    allowed = allowed[:, None, :]
    s = jnp.einsum(TO_KEYS, q, k, preferred_element_type=f32) * HEAD_DIM**-0.5
    s = jnp.where(allowed, s, masked_score)
    top = jnp.max(s, axis=-1, keepdims=True)
    w = jnp.where(allowed, jnp.exp(s - top), 0.0)
    mass = jnp.sum(w, axis=-1, keepdims=True)
    mixed = jnp.einsum(TO_ROWS, w.astype(bf16), v, preferred_element_type=f32) / mass
    return mixed.reshape(rows, local).astype(bf16), (q, k, v, allowed, mixed, top + jnp.log(mass))


def gathered_back(kept, dy):
    q, k, v, allowed, mixed, level = kept
    rows, heads, _ = q.shape
    n = k.shape[0]
    dy = dy.reshape(rows, heads, HEAD_DIM)
    scale = HEAD_DIM**-0.5
    delta = jnp.sum(dy.astype(f32) * mixed, axis=-1, keepdims=True)
    s = jnp.einsum(TO_KEYS, q, k, preferred_element_type=f32) * scale
    p = jnp.where(allowed, jnp.exp(s - level), 0.0)
    dp = jnp.einsum(TO_KEYS, dy, v, preferred_element_type=f32)
    ds = (p * (dp - delta)).astype(bf16)
    dq = jnp.einsum(TO_ROWS, ds, k, preferred_element_type=f32) * scale
    dk = jnp.einsum(TO_HEADS, ds, q, preferred_element_type=f32) * scale
    dv = jnp.einsum(TO_HEADS, p.astype(bf16), dy, preferred_element_type=f32)
    local = heads * HEAD_DIM
    dkv = jnp.concatenate([dk.reshape(n, local), dv.reshape(n, local)], axis=1).astype(bf16)
    dkv = lax.psum_scatter(dkv, SEQ, scatter_dimension=0, tiled=True)
    return jnp.concatenate([dq.reshape(rows, local).astype(bf16), dkv.astype(bf16)], axis=1)


class Line:
    def __init__(self, token):
        self.token = token
        self.waits = {}

    def add(self, *tasks):
        for t in tasks:
            self.waits[t] = next(t)[0]

    def mark(self, *arrays):
        for x in arrays:
            x = lax.slice(x, (0,) * x.ndim, (1,) * x.ndim).reshape(1)
            self.token = self.token + (x.astype(f32) > 3.4e38).astype(jnp.int32)

    def step(self, *tasks):
        tasks = [t for t in tasks if t in self.waits]
        if not tasks:
            return []
        held = [self.waits.pop(t) for t in tasks]
        if jax.tree.leaves(held):
            held, self.token = lax.optimization_barrier((held, self.token))
        for t, v in zip(tasks, held):
            try:
                self.waits[t], out = t.send(v)
            except StopIteration as end:
                out = end.value
            self.mark(*jax.tree.leaves(out)[:1])
        return [t for t in tasks if t in self.waits]


def idle(n):
    for _ in range(n):
        yield (), ()


class Place:
    def __init__(self, n_seq):
        self.n = n_seq
        self.dp, self.z = lax.axis_index(DP), lax.axis_index(SEQ)
        self.swap = [(0, 1), (1, 0)]
        self.lo, self.hi = n_seq // 2 - 1, n_seq // 2
        self.mid = [(self.lo, self.hi), (self.hi, self.lo)]
        self.inward = [
            [(i, i + 1), (n_seq - 1 - i, n_seq - 2 - i)] for i in range(n_seq // 2 - 1)
        ]

    def ends(self, pairs):
        return functools.reduce(jnp.logical_or, [self.z == b for _, b in pairs])


def take_half(x, dp, own):
    half = x.shape[1] // 2
    return lax.dynamic_slice_in_dim(x, (dp if own else 1 - dp) * half, half, 1)


def task_a(at, outs, which, x_send, x_keep, grad, cols, out_col):
    half = x_keep.shape[1]
    g = (yield grad, ())[:, cols]
    send = dot_t(x_send, g).astype(bf16)
    got = yield lax.ppermute(send, DP, at.swap), send
    s = (dot_t(x_keep, g) + got.astype(f32)).astype(bf16)
    for pairs in at.inward:
        got = yield lax.ppermute(s, SEQ, pairs), s
        s = add_low(s, got)
    got = yield lax.ppermute(s, SEQ, at.mid), s
    s = add_low(s, got)
    for pairs in reversed(at.inward):
        pairs = [(b, a) for a, b in pairs]
        got = yield lax.ppermute(s, SEQ, pairs), s
        s = jnp.where(at.ends(pairs), got, s)
    outs[which] = lax.dynamic_update_slice(outs[which], s.astype(f32), (at.dp * half, out_col))
    got = yield lax.ppermute(s, DP, at.swap), s
    outs[which] = lax.dynamic_update_slice(
        outs[which], got.astype(f32), ((1 - at.dp) * half, out_col)
    )
    return ()


def task_b(at, outs, which, x, grad, cols, out_col):
    g = (yield grad, ())[:, cols]
    s = dot_t(x, g).astype(bf16)
    for pairs in at.inward:
        got = yield lax.ppermute(s, SEQ, pairs), s
        s = add_low(s, got)
    h = s.shape[1] // 2
    first = at.z == at.lo
    send = jnp.where(first, s[:, h:], s[:, :h])
    keep = jnp.where(first, s[:, :h], s[:, h:])
    got = yield lax.ppermute(send, SEQ, at.mid), (send, keep)
    keep = add_low(keep, got)
    n = at.n
    pairs = [(d * n + k, (1 - d) * n + k) for d in (0, 1) for k in (at.lo, at.hi)]
    got = yield lax.ppermute(keep, (DP, SEQ), pairs), keep
    keep = add_low(keep, got)
    got = yield lax.ppermute(keep, SEQ, at.mid), keep
    s = jnp.concatenate([jnp.where(first, keep, got), jnp.where(first, got, keep)], axis=1)
    for pairs in reversed(at.inward):
        pairs = [(b, a) for a, b in pairs]
        got = yield lax.ppermute(s, SEQ, pairs), s
        s = jnp.where(at.ends(pairs), got, s)
    outs[which] = lax.dynamic_update_slice(outs[which], s.astype(f32), (0, out_col))
    return None


class Round:
    def __init__(self):
        self.refs, self.loads, self.keys = [], {}, {}

    def ref(self, array):
        for i, r in enumerate(self.refs):
            if r is array:
                return i
        self.refs.append(array)
        return len(self.refs) - 1

    def load(self, name, array, rows, cols=None):
        cols = (0, array.shape[1]) if cols is None else cols
        self.loads[name] = ((rows[1], cols[1]), ((self.ref(array), rows, cols, 0, 0),))

    def load_down(self, name, arrays, cols):
        n = arrays[0].shape[0]
        parts = tuple((self.ref(x), (0, n), cols, i * n, 0) for i, x in enumerate(arrays))
        self.loads[name] = ((n * len(arrays), cols[1]), parts)

    def load_across(self, name, arrays, rows):
        n = arrays[0].shape[1]
        parts = tuple((self.ref(x), rows, (0, n), 0, i * n) for i, x in enumerate(arrays))
        self.loads[name] = ((rows[1], n * len(arrays)), parts)


def first_row(first, count, dp):
    if isinstance(first, int):
        return first
    own, base = first
    return pl.multiple_of(base + (dp if own else 1 - dp) * count, count)


def round_kernel(kind, loads, n_in, pieces, extras, stores, scal, tok, *refs):
    ins = refs[:n_in]
    outs = refs[n_in + 1 : n_in + 1 + bool(pieces) + bool(extras) + len(stores)]
    refs[n_in][0] = tok[0]
    scratch = refs[n_in + 1 + len(outs) :]
    bufs = dict(zip([l[0] for l in loads], scratch))
    rest = list(scratch[len(loads) :])
    out_bufs = {}
    for name, _ in pieces + extras:
        out_bufs[name] = rest.pop(0)
    f_bufs = [rest.pop(0) for _ in stores]
    in_sem, out_sem = rest
    dp, z, n = scal[0], scal[1], scal[2]
    outer = (z == 0) | (z == n - 1)
    first = z == n // 2 - 1
    waits = {}
    t = 0
    for name, _, parts in loads:
        waits[name] = []
        for i, (r0, rows), (c0, cols), to_row, to_col in parts:
            src = ins[i].at[pl.ds(first_row(r0, rows, dp), rows), pl.ds(c0, cols)]
            dst = bufs[name].at[pl.ds(to_row, rows), pl.ds(to_col, cols)]
            cp = pltpu.make_async_copy(src, dst, in_sem.at[t])
            cp.start()
            waits[name].append(cp)
            t += 1

    def get(name):
        for cp in waits.pop(name, ()):
            cp.wait()
        return bufs[name]

    done = []
    slot = [0]

    def ship(src, dst):
        cp = pltpu.make_async_copy(src, dst, out_sem.at[slot[0]])
        slot[0] += 1
        cp.start()
        done.append(cp)

    where_out = {}
    k = 0
    for group in (pieces, extras):
        if group:
            at = 0
            for name, rows in group:
                where_out[name] = outs[k].at[pl.ds(at, rows)]
                at += rows
            k += 1

    def emit(name):
        if name in where_out:
            ship(out_bufs[name], where_out[name])

    def tiles(rows):
        t = min(rows, 256)
        return [slice(i, i + t) for i in range(0, rows, t)]

    have = lambda *names: all(n in bufs for n in names)
    low = lambda a, b: (a.astype(f32) + b.astype(f32)).astype(bf16)
    finals = {}
    if kind == "X":
        if have("a4r"):
            got, own, out = get("a4r"), get("a4o"), out_bufs["a4"]
            for t in tiles(out.shape[0]):
                out[t, :] = jnp.where(outer, got[t, :], own[t, :])
            emit("a4")
            finals["a4"] = out
        if have("b2r"):
            got, own, out = get("b2r"), get("b2o"), out_bufs["b2"]
            for t in tiles(out.shape[0]):
                out[t, :] = low(own[t, :], got[t, :])
            emit("b2")
        if have("a0g"):
            g, x, out = get("a0g"), get("a0x"), out_bufs["a0"]
            for t in tiles(out.shape[0]):
                out[t, :] = dot(x[t, :], g[...]).astype(bf16)
            emit("a0")
    if kind == "O":
        a_in, a_out = have("s1g"), have("s3r")
        if a_in:
            g, x, got, s1 = get("s1g"), get("s1x"), get("s1r"), out_bufs["s1"]
            for t in tiles(s1.shape[0]):
                s1[t, :] = (dot(x[t, :], g[...]) + got[t, :].astype(f32)).astype(bf16)
            emit("s1")
        if a_in or a_out:
            out = out_bufs["a"]
            n_in = s1.shape[0] if a_in else 0
            n_out = bufs["s3r"].shape[0] if a_out else 0
            if a_out:
                own, got = get("s3o"), get("s3r")
            for t in tiles(out.shape[0]):
                v = s1[t, :] if t.start < n_in else None
                if t.start < n_out:
                    u = low(own[t, :], got[t, :])
                    v = u if v is None else jnp.where(outer, v, u)
                out[t, :] = v
            emit("a")
        b_in, b_out = have("t0g"), have("t4r")
        if b_in:
            g, x, t0 = get("t0g"), get("t0x"), out_bufs["t0"]
            for t in tiles(t0.shape[0]):
                t0[t, :] = dot(x[t, :], g[...]).astype(bf16)
            emit("t0")
        if b_in or b_out:
            out = out_bufs["b"]
            n_in = t0.shape[0] if b_in else 0
            h = bufs["t4r"].shape[0] if b_out else 0
            if b_out:
                own, got = get("t4o"), get("t4r")
            for o in tiles(out.shape[0]):
                v = t0[o, :] if o.start < n_in else None
                if o.start < 2 * h:
                    back = h if o.start >= h else 0
                    t = slice(o.start - back, o.stop - back)
                    mine = jnp.logical_not(first) if back else first
                    u = jnp.where(mine, own[t, :], got[t, :])
                    v = u if v is None else jnp.where(outer, v, u)
                out[o, :] = v
            emit("b")
        if have("af"):
            finals["af"] = get("af")
    if kind == "M":
        if have("a2r"):
            own, got, out = get("a2o"), get("a2r"), out_bufs["a2"]
            for t in tiles(out.shape[0]):
                out[t, :] = low(own[t, :], got[t, :])
            emit("a2")
        if have("b3r"):
            own, got, out = get("b3o"), get("b3r"), out_bufs["b3"]
            for t in tiles(out.shape[0]):
                out[t, :] = low(own[t, :], got[t, :])
            emit("b3")
        if have("b1o"):
            own, got, out, keep = get("b1o"), get("ob"), out_bufs["b1"], out_bufs["keep"]
            h = out.shape[0]
            for t in tiles(h):
                o = slice(h + t.start, h + t.stop)
                top, bottom = low(own[t, :], got[t, :]), low(own[o, :], got[o, :])
                out[t, :] = jnp.where(first, bottom, top)
                keep[t, :] = jnp.where(first, top, bottom)
            emit("b1")
            emit("keep")
        if have("fino"):
            own, got = get("fino"), get("ob")
            finals["fin"] = (got, own)
    for i, (name, r0, rows, col) in enumerate(stores):
        src, buf = finals[name], f_bufs[i]
        for t in tiles(buf.shape[0]):
            if name == "fin":
                buf[t, :] = jnp.where(outer, src[0][t, :], src[1][t, :]).astype(f32)
            else:
                buf[t, :] = src[t, :].astype(f32)
        dst = outs[len(outs) - len(stores) + i]
        ship(buf, dst.at[pl.ds(first_row(r0, rows, dp), rows), pl.ds(col, buf.shape[1])])
    for cp in done:
        cp.wait()


class Rounds:
    def __init__(self, at, outs, line):
        self.at, self.outs, self.line = at, outs, line
        self.a, self.b = {}, {}
        self.got = {}
        self.r = 0
        self.swap_outer = [(0, 1), (1, 0), (2, 3), (3, 2)]
        self.scal = jnp.stack([at.dp, at.z, jnp.int32(at.n)]).astype(jnp.int32)

    def piece(self, kind, r, name, own=False, some=None):
        sent, got, table = self.got[kind, r]
        at = 0
        for k, rows in table:
            if k == name:
                return (sent if own else got), (at, rows if some is None else some)
            at += rows

    def run(self, kind, b, pieces, extras, stores, flops):
        rows = {n: r for n, r in pieces + extras}
        w = self.width
        loads = tuple((k,) + v for k, v in b.loads.items())
        any_ = pl.BlockSpec(memory_space=pl.ANY)
        smem = pl.BlockSpec(memory_space=pltpu.SMEM)
        shapes, aliases = [jax.ShapeDtypeStruct((1,), jnp.int32)], {}
        if pieces:
            shapes.append(jax.ShapeDtypeStruct((sum(r for _, r in pieces), w), bf16))
        if extras:
            shapes.append(jax.ShapeDtypeStruct((sum(r for _, r in extras), w), bf16))
        for which, *_ in stores:
            aliases[2 + len(b.refs) + len(aliases)] = len(shapes)
            shapes.append(jax.ShapeDtypeStruct(self.outs[which].shape, f32))
        scratch = [pltpu.VMEM(shape, bf16) for _, shape, _ in loads]
        scratch += [pltpu.VMEM((rows[n], w), bf16) for n, _ in pieces + extras]
        scratch += [pltpu.VMEM((r, w), f32) for _, _, _, r, _ in stores]
        n_out = len(pieces) + len(extras) + len(stores)
        n_load = sum(len(parts) for _, _, parts in loads)
        scratch += [pltpu.SemaphoreType.DMA((n_load,)), pltpu.SemaphoreType.DMA((n_out,))]
        moved = sum(m * n * 2 for _, (m, n), _ in loads) + sum(rows.values()) * w * 2
        moved += sum(r * w * 4 for _, _, _, r, _ in stores)
        n_in = len(b.refs) + len(stores)
        out = pl.pallas_call(
            functools.partial(
                round_kernel, kind, loads, n_in, tuple(pieces), tuple(extras),
                tuple(s[1:] for s in stores),
            ),
            out_shape=shapes,
            in_specs=[smem, smem] + [any_] * n_in,
            out_specs=[smem] + [any_] * (len(shapes) - 1),
            input_output_aliases=aliases,
            scratch_shapes=scratch,
            cost_estimate=pl.CostEstimate(flops=flops, bytes_accessed=moved, transcendentals=0),
            name="round_" + kind.lower(),
        )(self.scal, self.line.token, *b.refs, *[self.outs[s[0]] for s in stores])
        self.line.token, *out = out
        for which, *_ in reversed(stores):
            self.outs[which] = out.pop()
        extra = out.pop() if extras else None
        if pieces:
            axis, pairs = {
                "X": (DP, self.at.swap), "O": (SEQ, self.swap_outer), "M": (SEQ, self.at.mid),
            }[kind]
            self.got[kind, self.r] = (out[0], lax.ppermute(out[0], axis, pairs), pieces)
        return extra

    def step_x(self):
        r, A, B = self.r, self.a, self.b
        b, pieces, stores, flops = Round(), [], [], 0
        if r in A:
            c = A[r]
            half, tok = c["rows"][1] // 2, sum(x.shape[1] for x in c["x"])
            b.load_down("a0g", c["grad"], c["cols"])
            b.load_across("a0x", c["x"], ((False, c["rows"][0]), half))
            pieces.append(("a0", half))
            flops += 2 * half * tok * c["cols"][1]
        if r - 6 in A:
            c = A[r - 6]
            rows = c["rows"][1] // 2
            b.load("a4r", *self.piece("O", r - 2, "a", False, rows))
            b.load("a4o", *self.piece("O", r - 2, "a", True, rows))
            pieces.append(("a4", rows))
            stores.append((c["which"], "a4", (True, c["rows"][0]), rows, c["col"]))
        if r - 3 in B:
            c = B[r - 3]
            b.load("b2r", *self.piece("M", r - 2, "b1"))
            b.load("b2o", *c["keep"])
            pieces.append(("b2", b.loads["b2r"][0][0]))
        if pieces:
            self.run("X", b, pieces, [], stores, flops)

    def step_o(self):
        r, A, B = self.r, self.a, self.b
        b, pieces, extras, stores, flops = Round(), [], [], [], 0
        if r - 1 in A:
            c = A[r - 1]
            half, tok = c["rows"][1] // 2, sum(x.shape[1] for x in c["x"])
            b.load_down("s1g", c["grad"], c["cols"])
            b.load_across("s1x", c["x"], ((True, c["rows"][0]), half))
            b.load("s1r", *self.piece("X", r - 1, "a0"))
            extras.append(("s1", half))
            flops += 2 * half * tok * c["cols"][1]
        if r - 4 in A:
            b.load("s3o", *self.piece("M", r - 2, "a2", True))
            b.load("s3r", *self.piece("M", r - 2, "a2"))
        if r - 1 in A or r - 4 in A:
            sizes = [A[k]["rows"][1] // 2 for k in (r - 1, r - 4) if k in A]
            pieces.append(("a", max(sizes)))
        if r in B:
            c = B[r]
            rows, tok = c["rows"][1], sum(x.shape[1] for x in c["x"])
            b.load_down("t0g", c["grad"], c["cols"])
            b.load_across("t0x", c["x"], c["rows"])
            extras.append(("t0", rows))
            flops += 2 * rows * tok * c["cols"][1]
        if r - 6 in B:
            b.load("t4o", *self.piece("M", r - 2, "b3", True))
            b.load("t4r", *self.piece("M", r - 2, "b3"))
        if r in B or r - 6 in B:
            pieces.append(("b", max(B[k]["rows"][1] for k in (r, r - 6) if k in B)))
        if r - 7 in A:
            c = A.pop(r - 7)
            b.load("af", *self.piece("X", r - 1, "a4"))
            first = (False, c["rows"][0])
            stores.append((c["which"], "af", first, b.loads["af"][0][0], c["col"]))
        if pieces or stores:
            extra = self.run("O", b, pieces, extras, stores, flops)
            at = 0
            for name, n in extras:
                (A[r - 1] if name == "s1" else B[r])[name] = (extra, (at, n))
                at += n

    def step_m(self):
        r, A, B = self.r, self.a, self.b
        b, pieces, extras, stores = Round(), [], [], []
        if r - 2 in A:
            rows = A[r - 2]["rows"][1] // 2
            b.load("a2o", *A[r - 2]["s1"])
            b.load("a2r", *self.piece("O", r - 1, "a", False, rows))
            pieces.append(("a2", rows))
        if r - 1 in B or r - 7 in B:
            b.load("ob", *self.piece("O", r - 1, "b"))
        if r - 1 in B:
            h = B[r - 1]["rows"][1] // 2
            b.load("b1o", *B[r - 1]["t0"])
            pieces.append(("b1", h))
            extras.append(("keep", h))
        if r - 4 in B:
            b.load("b3o", *self.piece("X", r - 1, "b2", True))
            b.load("b3r", *self.piece("X", r - 1, "b2"))
            pieces.append(("b3", b.loads["b3r"][0][0]))
        if r - 7 in B:
            c = B.pop(r - 7)
            b.load("fino", *self.piece("O", r - 1, "b", True, c["rows"][1]))
            stores.append((c["which"], "fin", c["rows"][0], c["rows"][1], c["col"]))
        if pieces or stores:
            extra = self.run("M", b, pieces, extras, stores, 0)
            if extras:
                B[r - 1]["keep"] = (extra, (0, h))


def blank_kernel(*outs):
    pass


def blanks(shapes):
    return pl.pallas_call(
        blank_kernel,
        out_shape=[jax.ShapeDtypeStruct(s, f32) for s in shapes],
        out_specs=[pl.BlockSpec(memory_space=pl.ANY)] * len(shapes),
    )()


def gather_steps(x, n, axis=0, wait=0):
    got = None
    for b in reversed(bits_of(n)):
        if got is not None:
            x = jnp.concatenate([x, got], axis=axis)
        got = lax.ppermute(x, MP, xor_perm(n, b))
        if wait:
            yield (), x
            yield from idle(wait - 1)
            got = yield got, ()
        else:
            got = yield got, x
    return [x, got]


def joined(pieces, axis=0):
    return jnp.concatenate(pieces, axis=axis)


def scatter_steps(x, n, axis=0, wait=0):
    for b in bits_of(n):
        half = x.shape[axis] // 2
        keep = lax.slice_in_dim(x, 0, half, axis=axis)
        send = lax.slice_in_dim(x, half, 2 * half, axis=axis)
        got = lax.ppermute(send, MP, xor_perm(n, b))
        if wait:
            yield (), (send, keep)
            yield from idle(wait - 1)
            got = yield got, ()
        else:
            got = yield got, (send, keep)
        x = keep.astype(f32) + got.astype(f32)
        if 2 * b < n:
            x = x.astype(bf16)
    return x.astype(f32)


def sum_rows_steps(x, n):
    masks = row_masks(n)
    for b in bits_of(n):
        got = yield lax.ppermute(x, MP, xor_perm(n, b)), x
        got = got.reshape(x.shape[:-1] + (n, -1))
        order = [masks.index(m ^ b) for m in masks]
        got = jnp.stack([got[..., k, :] for k in order], axis=-2)
        x = x + got.reshape(x.shape)
    return x


def exchange_steps(pieces, n):
    got = yield exchange(pieces, n)[1:], pieces[1:]
    return [pieces[0]] + list(got)


class Layer:
    pass


def forward_task(c, m):
    f = c.fwd[m]
    own = c.tokens[m]
    length = c.lengths[m, 0]
    x = f.x = yield from gather_steps(own, c.n_mp)
    proj = dot(joined(x), c.qkv_weight)
    local = c.local
    squares = jnp.stack(
        [jnp.sum(jnp.square(proj[:, t * local : (t + 1) * local]), axis=1) for t in (0, 1)], axis=0
    )
    squares = yield from sum_rows_steps(squares, c.n_mp)
    inv = lax.rsqrt(squares / c.width + epsilon).T
    pieces = rope_call(c.slots, c.z_arr, proj, inv, c.cos, c.sin, c.qg, c.kg)
    if c.by_heads:
        scal = jnp.stack([c.z, c.me, length]).astype(jnp.int32)
        f.pieces = yield from exchange_steps(pieces, c.n_seq)
        mixed, f.kept = attend(scal, f.pieces, c.masks)
        mixed = yield from exchange_steps(mixed, c.n_seq)
        mixed = join_heads(c.z_arr, mixed)
    else:
        mixed, f.kept = gathered_attend(pieces[0], c.pos, length)
    attended = yield from scatter_steps(dot(mixed, c.o_weight).astype(bf16), c.n_mp)
    attn_inv = inv_rms(attended)
    hidden = own.astype(f32) + attended * attn_inv * c.attn_gain
    mlp_in = yield from gather_steps(hidden.astype(bf16), c.n_mp)
    f.mlp_in = mlp_in
    rows_in = joined(mlp_in)
    f.gate, f.up = dot(rows_in, c.gate_weight), dot(rows_in, c.up_weight)
    f.act = (f.gate * jax.nn.sigmoid(f.gate) * f.up).astype(bf16)
    mlp_out = yield from scatter_steps(dot(f.act, c.down_weight).astype(bf16), c.n_mp)
    mlp_inv = inv_rms(mlp_out)
    f.layer = (hidden + mlp_out * mlp_inv * c.mlp_gain).astype(bf16)
    f.seeds = c.cotangent[m].astype(f32) * (c.own_pos < length).astype(f32)[:, None]
    mlp_grad, gain_rows = norm_backward(mlp_out, mlp_inv, c.mlp_gain, f.seeds)
    f.mlp_gain = jnp.sum(gain_rows, axis=0)
    f.mlp_grad = yield from gather_steps(mlp_grad.astype(bf16), c.n_mp)
    f.proj, f.inv, f.mixed, f.attended, f.attn_inv = proj, inv, mixed, attended, attn_inv
    return ()


def backward_task(c):
    n, rows, fwd = len(c.fwd), c.rows, c.fwd
    yield (), ()
    gates = mlp_back(
        c.line, [x for f in fwd for x in f.mlp_grad], c.down_weight, [f.gate for f in fwd], [f.up for f in fwd]
    )
    for f, f.gate_grad, f.up_grad in zip(fwd, *gates):
        pass
    yield (), ()
    back = hidden_back(c.line, gates[0], c.gate_weight, gates[1], c.up_weight)
    back = yield from scatter_steps(back, c.n_mp, 1, c.far)
    hidden_grad, attn_grad = [], []
    for m, f in enumerate(fwd):
        hidden_grad.append(f.seeds + back[m])
        e, gain_rows = norm_backward(f.attended, f.attn_inv, c.attn_gain, hidden_grad[m])
        f.attn_gain = jnp.sum(gain_rows, axis=0)
        attn_grad.append(e.astype(bf16))
    attn_grad = yield from gather_steps(jnp.stack(attn_grad), c.n_mp, 1, c.far)
    c.attn_grad = [x.reshape(-1, c.width) for x in attn_grad]
    c.attn_grad_all = attn_grad = joined(attn_grad, 1).reshape(n * rows, c.width)
    dy = dot_nt(attn_grad, c.o_weight).astype(bf16)
    if c.by_heads:
        dys = split_heads(c.z_arr, dy, c.slots)
        dys = yield from exchange_steps(dys, c.n_seq)
        scal = jnp.concatenate([jnp.stack([c.z, c.me]), c.lengths[:, 0]]).astype(jnp.int32)
        grads = attend_back(scal, [f.pieces for f in fwd], [f.kept for f in fwd], dys, c.masks)
        grads = yield from exchange_steps(grads, c.n_seq)
    else:
        grads = [gathered_back(f.kept, dy[m * rows : (m + 1) * rows]) for m, f in enumerate(fwd)]
        grads = [jnp.concatenate(grads, axis=0)]
    tables = (c.cos, c.sin, c.qg, c.kg)
    cross = []
    for m, f in enumerate(fwd):
        e, f.gains = cross_call(c.slots, m, c.z_arr, grads, f.proj, f.inv, *tables)
        cross.append(e.T)
    cross = yield from sum_rows_steps(jnp.concatenate(cross, axis=0), c.n_mp)
    for m, f in enumerate(fwd):
        e = cross[2 * m : 2 * m + 2].T
        f.qkv_grad = raw_call(
            c.slots, c.width, m, c.z_arr, grads, f.proj, f.inv, e, *tables
        )
    yield (), [f.qkv_grad for f in fwd]
    back = jnp.stack([dot_nt(f.qkv_grad, c.qkv_weight).astype(bf16) for f in fwd])
    back = yield from scatter_steps(back, c.n_mp, 1, c.far)
    c.input_grad = jnp.stack(hidden_grad) + back
    return c.input_grad


def turning_task(c):
    yield (), ()
    c.attn_grad_t = []
    for m in range(len(c.fwd)):
        c.attn_grad_t.append(turn(c.line, c.attn_grad, m, len(c.fwd)))
        yield (), ()


def gains_task(c):
    yield (), ()
    gains = sum(f.gains for f in c.fwd)
    gains = lax.dynamic_update_slice(jnp.zeros((2, c.width), f32), gains, (0, c.me * c.local))
    gains = jnp.concatenate(
        [gains, sum(f.attn_gain for f in c.fwd)[None], sum(f.mlp_gain for f in c.fwd)[None]], axis=0
    )
    for name, n in ((MP, c.n_mp), (SEQ, c.n_seq), (DP, c.n_dp)):
        for b in bits_of(n):
            got = lax.ppermute(gains, name, xor_perm(n, b))
            yield (), gains
            if c.rounds:
                yield from idle(1)
            got = yield got, ()
            gains = gains + got
    c.gains = gains
    return gains


def per_device(
    n_dp, n_seq, n_mp,
    tokens, lengths, cotangent, q_weight, k_weight, v_weight, o_weight, q_gain, k_gain,
    attn_gain, gate_weight, up_weight, down_weight, mlp_gain,
):
    c = Layer()
    micros, own_rows, width = tokens.shape
    rows = own_rows * n_mp
    local = q_weight.shape[1]
    heads = local // HEAD_DIM
    ff = gate_weight.shape[1]
    me, z = lax.axis_index(MP), lax.axis_index(SEQ)
    c.tokens, c.lengths, c.cotangent, c.o_weight = tokens, lengths, cotangent, o_weight
    c.gate_weight, c.up_weight, c.down_weight = gate_weight, up_weight, down_weight
    c.attn_gain, c.mlp_gain = attn_gain, mlp_gain
    c.n_dp, c.n_seq, c.n_mp, c.rows, c.width, c.local = n_dp, n_seq, n_mp, rows, width, local
    c.me, c.z, c.masks = me, z, row_masks(n_mp)
    c.by_heads = heads == n_seq
    c.slots = n_seq if c.by_heads else 1
    c.z_arr = z.astype(jnp.int32).reshape(1)
    c.qkv_weight = jnp.concatenate([q_weight, k_weight, v_weight], axis=1)
    c.qg = lax.dynamic_slice_in_dim(q_gain, me * local, local)[None]
    c.kg = lax.dynamic_slice_in_dim(k_gain, me * local, local)[None]
    block = jnp.asarray(c.masks, jnp.int32) ^ me
    steps = jnp.arange(own_rows, dtype=jnp.int32)
    c.pos = z * rows + (block[:, None] * own_rows + steps).reshape(-1)
    c.own_pos = z * rows + me * own_rows + steps
    frequency = rope_base ** (-(jnp.arange(HALF, dtype=f32) * 2.0 / HEAD_DIM))
    angles = c.pos.astype(f32)[:, None] * frequency[None, :]
    cos, sin = jnp.cos(angles), jnp.sin(angles)
    c.cos = jnp.concatenate([cos, cos], axis=1)
    c.sin = jnp.concatenate([-sin, sin], axis=1)
    c.fwd = [Layer() for _ in range(micros)]

    at = Place(n_seq)
    c.rounds = rounds = n_seq == 4
    line = c.line = Line(jnp.zeros((1,), jnp.int32))
    fw = [forward_task(c, m) for m in range(micros)]
    line.add(*fw)
    def turned(m, name):
        f = c.fwd[m]
        rows_ = getattr(f, name)
        setattr(f, name + "_t", turn(line, rows_ if isinstance(rows_, list) else [rows_]))

    extra = {"a": (0, "x"), "b": (1, "x"), "c": (0, "act"), "d": (1, "act"), "e": (0, "mlp_in"), "f": (1, "mlp_in")}
    order = ORDER if (micros, n_mp, c.by_heads) == (2, 4, True) and rounds else ""
    for act in order:
        if act in extra:
            turned(*extra[act])
        else:
            line.step(fw[int(act)])
    while any(t in line.waits for t in fw):
        for t in fw:
            line.step(t)

    c.far = 0
    each = lambda name: [getattr(f, name) for f in c.fwd]
    outs = list(blanks(
        [(ff, width), (width, ff), (width, ff)]
        + [(width, local)] * 3
        + [(width, local) if rounds else (local, width)]
    ))
    back, gains = backward_task(c), gains_task(c)
    side = []
    line.add(back)

    stack = lambda lists: [x for pieces in lists for x in pieces]
    both = lambda name: jnp.concatenate(each(name), axis=0)
    both2 = lambda name: jnp.concatenate(stack(each(name)), axis=0)

    def work(key):
        if rounds:
            return {
                "down": lambda: (each("act_t"), stack(each("mlp_grad"))),
                "gate": lambda: (each("mlp_in_t"), each("gate_grad")),
                "up": lambda: (each("mlp_in_t"), each("up_grad")),
                "o": lambda: (c.attn_grad_t, each("mixed")),
                "qkv": lambda: (each("x_t"), each("qkv_grad")),
            }[key]()
        return {
            "down": lambda: (both("act"), both2("mlp_grad")),
            "gate": lambda: (both2("mlp_in"), both("gate_grad")),
            "up": lambda: (both2("mlp_in"), both("up_grad")),
            "o": lambda: (both("mixed"), c.attn_grad_all),
            "qkv": lambda: (both2("x"), both("qkv_grad")),
        }[key]()

    done, live = {}, []
    if rounds:
        reducer = Rounds(at, outs, line)
        reducer.width = local // 2

    def rows_of(key):
        if key not in done:
            done[key] = work(key)
        return done[key]

    def one_round(new_a, new_b, script=""):
        if rounds:
            for new, table in ((new_a, reducer.a), (new_b, reducer.b)):
                if new is not None:
                    key, which, first, n, col, span = new
                    x, grad = rows_of(key)
                    table[reducer.r] = dict(
                        x=x, grad=grad, cols=(first, n), which=which, col=col, rows=span
                    )
            for act in script:
                if act in "XOM":
                    getattr(reducer, "step_" + act.lower())()
                else:
                    line.step({"c": back, "t": turning, "g": gains}[act])
            reducer.r += 1
            return
        for new, kind in ((new_a, "a"), (new_b, "b")):
            if new is not None:
                key, which, first, n, col, _ = new
                x, grad = rows_of(key)
                if kind == "a":
                    if key + "/" not in done:
                        done[key + "/"] = (take_half(x, at.dp, False), take_half(x, at.dp, True))
                    t = task_a(at, outs, which, *done[key + "/"], grad, slice(first, first + n), col)
                else:
                    t = task_b(at, outs, which, x, grad, slice(first, first + n), col)
                line.add(t)
                live.append(t)
        live[:] = line.step(*live)
        for t in side:
            line.step(t)

    unit = local // 2
    cut = lambda key, which, n, u=unit, first=0, parts=1: [
        (key, which, first + t, u, t, (k * (width // parts), width // parts))
        for t in range(0, n, u)
        for k in range(parts)
    ]
    ready = {
        "down": lambda: True,
        "gate": lambda: all(hasattr(f, "up_grad") for f in c.fwd),
        "o": lambda: len(c.attn_grad_t) == micros if rounds else hasattr(c, "attn_grad_all"),
        "qkv": lambda: all(hasattr(f, "qkv_grad") for f in c.fwd),
    }
    ready["up"] = ready["gate"]
    todo = cut("down", 0, width) + cut("gate", 1, ff) + cut("up", 2, ff)
    todo += cut("o", 6, local) if rounds else cut("o", 6, width, width // 2)
    for t in range(3):
        todo += cut("qkv", 3 + t, local, first=t * local, parts=2 if rounds and t else 1)
    c.attn_grad_t = []
    if rounds:
        for m in range(micros):
            for name in ("x", "act", "mlp_in"):
                if not hasattr(c.fwd[m], name + "_t"):
                    turned(m, name)
        turning = turning_task(c)
        line.add(turning)
    else:
        side = [back]
    count_a = len(todo) // 2

    def take():
        for i, chunk in enumerate(todo):
            if ready[chunk[0]]():
                return todo.pop(i)
        return None

    gains_on = False
    r = taken_a = 0
    while todo or any(t in line.waits for t in (back, gains)) or (
        reducer.a or reducer.b if rounds else live
    ):
        late = ready["qkv"]()
        if late and not gains_on:
            gains_on = True
            side.append(gains)
            line.add(gains)
        new_a = take() if taken_a < count_a else None
        taken_a += new_a is not None
        script = SCRIPT[r] if r < len(SCRIPT) else "XgOcMg"
        lone = rounds and r < len(SCRIPT) and script[-1:] == "-"
        new_b = None if lone else take()
        one_round(new_a, new_b, script.strip("-") if rounds else "")
        r += 1
    return (
        jnp.stack(each("layer")),
        c.input_grad,
        outs[3],
        outs[4],
        outs[5],
        outs[6].T if rounds else outs[6],
        c.gains[0],
        c.gains[1],
        c.gains[2],
        outs[1],
        outs[2],
        outs[0],
        c.gains[3],
    )


SCRIPT = (
    "XOc",
    "XcOM",
    "XcOM",
    "XcOM",
    "XOcM",
    "XOcM",
    "XOMc",
    "XOtMtc",
    "XOcM",
    "XcOMc",
    "XOMc",
)

ORDER = "00101011ab0000010101ce0101011df111"


def solution(mesh):
    n_dp, n_seq, n_mp = (mesh.shape[a] for a in (DP, SEQ, MP))
    assert n_dp == 2
    rows = P(None, (DP, SEQ, MP), None)
    cols, flat, all_ = P(None, MP), P(MP, None), P()
    return jax.shard_map(
        functools.partial(per_device, n_dp, n_seq, n_mp),
        mesh=mesh,
        in_specs=(rows, P(None, DP), rows, cols, cols, cols, flat, all_, all_, all_, cols, cols, flat, all_),
        out_specs=(rows, rows, cols, cols, cols, flat, all_, all_, all_, cols, cols, flat, all_),
        check_vma=False,
    )
```

```python
import functools

import jax
import jax.numpy as jnp
from jax import lax
from jax.experimental import pallas as pl
from jax.experimental.pallas import tpu as pltpu
from jax.sharding import PartitionSpec as P

HEAD_DIM = 128
HALF = HEAD_DIM // 2
DP, SEQ, MP = "dp", "seq", "mp"
TO_KEYS, TO_ROWS, TO_HEADS = "shd,khd->shk", "shk,khd->shd", "shk,shd->khd"
epsilon = 1e-06
rope_base = 500000.0
masked_score = -1e30
LOG2E = 1.4426950408889634

f32 = jnp.float32
bf16 = jnp.bfloat16


def add_low(a, b):
    return (a.astype(f32) + b.astype(f32)).astype(bf16)


def bits_of(n):
    out = []
    b = 1
    while b < n:
        out.append(b)
        b *= 2
    return out


def xor_perm(n, b):
    return [(i, i ^ b) for i in range(n)]


def row_masks(n):
    masks = [0]
    for b in reversed(bits_of(n)):
        masks = masks + [m | b for m in masks]
    return masks


def inv_rms(v):
    return lax.rsqrt(jnp.mean(v * v, axis=-1, keepdims=True) + epsilon)


def norm_backward(source, inverse, gain_vec, upstream):
    normed = source * inverse
    weighted = upstream * gain_vec
    back = inverse * (weighted - normed * jnp.mean(weighted * normed, axis=-1, keepdims=True))
    return back, upstream * normed


def dot_t(a, b):
    return lax.dot_general(a, b, (((0,), (0,)), ((), ())), preferred_element_type=f32)


def dot_nt(a, b):
    return lax.dot_general(a, b, (((1,), (1,)), ((), ())), preferred_element_type=f32)


def dot(a, b):
    return jnp.dot(a, b, preferred_element_type=f32)


def rope_kernel(slots, width, local, z_ref, proj, inv, cos, sin, qg, kg, *outs):
    z = z_ref[0]
    c, s = cos[...], sin[...]
    for j in range(slots):
        base = (z ^ j) * width if slots > 1 else 0
        for h in range(width // HEAD_DIM):
            at = base + h * HEAD_DIM
            at = pl.multiple_of(at, HEAD_DIM) if slots > 1 else at
            for part, gain in ((0, qg), (1, kg)):
                raw = proj[:, pl.ds(part * local + at, HEAD_DIM)]
                v = raw * inv[:, part : part + 1] * gain[:, pl.ds(at, HEAD_DIM)]
                v = v * c + pltpu.roll(v, HALF, 1) * s
                lo = part * width + h * HEAD_DIM
                outs[j][:, lo : lo + HEAD_DIM] = v.astype(bf16)
            lo = 2 * width + h * HEAD_DIM
            outs[j][:, lo : lo + HEAD_DIM] = proj[:, pl.ds(2 * local + at, HEAD_DIM)].astype(bf16)


def rope_call(slots, z, proj, inv, cos, sin, qg, kg):
    rows, local = proj.shape[0], proj.shape[1] // 3
    width = local // slots
    blk = min(rows, 256)
    row = lambda n: pl.BlockSpec((blk, n), lambda i, *_: (i, 0))
    vec = pl.BlockSpec((1, local), lambda i, *_: (0, 0))
    return pl.pallas_call(
        functools.partial(rope_kernel, slots, width, local),
        out_shape=[jax.ShapeDtypeStruct((rows, 3 * width), bf16)] * slots,
        grid_spec=pltpu.PrefetchScalarGridSpec(
            num_scalar_prefetch=1,
            grid=(rows // blk,),
            in_specs=[row(3 * local), row(2), row(HEAD_DIM), row(HEAD_DIM), vec, vec],
            out_specs=[row(3 * width)] * slots,
        ),
        cost_estimate=pl.CostEstimate(
            flops=rows * local * 12, bytes_accessed=rows * local * 18, transcendentals=0
        ),
    )(z, proj, inv, cos, sin, qg, kg)


def unrope(grad, c, s):
    g = grad.astype(f32)
    return g * c - pltpu.roll(g, HALF, 1) * s


def cross_kernel(slots, width, local, z_ref, *refs):
    grads = refs[:slots]
    proj, inv, cos, sin, qg, kg, cross, gains = refs[slots:]
    z = z_ref[0]
    c, s = cos[...], sin[...]

    @pl.when(pl.program_id(0) == 0)
    def _():
        gains[...] = jnp.zeros_like(gains)

    for part, gain in ((0, qg), (1, kg)):
        total = None
        for j in range(slots):
            base = (z ^ j) * width if slots > 1 else 0
            for h in range(width // HEAD_DIM):
                at = base + h * HEAD_DIM
                at = pl.multiple_of(at, HEAD_DIM) if slots > 1 else at
                lo = part * width + h * HEAD_DIM
                g = unrope(grads[j][:, lo : lo + HEAD_DIM], c, s)
                gr = g * proj[:, pl.ds(part * local + at, HEAD_DIM)]
                w = gr * gain[:, pl.ds(at, HEAD_DIM)]
                total = w if total is None else total + w
                col = jnp.sum(gr * inv[:, part : part + 1], axis=0, keepdims=True)
                gains[part : part + 1, pl.ds(at, HEAD_DIM)] += col
        cross[:, part : part + 1] = jnp.sum(total, axis=1, keepdims=True)


def raw_kernel(slots, width, local, d, z_ref, *refs):
    grads = refs[:slots]
    proj, inv, cross, cos, sin, qg, kg, out = refs[slots:]
    z = z_ref[0]
    c, s = cos[...], sin[...]
    for j in range(slots):
        base = (z ^ j) * width if slots > 1 else 0
        for h in range(width // HEAD_DIM):
            at = base + h * HEAD_DIM
            at = pl.multiple_of(at, HEAD_DIM) if slots > 1 else at
            for part, gain in ((0, qg), (1, kg)):
                lo = part * width + h * HEAD_DIM
                g = unrope(grads[j][:, lo : lo + HEAD_DIM], c, s)
                r = inv[:, part : part + 1]
                w = g * gain[:, pl.ds(at, HEAD_DIM)] * r
                k = r * r * r * (cross[:, part : part + 1] * (1.0 / d))
                w = w - proj[:, pl.ds(part * local + at, HEAD_DIM)] * k
                out[:, pl.ds(part * local + at, HEAD_DIM)] = w.astype(bf16)
            lo = 2 * width + h * HEAD_DIM
            out[:, pl.ds(2 * local + at, HEAD_DIM)] = grads[j][:, lo : lo + HEAD_DIM]


def cross_call(slots, m, z, grads, proj, inv, cos, sin, qg, kg):
    rows, local = proj.shape[0], proj.shape[1] // 3
    width = local // slots
    blk = min(rows, 256)
    far = lambda n: pl.BlockSpec((blk, n), lambda i, *_: (i + m * (rows // blk), 0))
    row = lambda n: pl.BlockSpec((blk, n), lambda i, *_: (i, 0))
    vec = pl.BlockSpec((1, local), lambda i, *_: (0, 0))
    return pl.pallas_call(
        functools.partial(cross_kernel, slots, width, local),
        out_shape=[
            jax.ShapeDtypeStruct((rows, 2), f32),
            jax.ShapeDtypeStruct((2, local), f32),
        ],
        grid_spec=pltpu.PrefetchScalarGridSpec(
            num_scalar_prefetch=1,
            grid=(rows // blk,),
            in_specs=[far(3 * width)] * slots
            + [row(3 * local), row(2), row(HEAD_DIM), row(HEAD_DIM), vec, vec],
            out_specs=[row(2), pl.BlockSpec((2, local), lambda i, *_: (0, 0))],
        ),
        cost_estimate=pl.CostEstimate(
            flops=rows * local * 20, bytes_accessed=rows * local * 18, transcendentals=0
        ),
    )(z, *grads, proj, inv, cos, sin, qg, kg)


def raw_call(slots, d, m, z, grads, proj, inv, cross, cos, sin, qg, kg):
    rows, local = proj.shape[0], proj.shape[1] // 3
    width = local // slots
    blk = min(rows, 256)
    far = lambda n: pl.BlockSpec((blk, n), lambda i, *_: (i + m * (rows // blk), 0))
    row = lambda n: pl.BlockSpec((blk, n), lambda i, *_: (i, 0))
    vec = pl.BlockSpec((1, local), lambda i, *_: (0, 0))
    return pl.pallas_call(
        functools.partial(raw_kernel, slots, width, local, d),
        out_shape=jax.ShapeDtypeStruct((rows, 3 * local), bf16),
        grid_spec=pltpu.PrefetchScalarGridSpec(
            num_scalar_prefetch=1,
            grid=(rows // blk,),
            in_specs=[far(3 * width)] * slots
            + [row(3 * local), row(2), row(2), row(HEAD_DIM), row(HEAD_DIM), vec, vec],
            out_specs=row(3 * local),
        ),
        cost_estimate=pl.CostEstimate(
            flops=rows * local * 20, bytes_accessed=rows * local * 24, transcendentals=0
        ),
    )(z, *grads, proj, inv, cross, cos, sin, qg, kg)


def join_kernel(slots, width, z_ref, *refs):
    z = z_ref[0]
    out = refs[slots]
    for j in range(slots):
        out[:, pl.ds(pl.multiple_of((z ^ j) * width, HEAD_DIM), width)] = refs[j][...]


def join_heads(z, pieces):
    rows, width = pieces[0].shape
    slots = len(pieces)
    blk = min(rows, 256)
    return pl.pallas_call(
        functools.partial(join_kernel, slots, width),
        out_shape=jax.ShapeDtypeStruct((rows, slots * width), bf16),
        grid_spec=pltpu.PrefetchScalarGridSpec(
            num_scalar_prefetch=1,
            grid=(rows // blk,),
            in_specs=[pl.BlockSpec((blk, width), lambda i, *_: (i, 0))] * slots,
            out_specs=pl.BlockSpec((blk, slots * width), lambda i, *_: (i, 0)),
        ),
    )(z, *pieces)


def split_kernel(slots, width, z_ref, x, *outs):
    z = z_ref[0]
    for j in range(slots):
        outs[j][...] = x[:, pl.ds(pl.multiple_of((z ^ j) * width, HEAD_DIM), width)]


def split_heads(z, x, slots):
    rows, local = x.shape
    width = local // slots
    blk = min(rows, 256)
    return pl.pallas_call(
        functools.partial(split_kernel, slots, width),
        out_shape=[jax.ShapeDtypeStruct((rows, width), bf16)] * slots,
        grid_spec=pltpu.PrefetchScalarGridSpec(
            num_scalar_prefetch=1,
            grid=(rows // blk,),
            in_specs=[pl.BlockSpec((blk, local), lambda i, *_: (i, 0))],
            out_specs=[pl.BlockSpec((blk, width), lambda i, *_: (i, 0))] * slots,
        ),
    )(z, x)


def exchange(pieces, n):
    return [p if j == 0 else lax.ppermute(p, SEQ, xor_perm(n, j)) for j, p in enumerate(pieces)]


def row_places(slots, masks, rows, z, me):
    count = rows // len(masks)
    for j in range(slots):
        for k, m in enumerate(masks):
            yield j, k * count, pl.multiple_of((z ^ j) * rows + (me ^ m) * count, count), count


def key_bias(total, length):
    pos = lax.broadcasted_iota(jnp.int32, (1, total), 1)
    return jnp.where(pos < length, 0.0, masked_score).astype(f32)


def diag_mask(size):
    r = lax.broadcasted_iota(jnp.int32, (size, size), 0)
    c = lax.broadcasted_iota(jnp.int32, (size, size), 1)
    return c <= r


def attend_kernel(slots, masks, rows, blk, scal, *refs):
    pieces, outs = refs[:slots], refs[slots : 2 * slots]
    o32, lse, qkv, o16, sem = refs[2 * slots :]
    z, me, length = scal[0], scal[1], scal[2]
    total = slots * rows
    copies = []
    for t, (j, at, to, n) in enumerate(row_places(slots, masks, rows, z, me)):
        cp = pltpu.make_async_copy(pieces[j].at[pl.ds(at, n)], qkv.at[pl.ds(to, n)], sem.at[t])
        cp.start()
        copies.append(cp)
    bias = key_bias(total, length)
    causal = diag_mask(blk)
    for cp in copies:
        cp.wait()
    factor = HEAD_DIM**-0.5 * LOG2E
    for i in range(total // blk):
        lo = i * blk
        q = qkv[lo : lo + blk, :HEAD_DIM]
        s = dot_nt(q, qkv[lo : lo + blk, HEAD_DIM : 2 * HEAD_DIM]) * factor
        s = jnp.where(causal, s + bias[:, lo : lo + blk], masked_score)
        top = jnp.max(s, axis=1, keepdims=True)
        if i:
            before = dot_nt(q, qkv[:lo, HEAD_DIM : 2 * HEAD_DIM]) * factor + bias[:, :lo]
            top = jnp.maximum(top, jnp.max(before, axis=1, keepdims=True))
        p = jnp.exp2(s - top)
        mass = jnp.sum(p, axis=1, keepdims=True)
        acc = dot(p.astype(bf16), qkv[lo : lo + blk, 2 * HEAD_DIM :])
        if i:
            p = jnp.exp2(before - top)
            mass = mass + jnp.sum(p, axis=1, keepdims=True)
            acc = acc + dot(p.astype(bf16), qkv[:lo, 2 * HEAD_DIM :])
        acc = acc / mass
        o32[lo : lo + blk, :] = acc
        o16[lo : lo + blk, :] = acc.astype(bf16)
        lse[lo : lo + blk, :] = top + jnp.log(mass) * LOG2E
    copies = []
    for t, (j, at, to, n) in enumerate(row_places(slots, masks, rows, z, me)):
        cp = pltpu.make_async_copy(o16.at[pl.ds(to, n)], outs[j].at[pl.ds(at, n)], sem.at[t])
        cp.start()
        copies.append(cp)
    for cp in copies:
        cp.wait()


def attend(scal, pieces, masks):
    slots = len(pieces)
    rows = pieces[0].shape[0]
    total = slots * rows
    hbm = pl.BlockSpec(memory_space=pl.ANY)
    vmem = pl.BlockSpec(memory_space=pltpu.VMEM)
    out = pl.pallas_call(
        functools.partial(attend_kernel, slots, masks, rows, 256),
        out_shape=[jax.ShapeDtypeStruct((rows, HEAD_DIM), bf16)] * slots
        + [
            jax.ShapeDtypeStruct((total, HEAD_DIM), f32),
            jax.ShapeDtypeStruct((total, 1), f32),
        ],
        in_specs=[pl.BlockSpec(memory_space=pltpu.SMEM)] + [hbm] * slots,
        out_specs=[hbm] * slots + [vmem, vmem],
        scratch_shapes=[
            pltpu.VMEM((total, 3 * HEAD_DIM), bf16),
            pltpu.VMEM((total, HEAD_DIM), bf16),
            pltpu.SemaphoreType.DMA((slots * len(masks),)),
        ],
        cost_estimate=pl.CostEstimate(
            flops=total * total * HEAD_DIM * 4,
            bytes_accessed=total * HEAD_DIM * 12,
            transcendentals=total * total // 2,
        ),
        name="attend",
    )(scal, *pieces)
    return out[:slots], (out[slots], out[slots + 1])


def attend_back_kernel(slots, masks, rows, blk, micros, scal, *refs):
    pieces = [refs[m * slots : (m + 1) * slots] for m in range(micros)]
    refs = refs[micros * slots :]
    kept = [refs[2 * m : 2 * m + 2] for m in range(micros)]
    dos, outs = refs[2 * micros : 2 * micros + slots], refs[2 * micros + slots :][:slots]
    qkv, do, o32, lse, dkv, grad, sem = refs[2 * micros + 2 * slots :]
    micro = pl.program_id(0)
    z, me, length = scal[0], scal[1], scal[2 + micro]
    total = slots * rows
    runs = slots * len(masks)
    places = list(row_places(slots, masks, rows, z, me))
    base = micro * rows

    def incoming(m):
        out = []
        for t, (j, at, to, n) in enumerate(places):
            from_, to_ = pl.ds(at, n), pl.ds(to, n)
            out.append(pltpu.make_async_copy(pieces[m][j].at[from_], qkv.at[to_], sem.at[t]))
            far = pl.ds(pl.multiple_of(base + at, n), n)
            out.append(pltpu.make_async_copy(dos[j].at[far], do.at[to_], sem.at[runs + t]))
        out.append(pltpu.make_async_copy(kept[m][0], o32, sem.at[2 * runs]))
        out.append(pltpu.make_async_copy(kept[m][1], lse, sem.at[2 * runs + 1]))
        return out

    for m in range(micros):

        @pl.when(micro == m)
        def _(m=m):
            copies = incoming(m)
            for cp in copies:
                cp.start()
            for cp in copies:
                cp.wait()

    bias = key_bias(total, length)
    causal = diag_mask(blk)
    dkv[...] = jnp.zeros_like(dkv)
    scale = HEAD_DIM**-0.5
    factor = scale * LOG2E
    D = HEAD_DIM
    for i in range(total // blk):
        lo = i * blk
        q, dy = qkv[lo : lo + blk, :D], do[lo : lo + blk, :]
        delta = jnp.sum(dy.astype(f32) * o32[lo : lo + blk, :], axis=1, keepdims=True)
        level = lse[lo : lo + blk, :]
        dq = None
        for start, stop in ((lo, lo + blk), (0, lo)):
            if start == stop:
                continue
            keys, vals = qkv[start:stop, D : 2 * D], qkv[start:stop, 2 * D :]
            s = dot_nt(q, keys) * factor + bias[:, start:stop]
            if start == lo:
                s = jnp.where(causal, s, masked_score)
            p = jnp.exp2(s - level)
            ds = (p * (dot_nt(dy, vals) - delta)).astype(bf16)
            part = dot(ds, keys)
            dq = part if dq is None else dq + part
            dkv[start:stop, :D] += dot_t(ds, q)
            dkv[start:stop, D:] += dot_t(p.astype(bf16), dy)
        grad[lo : lo + blk, :D] = (dq * scale).astype(bf16)
    grad[:, D : 2 * D] = (dkv[:, :D] * scale).astype(bf16)
    grad[:, 2 * D :] = dkv[:, D:].astype(bf16)
    copies = []
    for t, (j, at, to, n) in enumerate(places):
        far = pl.ds(pl.multiple_of(base + at, n), n)
        cp = pltpu.make_async_copy(grad.at[pl.ds(to, n)], outs[j].at[far], sem.at[t])
        cp.start()
        copies.append(cp)
    for cp in copies:
        cp.wait()


def attend_back(scal, pieces, kept, dos, masks):
    micros, slots = len(pieces), len(dos)
    rows = dos[0].shape[0] // micros
    total = slots * rows
    hbm = pl.BlockSpec(memory_space=pl.ANY)
    return pl.pallas_call(
        functools.partial(attend_back_kernel, slots, masks, rows, 256, micros),
        out_shape=[jax.ShapeDtypeStruct((micros * rows, 3 * HEAD_DIM), bf16)] * slots,
        grid=(micros,),
        in_specs=[pl.BlockSpec(memory_space=pltpu.SMEM)] + [hbm] * ((micros + 1) * slots + 2 * micros),
        out_specs=[hbm] * slots,
        scratch_shapes=[
            pltpu.VMEM((total, 3 * HEAD_DIM), bf16),
            pltpu.VMEM((total, HEAD_DIM), bf16),
            pltpu.VMEM((total, HEAD_DIM), f32),
            pltpu.VMEM((total, 1), f32),
            pltpu.VMEM((total, 2 * HEAD_DIM), f32),
            pltpu.VMEM((total, 3 * HEAD_DIM), bf16),
            pltpu.SemaphoreType.DMA((2 * slots * len(masks) + 2,)),
        ],
        cost_estimate=pl.CostEstimate(
            flops=micros * total * total * HEAD_DIM * 10,
            bytes_accessed=micros * total * HEAD_DIM * 24,
            transcendentals=micros * total * total // 2,
        ),
        name="attend_back",
    )(scal, *[p for ps in pieces for p in ps], *[k for ks in kept for k in ks], *dos)


def mlp_back_kernel(n, *refs):
    grads, dw, gates, ups = refs[: 2 * n], refs[2 * n], refs[2 * n + 1 :][:n], refs[3 * n + 1 :][:n]
    tok, outs, tok_out = refs[4 * n + 1], refs[4 * n + 2 : 6 * n + 2], refs[6 * n + 2]
    w = dw[...]
    half = grads[0].shape[0]
    for i, x in enumerate(grads):
        m, t = i // 2, slice(i % 2 * half, (i % 2 + 1) * half)
        a = dot_nt(x[...], w)
        g, u = gates[m][t, :], ups[m][t, :]
        s = jax.nn.sigmoid(g)
        outs[m][t, :] = (a * u * s * (1.0 + g * (1.0 - s))).astype(bf16)
        outs[n + m][t, :] = (a * g * s).astype(bf16)
    tok_out[0] = tok[0]


def mlp_back(line, grads, down_weight, gates, ups):
    n = len(gates)
    half, width = grads[0].shape
    rows = 2 * half
    ff = down_weight.shape[0]
    t = min(ff, 256)
    tall = pl.BlockSpec((rows, t), lambda i: (0, i))
    smem = pl.BlockSpec(memory_space=pltpu.SMEM)
    full = jax.ShapeDtypeStruct((rows, ff), bf16)
    *out, line.token = pl.pallas_call(
        functools.partial(mlp_back_kernel, n),
        out_shape=[full] * (2 * n) + [jax.ShapeDtypeStruct((1,), jnp.int32)],
        grid=(ff // t,),
        in_specs=[pl.BlockSpec((half, width), lambda i: (0, 0))] * (2 * n)
        + [pl.BlockSpec((t, width), lambda i: (i, 0))]
        + [tall] * (2 * n)
        + [smem],
        out_specs=[tall] * (2 * n) + [smem],
        cost_estimate=pl.CostEstimate(
            flops=2 * n * rows * width * ff,
            bytes_accessed=2 * width * ff + n * (2 * rows * width + 12 * rows * ff),
            transcendentals=n * rows * ff,
        ),
        name="mlp_back",
    )(*grads, down_weight, *gates, *ups, line.token)
    return out[:n], out[n:]


def hidden_back_kernel(n, *refs):
    gate_grads, gw, up_grads, uw = refs[:n], refs[n], refs[n + 1 : 2 * n + 1], refs[2 * n + 1]
    tok, keep, send, tok_out = refs[2 * n + 2 :]
    g, u = gw[...], uw[...]
    half = keep.shape[1]
    for m in range(n):
        v = (dot_nt(gate_grads[m][...], g) + dot_nt(up_grads[m][...], u)).astype(bf16)
        keep[m] = v[:half, :]
        send[m] = v[half:, :]
    tok_out[0] = tok[0]


def hidden_back(line, gate_grads, gate_weight, up_grads, up_weight):
    n = len(gate_grads)
    rows, ff = gate_grads[0].shape
    width = gate_weight.shape[0]
    t = min(width, 256)
    all_ = pl.BlockSpec((rows, ff), lambda i: (0, 0), pipeline_mode=pl.Buffered(1))
    tile = pl.BlockSpec((t, ff), lambda i: (i, 0))
    smem = pl.BlockSpec(memory_space=pltpu.SMEM)
    half = jax.ShapeDtypeStruct((n, rows // 2, width), bf16)
    part = pl.BlockSpec((n, rows // 2, t), lambda i: (0, 0, i))
    keep, send, line.token = pl.pallas_call(
        functools.partial(hidden_back_kernel, n),
        out_shape=[half, half, jax.ShapeDtypeStruct((1,), jnp.int32)],
        grid=(width // t,),
        in_specs=[all_] * n + [tile] + [all_] * n + [tile, smem],
        out_specs=[part, part, smem],
        cost_estimate=pl.CostEstimate(
            flops=4 * n * rows * width * ff,
            bytes_accessed=4 * width * ff + n * (4 * rows * ff + 2 * rows * width),
            transcendentals=0,
        ),
        name="hidden_back",
    )(*gate_grads, gate_weight, *up_grads, up_weight, line.token)
    return keep, send


def turn_kernel(n, *refs):
    out, tok_out = refs[n + 1 :]
    at = 0
    for x in refs[:n]:
        out[:, at : at + x.shape[0]] = x[...].T
        at += x.shape[0]
    tok_out[0] = refs[n][0]


def turn(line, pieces, m=0, count=1):
    counts = [x.shape[0] // count for x in pieces]
    rows, cols = sum(counts), pieces[0].shape[1]
    t = min(cols, 512)
    smem = pl.BlockSpec(memory_space=pltpu.SMEM)
    out, line.token = pl.pallas_call(
        functools.partial(turn_kernel, len(pieces)),
        out_shape=[
            jax.ShapeDtypeStruct((cols, rows), pieces[0].dtype),
            jax.ShapeDtypeStruct((1,), jnp.int32),
        ],
        grid=(cols // t,),
        in_specs=[pl.BlockSpec((n, t), lambda i: (m, i)) for n in counts] + [smem],
        out_specs=[pl.BlockSpec((t, rows), lambda i: (i, 0)), smem],
        cost_estimate=pl.CostEstimate(flops=0, bytes_accessed=4 * rows * cols, transcendentals=0),
        name="turn",
    )(*pieces, line.token)
    return out


def gathered_attend(piece, pos, length):
    rows, local = piece.shape[0], piece.shape[1] // 3
    heads = local // HEAD_DIM
    q = piece[:, :local].reshape(rows, heads, HEAD_DIM)
    kv = lax.all_gather(piece[:, local:], SEQ, axis=0, tiled=True)
    n = kv.shape[0]
    k = kv[:, :local].reshape(n, heads, HEAD_DIM)
    v = kv[:, local:].reshape(n, heads, HEAD_DIM)
    base = jnp.arange(n // rows, dtype=jnp.int32) * rows
    own = pos - lax.axis_index(SEQ) * rows
    key_pos = (base[:, None] + own[None, :]).reshape(n)
    allowed = (key_pos[None, :] <= pos[:, None]) & (key_pos[None, :] < length)
    allowed = allowed[:, None, :]
    s = jnp.einsum(TO_KEYS, q, k, preferred_element_type=f32) * HEAD_DIM**-0.5
    s = jnp.where(allowed, s, masked_score)
    top = jnp.max(s, axis=-1, keepdims=True)
    w = jnp.where(allowed, jnp.exp(s - top), 0.0)
    mass = jnp.sum(w, axis=-1, keepdims=True)
    mixed = jnp.einsum(TO_ROWS, w.astype(bf16), v, preferred_element_type=f32) / mass
    return mixed.reshape(rows, local).astype(bf16), (q, k, v, allowed, mixed, top + jnp.log(mass))


def gathered_back(kept, dy):
    q, k, v, allowed, mixed, level = kept
    rows, heads, _ = q.shape
    n = k.shape[0]
    dy = dy.reshape(rows, heads, HEAD_DIM)
    scale = HEAD_DIM**-0.5
    delta = jnp.sum(dy.astype(f32) * mixed, axis=-1, keepdims=True)
    s = jnp.einsum(TO_KEYS, q, k, preferred_element_type=f32) * scale
    p = jnp.where(allowed, jnp.exp(s - level), 0.0)
    dp = jnp.einsum(TO_KEYS, dy, v, preferred_element_type=f32)
    ds = (p * (dp - delta)).astype(bf16)
    dq = jnp.einsum(TO_ROWS, ds, k, preferred_element_type=f32) * scale
    dk = jnp.einsum(TO_HEADS, ds, q, preferred_element_type=f32) * scale
    dv = jnp.einsum(TO_HEADS, p.astype(bf16), dy, preferred_element_type=f32)
    local = heads * HEAD_DIM
    dkv = jnp.concatenate([dk.reshape(n, local), dv.reshape(n, local)], axis=1).astype(bf16)
    dkv = lax.psum_scatter(dkv, SEQ, scatter_dimension=0, tiled=True)
    return jnp.concatenate([dq.reshape(rows, local).astype(bf16), dkv.astype(bf16)], axis=1)


class Line:
    def __init__(self, token):
        self.token = token
        self.waits = {}

    def add(self, *tasks):
        for t in tasks:
            self.waits[t] = next(t)[0]

    def mark(self, *arrays):
        for x in arrays:
            x = lax.slice(x, (0,) * x.ndim, (1,) * x.ndim).reshape(1)
            self.token = self.token + (x.astype(f32) > 3.4e38).astype(jnp.int32)

    def step(self, *tasks):
        tasks = [t for t in tasks if t in self.waits]
        if not tasks:
            return []
        held = [self.waits.pop(t) for t in tasks]
        if jax.tree.leaves(held):
            held, self.token = lax.optimization_barrier((held, self.token))
        for t, v in zip(tasks, held):
            try:
                self.waits[t], out = t.send(v)
            except StopIteration as end:
                out = end.value
            self.mark(*jax.tree.leaves(out)[:1])
        return [t for t in tasks if t in self.waits]


def idle(n):
    for _ in range(n):
        yield (), ()


class Place:
    def __init__(self, n_seq):
        self.n = n_seq
        self.dp, self.z = lax.axis_index(DP), lax.axis_index(SEQ)
        self.swap = [(0, 1), (1, 0)]
        self.lo, self.hi = n_seq // 2 - 1, n_seq // 2
        self.mid = [(self.lo, self.hi), (self.hi, self.lo)]
        self.inward = [
            [(i, i + 1), (n_seq - 1 - i, n_seq - 2 - i)] for i in range(n_seq // 2 - 1)
        ]

    def ends(self, pairs):
        return functools.reduce(jnp.logical_or, [self.z == b for _, b in pairs])


def take_half(x, dp, own):
    half = x.shape[1] // 2
    return lax.dynamic_slice_in_dim(x, (dp if own else 1 - dp) * half, half, 1)


def task_a(at, outs, which, x_send, x_keep, grad, cols, out_col):
    half = x_keep.shape[1]
    g = (yield grad, ())[:, cols]
    send = dot_t(x_send, g).astype(bf16)
    got = yield lax.ppermute(send, DP, at.swap), send
    s = (dot_t(x_keep, g) + got.astype(f32)).astype(bf16)
    for pairs in at.inward:
        got = yield lax.ppermute(s, SEQ, pairs), s
        s = add_low(s, got)
    got = yield lax.ppermute(s, SEQ, at.mid), s
    s = add_low(s, got)
    for pairs in reversed(at.inward):
        pairs = [(b, a) for a, b in pairs]
        got = yield lax.ppermute(s, SEQ, pairs), s
        s = jnp.where(at.ends(pairs), got, s)
    outs[which] = lax.dynamic_update_slice(outs[which], s.astype(f32), (at.dp * half, out_col))
    got = yield lax.ppermute(s, DP, at.swap), s
    outs[which] = lax.dynamic_update_slice(
        outs[which], got.astype(f32), ((1 - at.dp) * half, out_col)
    )
    return ()


def task_b(at, outs, which, x, grad, cols, out_col):
    g = (yield grad, ())[:, cols]
    s = dot_t(x, g).astype(bf16)
    for pairs in at.inward:
        got = yield lax.ppermute(s, SEQ, pairs), s
        s = add_low(s, got)
    h = s.shape[1] // 2
    first = at.z == at.lo
    send = jnp.where(first, s[:, h:], s[:, :h])
    keep = jnp.where(first, s[:, :h], s[:, h:])
    got = yield lax.ppermute(send, SEQ, at.mid), (send, keep)
    keep = add_low(keep, got)
    n = at.n
    pairs = [(d * n + k, (1 - d) * n + k) for d in (0, 1) for k in (at.lo, at.hi)]
    got = yield lax.ppermute(keep, (DP, SEQ), pairs), keep
    keep = add_low(keep, got)
    got = yield lax.ppermute(keep, SEQ, at.mid), keep
    s = jnp.concatenate([jnp.where(first, keep, got), jnp.where(first, got, keep)], axis=1)
    for pairs in reversed(at.inward):
        pairs = [(b, a) for a, b in pairs]
        got = yield lax.ppermute(s, SEQ, pairs), s
        s = jnp.where(at.ends(pairs), got, s)
    outs[which] = lax.dynamic_update_slice(outs[which], s.astype(f32), (0, out_col))
    return None


class Round:
    def __init__(self):
        self.refs, self.loads, self.keys = [], {}, {}

    def ref(self, array):
        for i, r in enumerate(self.refs):
            if r is array:
                return i
        self.refs.append(array)
        return len(self.refs) - 1

    def load(self, name, array, rows, cols=None):
        cols = (0, array.shape[1]) if cols is None else cols
        self.loads[name] = ((rows[1], cols[1]), ((self.ref(array), rows, cols, 0, 0),))

    def load_down(self, name, arrays, cols):
        n = arrays[0].shape[0]
        parts = tuple((self.ref(x), (0, n), cols, i * n, 0) for i, x in enumerate(arrays))
        self.loads[name] = ((n * len(arrays), cols[1]), parts)

    def load_across(self, name, arrays, rows):
        n = arrays[0].shape[1]
        parts = tuple((self.ref(x), rows, (0, n), 0, i * n) for i, x in enumerate(arrays))
        self.loads[name] = ((rows[1], n * len(arrays)), parts)


def first_row(first, count, dp):
    if isinstance(first, int):
        return first
    own, base = first
    return pl.multiple_of(base + (dp if own else 1 - dp) * count, count)


def round_kernel(kind, loads, n_in, pieces, extras, stores, scal, tok, *refs):
    ins = refs[:n_in]
    outs = refs[n_in + 1 : n_in + 1 + bool(pieces) + bool(extras) + len(stores)]
    refs[n_in][0] = tok[0]
    scratch = refs[n_in + 1 + len(outs) :]
    bufs = dict(zip([l[0] for l in loads], scratch))
    rest = list(scratch[len(loads) :])
    out_bufs = {}
    for name, _ in pieces + extras:
        out_bufs[name] = rest.pop(0)
    f_bufs = [rest.pop(0) for _ in stores]
    in_sem, out_sem = rest
    dp, z, n = scal[0], scal[1], scal[2]
    outer = (z == 0) | (z == n - 1)
    first = z == n // 2 - 1
    waits = {}
    t = 0
    for name, _, parts in loads:
        waits[name] = []
        for i, (r0, rows), (c0, cols), to_row, to_col in parts:
            src = ins[i].at[pl.ds(first_row(r0, rows, dp), rows), pl.ds(c0, cols)]
            dst = bufs[name].at[pl.ds(to_row, rows), pl.ds(to_col, cols)]
            cp = pltpu.make_async_copy(src, dst, in_sem.at[t])
            cp.start()
            waits[name].append(cp)
            t += 1

    def get(name):
        for cp in waits.pop(name, ()):
            cp.wait()
        return bufs[name]

    done = []
    slot = [0]

    def ship(src, dst):
        cp = pltpu.make_async_copy(src, dst, out_sem.at[slot[0]])
        slot[0] += 1
        cp.start()
        done.append(cp)

    where_out = {}
    k = 0
    for group in (pieces, extras):
        if group:
            at = 0
            for name, rows in group:
                where_out[name] = outs[k].at[pl.ds(at, rows)]
                at += rows
            k += 1

    def emit(name):
        if name in where_out:
            ship(out_bufs[name], where_out[name])

    def tiles(rows):
        t = min(rows, 256)
        return [slice(i, i + t) for i in range(0, rows, t)]

    have = lambda *names: all(n in bufs for n in names)
    low = lambda a, b: (a.astype(f32) + b.astype(f32)).astype(bf16)
    finals = {}
    if kind == "X":
        if have("a4r"):
            got, own, out = get("a4r"), get("a4o"), out_bufs["a4"]
            for t in tiles(out.shape[0]):
                out[t, :] = jnp.where(outer, got[t, :], own[t, :])
            emit("a4")
            finals["a4"] = out
        if have("b2r"):
            got, own, out = get("b2r"), get("b2o"), out_bufs["b2"]
            for t in tiles(out.shape[0]):
                out[t, :] = low(own[t, :], got[t, :])
            emit("b2")
        if have("a0g"):
            g, x, out = get("a0g"), get("a0x"), out_bufs["a0"]
            for t in tiles(out.shape[0]):
                out[t, :] = dot(x[t, :], g[...]).astype(bf16)
            emit("a0")
    if kind == "O":
        a_in, a_out = have("s1g"), have("s3r")
        if a_in:
            g, x, got, s1 = get("s1g"), get("s1x"), get("s1r"), out_bufs["s1"]
            for t in tiles(s1.shape[0]):
                s1[t, :] = (dot(x[t, :], g[...]) + got[t, :].astype(f32)).astype(bf16)
            emit("s1")
        if a_in or a_out:
            out = out_bufs["a"]
            n_in = s1.shape[0] if a_in else 0
            n_out = bufs["s3r"].shape[0] if a_out else 0
            if a_out:
                own, got = get("s3o"), get("s3r")
            for t in tiles(out.shape[0]):
                v = s1[t, :] if t.start < n_in else None
                if t.start < n_out:
                    u = low(own[t, :], got[t, :])
                    v = u if v is None else jnp.where(outer, v, u)
                out[t, :] = v
            emit("a")
        b_in, b_out = have("t0g"), have("t4r")
        if b_in:
            g, x, t0 = get("t0g"), get("t0x"), out_bufs["t0"]
            for t in tiles(t0.shape[0]):
                t0[t, :] = dot(x[t, :], g[...]).astype(bf16)
            emit("t0")
        if b_in or b_out:
            out = out_bufs["b"]
            n_in = t0.shape[0] if b_in else 0
            h = bufs["t4r"].shape[0] if b_out else 0
            if b_out:
                own, got = get("t4o"), get("t4r")
            for o in tiles(out.shape[0]):
                v = t0[o, :] if o.start < n_in else None
                if o.start < 2 * h:
                    back = h if o.start >= h else 0
                    t = slice(o.start - back, o.stop - back)
                    mine = jnp.logical_not(first) if back else first
                    u = jnp.where(mine, own[t, :], got[t, :])
                    v = u if v is None else jnp.where(outer, v, u)
                out[o, :] = v
            emit("b")
        if have("af"):
            finals["af"] = get("af")
    if kind == "M":
        if have("a2r"):
            own, got, out = get("a2o"), get("a2r"), out_bufs["a2"]
            for t in tiles(out.shape[0]):
                out[t, :] = low(own[t, :], got[t, :])
            emit("a2")
        if have("b3r"):
            own, got, out = get("b3o"), get("b3r"), out_bufs["b3"]
            for t in tiles(out.shape[0]):
                out[t, :] = low(own[t, :], got[t, :])
            emit("b3")
        if have("b1o"):
            own, got, out, keep = get("b1o"), get("ob"), out_bufs["b1"], out_bufs["keep"]
            h = out.shape[0]
            for t in tiles(h):
                o = slice(h + t.start, h + t.stop)
                top, bottom = low(own[t, :], got[t, :]), low(own[o, :], got[o, :])
                out[t, :] = jnp.where(first, bottom, top)
                keep[t, :] = jnp.where(first, top, bottom)
            emit("b1")
            emit("keep")
        if have("fino"):
            own, got = get("fino"), get("ob")
            finals["fin"] = (got, own)
    for i, (name, r0, rows, col) in enumerate(stores):
        src, buf = finals[name], f_bufs[i]
        for t in tiles(buf.shape[0]):
            if name == "fin":
                buf[t, :] = jnp.where(outer, src[0][t, :], src[1][t, :]).astype(f32)
            else:
                buf[t, :] = src[t, :].astype(f32)
        dst = outs[len(outs) - len(stores) + i]
        ship(buf, dst.at[pl.ds(first_row(r0, rows, dp), rows), pl.ds(col, buf.shape[1])])
    for cp in done:
        cp.wait()


class Rounds:
    def __init__(self, at, outs, line):
        self.at, self.outs, self.line = at, outs, line
        self.a, self.b = {}, {}
        self.got = {}
        self.r = 0
        self.swap_outer = [(0, 1), (1, 0), (2, 3), (3, 2)]
        self.scal = jnp.stack([at.dp, at.z, jnp.int32(at.n)]).astype(jnp.int32)

    def piece(self, kind, r, name, own=False, some=None):
        sent, got, table = self.got[kind, r]
        at = 0
        for k, rows in table:
            if k == name:
                return (sent if own else got), (at, rows if some is None else some)
            at += rows

    def run(self, kind, b, pieces, extras, stores, flops):
        rows = {n: r for n, r in pieces + extras}
        w = self.width
        loads = tuple((k,) + v for k, v in b.loads.items())
        any_ = pl.BlockSpec(memory_space=pl.ANY)
        smem = pl.BlockSpec(memory_space=pltpu.SMEM)
        shapes, aliases = [jax.ShapeDtypeStruct((1,), jnp.int32)], {}
        if pieces:
            shapes.append(jax.ShapeDtypeStruct((sum(r for _, r in pieces), w), bf16))
        if extras:
            shapes.append(jax.ShapeDtypeStruct((sum(r for _, r in extras), w), bf16))
        for which, *_ in stores:
            aliases[2 + len(b.refs) + len(aliases)] = len(shapes)
            shapes.append(jax.ShapeDtypeStruct(self.outs[which].shape, f32))
        scratch = [pltpu.VMEM(shape, bf16) for _, shape, _ in loads]
        scratch += [pltpu.VMEM((rows[n], w), bf16) for n, _ in pieces + extras]
        scratch += [pltpu.VMEM((r, w), f32) for _, _, _, r, _ in stores]
        n_out = len(pieces) + len(extras) + len(stores)
        n_load = sum(len(parts) for _, _, parts in loads)
        scratch += [pltpu.SemaphoreType.DMA((n_load,)), pltpu.SemaphoreType.DMA((n_out,))]
        moved = sum(m * n * 2 for _, (m, n), _ in loads) + sum(rows.values()) * w * 2
        moved += sum(r * w * 4 for _, _, _, r, _ in stores)
        n_in = len(b.refs) + len(stores)
        out = pl.pallas_call(
            functools.partial(
                round_kernel, kind, loads, n_in, tuple(pieces), tuple(extras),
                tuple(s[1:] for s in stores),
            ),
            out_shape=shapes,
            in_specs=[smem, smem] + [any_] * n_in,
            out_specs=[smem] + [any_] * (len(shapes) - 1),
            input_output_aliases=aliases,
            scratch_shapes=scratch,
            cost_estimate=pl.CostEstimate(flops=flops, bytes_accessed=moved, transcendentals=0),
            name="round_" + kind.lower(),
        )(self.scal, self.line.token, *b.refs, *[self.outs[s[0]] for s in stores])
        self.line.token, *out = out
        for which, *_ in reversed(stores):
            self.outs[which] = out.pop()
        extra = out.pop() if extras else None
        if pieces:
            axis, pairs = {
                "X": (DP, self.at.swap), "O": (SEQ, self.swap_outer), "M": (SEQ, self.at.mid),
            }[kind]
            self.got[kind, self.r] = (out[0], lax.ppermute(out[0], axis, pairs), pieces)
        return extra

    def step_x(self):
        r, A, B = self.r, self.a, self.b
        b, pieces, stores, flops = Round(), [], [], 0
        if r in A:
            c = A[r]
            half, tok = c["rows"][1] // 2, sum(x.shape[1] for x in c["x"])
            b.load_down("a0g", c["grad"], c["cols"])
            b.load_across("a0x", c["x"], ((False, c["rows"][0]), half))
            pieces.append(("a0", half))
            flops += 2 * half * tok * c["cols"][1]
        if r - 6 in A:
            c = A[r - 6]
            rows = c["rows"][1] // 2
            b.load("a4r", *self.piece("O", r - 2, "a", False, rows))
            b.load("a4o", *self.piece("O", r - 2, "a", True, rows))
            pieces.append(("a4", rows))
            stores.append((c["which"], "a4", (True, c["rows"][0]), rows, c["col"]))
        if r - 3 in B:
            c = B[r - 3]
            b.load("b2r", *self.piece("M", r - 2, "b1"))
            b.load("b2o", *c["keep"])
            pieces.append(("b2", b.loads["b2r"][0][0]))
        if pieces:
            self.run("X", b, pieces, [], stores, flops)

    def step_o(self):
        r, A, B = self.r, self.a, self.b
        b, pieces, extras, stores, flops = Round(), [], [], [], 0
        if r - 1 in A:
            c = A[r - 1]
            half, tok = c["rows"][1] // 2, sum(x.shape[1] for x in c["x"])
            b.load_down("s1g", c["grad"], c["cols"])
            b.load_across("s1x", c["x"], ((True, c["rows"][0]), half))
            b.load("s1r", *self.piece("X", r - 1, "a0"))
            extras.append(("s1", half))
            flops += 2 * half * tok * c["cols"][1]
        if r - 4 in A:
            b.load("s3o", *self.piece("M", r - 2, "a2", True))
            b.load("s3r", *self.piece("M", r - 2, "a2"))
        if r - 1 in A or r - 4 in A:
            sizes = [A[k]["rows"][1] // 2 for k in (r - 1, r - 4) if k in A]
            pieces.append(("a", max(sizes)))
        if r in B:
            c = B[r]
            rows, tok = c["rows"][1], sum(x.shape[1] for x in c["x"])
            b.load_down("t0g", c["grad"], c["cols"])
            b.load_across("t0x", c["x"], c["rows"])
            extras.append(("t0", rows))
            flops += 2 * rows * tok * c["cols"][1]
        if r - 6 in B:
            b.load("t4o", *self.piece("M", r - 2, "b3", True))
            b.load("t4r", *self.piece("M", r - 2, "b3"))
        if r in B or r - 6 in B:
            pieces.append(("b", max(B[k]["rows"][1] for k in (r, r - 6) if k in B)))
        if r - 7 in A:
            c = A.pop(r - 7)
            b.load("af", *self.piece("X", r - 1, "a4"))
            first = (False, c["rows"][0])
            stores.append((c["which"], "af", first, b.loads["af"][0][0], c["col"]))
        if pieces or stores:
            extra = self.run("O", b, pieces, extras, stores, flops)
            at = 0
            for name, n in extras:
                (A[r - 1] if name == "s1" else B[r])[name] = (extra, (at, n))
                at += n

    def step_m(self):
        r, A, B = self.r, self.a, self.b
        b, pieces, extras, stores = Round(), [], [], []
        if r - 2 in A:
            rows = A[r - 2]["rows"][1] // 2
            b.load("a2o", *A[r - 2]["s1"])
            b.load("a2r", *self.piece("O", r - 1, "a", False, rows))
            pieces.append(("a2", rows))
        if r - 1 in B or r - 7 in B:
            b.load("ob", *self.piece("O", r - 1, "b"))
        if r - 1 in B:
            h = B[r - 1]["rows"][1] // 2
            b.load("b1o", *B[r - 1]["t0"])
            pieces.append(("b1", h))
            extras.append(("keep", h))
        if r - 4 in B:
            b.load("b3o", *self.piece("X", r - 1, "b2", True))
            b.load("b3r", *self.piece("X", r - 1, "b2"))
            pieces.append(("b3", b.loads["b3r"][0][0]))
        if r - 7 in B:
            c = B.pop(r - 7)
            b.load("fino", *self.piece("O", r - 1, "b", True, c["rows"][1]))
            stores.append((c["which"], "fin", c["rows"][0], c["rows"][1], c["col"]))
        if pieces or stores:
            extra = self.run("M", b, pieces, extras, stores, 0)
            if extras:
                B[r - 1]["keep"] = (extra, (0, h))


def blank_kernel(*outs):
    pass


def blanks(shapes):
    return pl.pallas_call(
        blank_kernel,
        out_shape=[jax.ShapeDtypeStruct(s, f32) for s in shapes],
        out_specs=[pl.BlockSpec(memory_space=pl.ANY)] * len(shapes),
    )()


def gather_steps(x, n, axis=0, wait=0):
    got = None
    for b in reversed(bits_of(n)):
        if got is not None:
            x = jnp.concatenate([x, got], axis=axis)
        got = lax.ppermute(x, MP, xor_perm(n, b))
        if wait:
            yield (), x
            yield from idle(wait - 1)
            got = yield got, ()
        else:
            got = yield got, x
    return [x, got]


def joined(pieces, axis=0):
    return jnp.concatenate(pieces, axis=axis)


def scatter_steps(x, n, axis=0, wait=0):
    for b in bits_of(n):
        if isinstance(x, tuple):
            keep, send = x
        else:
            half = x.shape[axis] // 2
            keep = lax.slice_in_dim(x, 0, half, axis=axis)
            send = lax.slice_in_dim(x, half, 2 * half, axis=axis)
        got = lax.ppermute(send, MP, xor_perm(n, b))
        if wait:
            yield (), (send, keep)
            yield from idle(wait - 1)
            got = yield got, ()
        else:
            got = yield got, (send, keep)
        x = keep.astype(f32) + got.astype(f32)
        if 2 * b < n:
            x = x.astype(bf16)
    return x.astype(f32)


def sum_rows_steps(x, n):
    masks = row_masks(n)
    for b in bits_of(n):
        got = yield lax.ppermute(x, MP, xor_perm(n, b)), x
        got = got.reshape(x.shape[:-1] + (n, -1))
        order = [masks.index(m ^ b) for m in masks]
        got = jnp.stack([got[..., k, :] for k in order], axis=-2)
        x = x + got.reshape(x.shape)
    return x


def exchange_steps(pieces, n):
    got = yield exchange(pieces, n)[1:], pieces[1:]
    return [pieces[0]] + list(got)


class Layer:
    pass


def forward_task(c, m):
    f = c.fwd[m]
    own = c.tokens[m]
    length = c.lengths[m, 0]
    x = f.x = yield from gather_steps(own, c.n_mp)
    proj = dot(joined(x), c.qkv_weight)
    local = c.local
    squares = jnp.stack(
        [jnp.sum(jnp.square(proj[:, t * local : (t + 1) * local]), axis=1) for t in (0, 1)], axis=0
    )
    squares = yield from sum_rows_steps(squares, c.n_mp)
    inv = lax.rsqrt(squares / c.width + epsilon).T
    pieces = rope_call(c.slots, c.z_arr, proj, inv, c.cos, c.sin, c.qg, c.kg)
    if c.by_heads:
        scal = jnp.stack([c.z, c.me, length]).astype(jnp.int32)
        f.pieces = yield from exchange_steps(pieces, c.n_seq)
        mixed, f.kept = attend(scal, f.pieces, c.masks)
        mixed = yield from exchange_steps(mixed, c.n_seq)
        mixed = join_heads(c.z_arr, mixed)
    else:
        mixed, f.kept = gathered_attend(pieces[0], c.pos, length)
    attended = yield from scatter_steps(dot(mixed, c.o_weight).astype(bf16), c.n_mp)
    attn_inv = inv_rms(attended)
    hidden = own.astype(f32) + attended * attn_inv * c.attn_gain
    mlp_in = yield from gather_steps(hidden.astype(bf16), c.n_mp)
    f.mlp_in = mlp_in
    rows_in = joined(mlp_in)
    f.gate, f.up = dot(rows_in, c.gate_weight), dot(rows_in, c.up_weight)
    f.act = (f.gate * jax.nn.sigmoid(f.gate) * f.up).astype(bf16)
    mlp_out = yield from scatter_steps(dot(f.act, c.down_weight).astype(bf16), c.n_mp)
    mlp_inv = inv_rms(mlp_out)
    f.layer = (hidden + mlp_out * mlp_inv * c.mlp_gain).astype(bf16)
    f.seeds = c.cotangent[m].astype(f32) * (c.own_pos < length).astype(f32)[:, None]
    mlp_grad, gain_rows = norm_backward(mlp_out, mlp_inv, c.mlp_gain, f.seeds)
    f.mlp_gain = jnp.sum(gain_rows, axis=0)
    f.mlp_grad = yield from gather_steps(mlp_grad.astype(bf16), c.n_mp)
    f.proj, f.inv, f.mixed, f.attended, f.attn_inv = proj, inv, mixed, attended, attn_inv
    return ()


def backward_task(c):
    n, rows, fwd = len(c.fwd), c.rows, c.fwd
    yield (), ()
    gates = mlp_back(
        c.line, [x for f in fwd for x in f.mlp_grad], c.down_weight, [f.gate for f in fwd], [f.up for f in fwd]
    )
    for f, f.gate_grad, f.up_grad in zip(fwd, *gates):
        pass
    yield (), ()
    back = hidden_back(c.line, gates[0], c.gate_weight, gates[1], c.up_weight)
    back = yield from scatter_steps(back, c.n_mp, 1, c.far)
    hidden_grad, attn_grad = [], []
    for m, f in enumerate(fwd):
        hidden_grad.append(f.seeds + back[m])
        e, gain_rows = norm_backward(f.attended, f.attn_inv, c.attn_gain, hidden_grad[m])
        f.attn_gain = jnp.sum(gain_rows, axis=0)
        attn_grad.append(e.astype(bf16))
    attn_grad = yield from gather_steps(jnp.stack(attn_grad), c.n_mp, 1, c.far)
    c.attn_grad = [x.reshape(-1, c.width) for x in attn_grad]
    dy = [dot_nt(x, c.o_weight).astype(bf16).reshape(n, -1, c.local) for x in c.attn_grad]
    dy = joined(dy, 1).reshape(n * rows, c.local)
    if not c.rounds:
        c.attn_grad_all = joined(attn_grad, 1).reshape(n * rows, c.width)
    if c.by_heads:
        dys = split_heads(c.z_arr, dy, c.slots)
        dys = yield from exchange_steps(dys, c.n_seq)
        scal = jnp.concatenate([jnp.stack([c.z, c.me]), c.lengths[:, 0]]).astype(jnp.int32)
        grads = attend_back(scal, [f.pieces for f in fwd], [f.kept for f in fwd], dys, c.masks)
        grads = yield from exchange_steps(grads, c.n_seq)
    else:
        grads = [gathered_back(f.kept, dy[m * rows : (m + 1) * rows]) for m, f in enumerate(fwd)]
        grads = [jnp.concatenate(grads, axis=0)]
    tables = (c.cos, c.sin, c.qg, c.kg)
    cross = []
    for m, f in enumerate(fwd):
        e, f.gains = cross_call(c.slots, m, c.z_arr, grads, f.proj, f.inv, *tables)
        cross.append(e.T)
    cross = yield from sum_rows_steps(jnp.concatenate(cross, axis=0), c.n_mp)
    for m, f in enumerate(fwd):
        e = cross[2 * m : 2 * m + 2].T
        f.qkv_grad = raw_call(
            c.slots, c.width, m, c.z_arr, grads, f.proj, f.inv, e, *tables
        )
    yield (), [f.qkv_grad for f in fwd]
    back = jnp.stack([dot_nt(f.qkv_grad, c.qkv_weight).astype(bf16) for f in fwd])
    back = yield from scatter_steps(back, c.n_mp, 1, c.far)
    c.input_grad = jnp.stack(hidden_grad) + back
    return c.input_grad


def turning_task(c):
    yield (), ()
    c.attn_grad_t = []
    for m in range(len(c.fwd)):
        c.attn_grad_t.append(turn(c.line, c.attn_grad, m, len(c.fwd)))
        yield (), ()


def gains_task(c):
    yield (), ()
    gains = sum(f.gains for f in c.fwd)
    gains = lax.dynamic_update_slice(jnp.zeros((2, c.width), f32), gains, (0, c.me * c.local))
    gains = jnp.concatenate(
        [gains, sum(f.attn_gain for f in c.fwd)[None], sum(f.mlp_gain for f in c.fwd)[None]], axis=0
    )
    for name, n in ((MP, c.n_mp), (SEQ, c.n_seq), (DP, c.n_dp)):
        for b in bits_of(n):
            got = lax.ppermute(gains, name, xor_perm(n, b))
            yield (), gains
            if c.rounds:
                yield from idle(2)
            got = yield got, ()
            gains = gains + got
    c.gains = gains
    return gains


def per_device(
    n_dp, n_seq, n_mp,
    tokens, lengths, cotangent, q_weight, k_weight, v_weight, o_weight, q_gain, k_gain,
    attn_gain, gate_weight, up_weight, down_weight, mlp_gain,
):
    c = Layer()
    micros, own_rows, width = tokens.shape
    rows = own_rows * n_mp
    local = q_weight.shape[1]
    heads = local // HEAD_DIM
    ff = gate_weight.shape[1]
    me, z = lax.axis_index(MP), lax.axis_index(SEQ)
    c.tokens, c.lengths, c.cotangent, c.o_weight = tokens, lengths, cotangent, o_weight
    c.gate_weight, c.up_weight, c.down_weight = gate_weight, up_weight, down_weight
    c.attn_gain, c.mlp_gain = attn_gain, mlp_gain
    c.n_dp, c.n_seq, c.n_mp, c.rows, c.width, c.local = n_dp, n_seq, n_mp, rows, width, local
    c.me, c.z, c.masks = me, z, row_masks(n_mp)
    c.by_heads = heads == n_seq
    c.slots = n_seq if c.by_heads else 1
    c.z_arr = z.astype(jnp.int32).reshape(1)
    c.qkv_weight = jnp.concatenate([q_weight, k_weight, v_weight], axis=1)
    c.qg = lax.dynamic_slice_in_dim(q_gain, me * local, local)[None]
    c.kg = lax.dynamic_slice_in_dim(k_gain, me * local, local)[None]
    block = jnp.asarray(c.masks, jnp.int32) ^ me
    steps = jnp.arange(own_rows, dtype=jnp.int32)
    c.pos = z * rows + (block[:, None] * own_rows + steps).reshape(-1)
    c.own_pos = z * rows + me * own_rows + steps
    frequency = rope_base ** (-(jnp.arange(HALF, dtype=f32) * 2.0 / HEAD_DIM))
    angles = c.pos.astype(f32)[:, None] * frequency[None, :]
    cos, sin = jnp.cos(angles), jnp.sin(angles)
    c.cos = jnp.concatenate([cos, cos], axis=1)
    c.sin = jnp.concatenate([-sin, sin], axis=1)
    c.fwd = [Layer() for _ in range(micros)]

    at = Place(n_seq)
    c.rounds = rounds = n_seq == 4
    line = c.line = Line(jnp.zeros((1,), jnp.int32))
    fw = [forward_task(c, m) for m in range(micros)]
    line.add(*fw)
    def turned(m, name):
        f = c.fwd[m]
        rows_ = getattr(f, name)
        setattr(f, name + "_t", turn(line, rows_ if isinstance(rows_, list) else [rows_]))

    extra = {"a": (0, "x"), "b": (1, "x"), "c": (0, "act"), "d": (1, "act"), "e": (0, "mlp_in"), "f": (1, "mlp_in")}
    order = ORDER if (micros, n_mp, c.by_heads) == (2, 4, True) and rounds else ""
    for act in order:
        if act in extra:
            turned(*extra[act])
        else:
            line.step(fw[int(act)])
    while any(t in line.waits for t in fw):
        for t in fw:
            line.step(t)

    c.far = 0
    each = lambda name: [getattr(f, name) for f in c.fwd]
    outs = list(blanks(
        [(ff, width), (width, ff), (width, ff)]
        + [(width, local)] * 3
        + [(width, local) if rounds else (local, width)]
    ))
    back, gains = backward_task(c), gains_task(c)
    side = []
    line.add(back)

    stack = lambda lists: [x for pieces in lists for x in pieces]
    both = lambda name: jnp.concatenate(each(name), axis=0)
    both2 = lambda name: jnp.concatenate(stack(each(name)), axis=0)

    def work(key):
        if rounds:
            return {
                "down": lambda: (each("act_t"), stack(each("mlp_grad"))),
                "gate": lambda: (each("mlp_in_t"), each("gate_grad")),
                "up": lambda: (each("mlp_in_t"), each("up_grad")),
                "o": lambda: (c.attn_grad_t, each("mixed")),
                "qkv": lambda: (each("x_t"), each("qkv_grad")),
            }[key]()
        return {
            "down": lambda: (both("act"), both2("mlp_grad")),
            "gate": lambda: (both2("mlp_in"), both("gate_grad")),
            "up": lambda: (both2("mlp_in"), both("up_grad")),
            "o": lambda: (both("mixed"), c.attn_grad_all),
            "qkv": lambda: (both2("x"), both("qkv_grad")),
        }[key]()

    done, live = {}, []
    if rounds:
        reducer = Rounds(at, outs, line)
        reducer.width = local // 2

    def rows_of(key):
        if key not in done:
            done[key] = work(key)
        return done[key]

    def one_round(new_a, new_b, script=""):
        if rounds:
            for new, table in ((new_a, reducer.a), (new_b, reducer.b)):
                if new is not None:
                    key, which, first, n, col, span = new
                    x, grad = rows_of(key)
                    table[reducer.r] = dict(
                        x=x, grad=grad, cols=(first, n), which=which, col=col, rows=span
                    )
            for act in script:
                if act in "XOM":
                    getattr(reducer, "step_" + act.lower())()
                else:
                    line.step({"c": back, "t": turning, "g": gains}[act])
            reducer.r += 1
            return
        for new, kind in ((new_a, "a"), (new_b, "b")):
            if new is not None:
                key, which, first, n, col, _ = new
                x, grad = rows_of(key)
                if kind == "a":
                    if key + "/" not in done:
                        done[key + "/"] = (take_half(x, at.dp, False), take_half(x, at.dp, True))
                    t = task_a(at, outs, which, *done[key + "/"], grad, slice(first, first + n), col)
                else:
                    t = task_b(at, outs, which, x, grad, slice(first, first + n), col)
                line.add(t)
                live.append(t)
        live[:] = line.step(*live)
        for t in side:
            line.step(t)

    unit = local // 2
    cut = lambda key, which, n, u=unit, first=0, parts=1: [
        (key, which, first + t, u, t, (k * (width // parts), width // parts))
        for t in range(0, n, u)
        for k in range(parts)
    ]
    ready = {
        "down": lambda: True,
        "gate": lambda: all(hasattr(f, "up_grad") for f in c.fwd),
        "o": lambda: len(c.attn_grad_t) == micros if rounds else hasattr(c, "attn_grad_all"),
        "qkv": lambda: all(hasattr(f, "qkv_grad") for f in c.fwd),
    }
    ready["up"] = ready["gate"]
    todo = cut("down", 0, width) + cut("gate", 1, ff) + cut("up", 2, ff)
    todo += cut("o", 6, local) if rounds else cut("o", 6, width, width // 2)
    for t in range(3):
        todo += cut("qkv", 3 + t, local, first=t * local, parts=2 if rounds and t else 1)
    c.attn_grad_t = []
    if rounds:
        for m in range(micros):
            for name in ("x", "act", "mlp_in"):
                if not hasattr(c.fwd[m], name + "_t"):
                    turned(m, name)
        turning = turning_task(c)
        line.add(turning)
    else:
        side = [back]
    count_a = len(todo) // 2

    def take():
        for i, chunk in enumerate(todo):
            if ready[chunk[0]]():
                return todo.pop(i)
        return None

    gains_on = False
    r = taken_a = 0
    while todo or any(t in line.waits for t in (back, gains)) or (
        reducer.a or reducer.b if rounds else live
    ):
        late = ready["qkv"]()
        if late and not gains_on:
            gains_on = True
            side.append(gains)
            line.add(gains)
        new_a = take() if taken_a < count_a else None
        taken_a += new_a is not None
        script = SCRIPT[r] if r < len(SCRIPT) else "XgOcMg"
        lone = rounds and r < len(SCRIPT) and script[-1:] == "-"
        new_b = None if lone else take()
        one_round(new_a, new_b, script.strip("-") if rounds else "")
        r += 1
    return (
        jnp.stack(each("layer")),
        c.input_grad,
        outs[3],
        outs[4],
        outs[5],
        outs[6].T if rounds else outs[6],
        c.gains[0],
        c.gains[1],
        c.gains[2],
        outs[1],
        outs[2],
        outs[0],
        c.gains[3],
    )


SCRIPT = (
    "XOc",
    "XcOM",
    "XcOM",
    "XcOM",
    "XOcM",
    "XOcM",
    "XOMc",
    "XOtMtc",
    "XOcM",
    "XcOMc",
    "XOMc",
)

ORDER = "00001111ab00010101010ce1101d0f1011"


def solution(mesh):
    n_dp, n_seq, n_mp = (mesh.shape[a] for a in (DP, SEQ, MP))
    assert n_dp == 2
    rows = P(None, (DP, SEQ, MP), None)
    cols, flat, all_ = P(None, MP), P(MP, None), P()
    return jax.shard_map(
        functools.partial(per_device, n_dp, n_seq, n_mp),
        mesh=mesh,
        in_specs=(rows, P(None, DP), rows, cols, cols, cols, flat, all_, all_, all_, cols, cols, flat, all_),
        out_specs=(rows, rows, cols, cols, cols, flat, all_, all_, all_, cols, cols, flat, all_),
        check_vma=False,
    )
```

```python
import functools

import jax
import jax.numpy as jnp
from jax import lax
from jax.experimental import pallas as pl
from jax.experimental.pallas import tpu as pltpu
from jax.sharding import PartitionSpec as P

HEAD_DIM = 128
HALF = HEAD_DIM // 2
DP, SEQ, MP = "dp", "seq", "mp"
TO_KEYS, TO_ROWS, TO_HEADS = "shd,khd->shk", "shk,khd->shd", "shk,shd->khd"
epsilon = 1e-06
rope_base = 500000.0
masked_score = -1e30
LOG2E = 1.4426950408889634

BRIEF = pl.CostEstimate(flops=1000, bytes_accessed=1000, transcendentals=0)

f32 = jnp.float32
bf16 = jnp.bfloat16


def add_low(a, b):
    return (a.astype(f32) + b.astype(f32)).astype(bf16)


def bits_of(n):
    out = []
    b = 1
    while b < n:
        out.append(b)
        b *= 2
    return out


def xor_perm(n, b):
    return [(i, i ^ b) for i in range(n)]


def row_masks(n):
    masks = [0]
    for b in reversed(bits_of(n)):
        masks = masks + [m | b for m in masks]
    return masks


def inv_rms(v):
    return lax.rsqrt(jnp.mean(v * v, axis=-1, keepdims=True) + epsilon)


def norm_backward(source, inverse, gain_vec, upstream):
    normed = source * inverse
    weighted = upstream * gain_vec
    back = inverse * (weighted - normed * jnp.mean(weighted * normed, axis=-1, keepdims=True))
    return back, upstream * normed


def dot_t(a, b):
    return lax.dot_general(a, b, (((0,), (0,)), ((), ())), preferred_element_type=f32)


def dot_nt(a, b):
    return lax.dot_general(a, b, (((1,), (1,)), ((), ())), preferred_element_type=f32)


def dot(a, b):
    return jnp.dot(a, b, preferred_element_type=f32)


def rope_kernel(slots, width, local, z_ref, proj, inv, cos, sin, qg, kg, *outs):
    z = z_ref[0]
    c, s = cos[...], sin[...]
    for j in range(slots):
        base = (z ^ j) * width if slots > 1 else 0
        for h in range(width // HEAD_DIM):
            at = base + h * HEAD_DIM
            at = pl.multiple_of(at, HEAD_DIM) if slots > 1 else at
            for part, gain in ((0, qg), (1, kg)):
                raw = proj[:, pl.ds(part * local + at, HEAD_DIM)]
                v = raw * inv[:, part : part + 1] * gain[:, pl.ds(at, HEAD_DIM)]
                v = v * c + pltpu.roll(v, HALF, 1) * s
                lo = part * width + h * HEAD_DIM
                outs[j][:, lo : lo + HEAD_DIM] = v.astype(bf16)
            lo = 2 * width + h * HEAD_DIM
            outs[j][:, lo : lo + HEAD_DIM] = proj[:, pl.ds(2 * local + at, HEAD_DIM)].astype(bf16)


def rope_call(slots, z, proj, inv, cos, sin, qg, kg):
    rows, local = proj.shape[0], proj.shape[1] // 3
    width = local // slots
    blk = min(rows, 256)
    row = lambda n: pl.BlockSpec((blk, n), lambda i, *_: (i, 0))
    vec = pl.BlockSpec((1, local), lambda i, *_: (0, 0))
    return pl.pallas_call(
        functools.partial(rope_kernel, slots, width, local),
        out_shape=[jax.ShapeDtypeStruct((rows, 3 * width), bf16)] * slots,
        grid_spec=pltpu.PrefetchScalarGridSpec(
            num_scalar_prefetch=1,
            grid=(rows // blk,),
            in_specs=[row(3 * local), row(2), row(HEAD_DIM), row(HEAD_DIM), vec, vec],
            out_specs=[row(3 * width)] * slots,
        ),
        cost_estimate=BRIEF,
    )(z, proj, inv, cos, sin, qg, kg)


def unrope(grad, c, s):
    g = grad.astype(f32)
    return g * c - pltpu.roll(g, HALF, 1) * s


def cross_kernel(slots, width, local, z_ref, *refs):
    grads = refs[:slots]
    proj, inv, cos, sin, qg, kg, cross, gains = refs[slots:]
    z = z_ref[0]
    c, s = cos[...], sin[...]

    @pl.when(pl.program_id(0) == 0)
    def _():
        gains[...] = jnp.zeros_like(gains)

    for part, gain in ((0, qg), (1, kg)):
        total = None
        for j in range(slots):
            base = (z ^ j) * width if slots > 1 else 0
            for h in range(width // HEAD_DIM):
                at = base + h * HEAD_DIM
                at = pl.multiple_of(at, HEAD_DIM) if slots > 1 else at
                lo = part * width + h * HEAD_DIM
                g = unrope(grads[j][:, lo : lo + HEAD_DIM], c, s)
                gr = g * proj[:, pl.ds(part * local + at, HEAD_DIM)]
                w = gr * gain[:, pl.ds(at, HEAD_DIM)]
                total = w if total is None else total + w
                col = jnp.sum(gr * inv[:, part : part + 1], axis=0, keepdims=True)
                gains[part : part + 1, pl.ds(at, HEAD_DIM)] += col
        cross[:, part : part + 1] = jnp.sum(total, axis=1, keepdims=True)


def raw_kernel(slots, width, local, d, z_ref, *refs):
    grads = refs[:slots]
    proj, inv, cross, cos, sin, qg, kg, out = refs[slots:]
    z = z_ref[0]
    c, s = cos[...], sin[...]
    for j in range(slots):
        base = (z ^ j) * width if slots > 1 else 0
        for h in range(width // HEAD_DIM):
            at = base + h * HEAD_DIM
            at = pl.multiple_of(at, HEAD_DIM) if slots > 1 else at
            for part, gain in ((0, qg), (1, kg)):
                lo = part * width + h * HEAD_DIM
                g = unrope(grads[j][:, lo : lo + HEAD_DIM], c, s)
                r = inv[:, part : part + 1]
                w = g * gain[:, pl.ds(at, HEAD_DIM)] * r
                k = r * r * r * (cross[:, part : part + 1] * (1.0 / d))
                w = w - proj[:, pl.ds(part * local + at, HEAD_DIM)] * k
                out[:, pl.ds(part * local + at, HEAD_DIM)] = w.astype(bf16)
            lo = 2 * width + h * HEAD_DIM
            out[:, pl.ds(2 * local + at, HEAD_DIM)] = grads[j][:, lo : lo + HEAD_DIM]


def cross_call(slots, m, z, grads, proj, inv, cos, sin, qg, kg):
    rows, local = proj.shape[0], proj.shape[1] // 3
    width = local // slots
    blk = min(rows, 256)
    far = lambda n: pl.BlockSpec((blk, n), lambda i, *_: (i + m * (rows // blk), 0))
    row = lambda n: pl.BlockSpec((blk, n), lambda i, *_: (i, 0))
    vec = pl.BlockSpec((1, local), lambda i, *_: (0, 0))
    return pl.pallas_call(
        functools.partial(cross_kernel, slots, width, local),
        out_shape=[
            jax.ShapeDtypeStruct((rows, 2), f32),
            jax.ShapeDtypeStruct((2, local), f32),
        ],
        grid_spec=pltpu.PrefetchScalarGridSpec(
            num_scalar_prefetch=1,
            grid=(rows // blk,),
            in_specs=[far(3 * width)] * slots
            + [row(3 * local), row(2), row(HEAD_DIM), row(HEAD_DIM), vec, vec],
            out_specs=[row(2), pl.BlockSpec((2, local), lambda i, *_: (0, 0))],
        ),
        cost_estimate=BRIEF,
    )(z, *grads, proj, inv, cos, sin, qg, kg)


def raw_call(slots, d, m, z, grads, proj, inv, cross, cos, sin, qg, kg):
    rows, local = proj.shape[0], proj.shape[1] // 3
    width = local // slots
    blk = min(rows, 256)
    far = lambda n: pl.BlockSpec((blk, n), lambda i, *_: (i + m * (rows // blk), 0))
    row = lambda n: pl.BlockSpec((blk, n), lambda i, *_: (i, 0))
    vec = pl.BlockSpec((1, local), lambda i, *_: (0, 0))
    return pl.pallas_call(
        functools.partial(raw_kernel, slots, width, local, d),
        out_shape=jax.ShapeDtypeStruct((rows, 3 * local), bf16),
        grid_spec=pltpu.PrefetchScalarGridSpec(
            num_scalar_prefetch=1,
            grid=(rows // blk,),
            in_specs=[far(3 * width)] * slots
            + [row(3 * local), row(2), row(2), row(HEAD_DIM), row(HEAD_DIM), vec, vec],
            out_specs=row(3 * local),
        ),
        cost_estimate=BRIEF,
    )(z, *grads, proj, inv, cross, cos, sin, qg, kg)


def join_kernel(slots, width, z_ref, *refs):
    z = z_ref[0]
    out = refs[slots]
    for j in range(slots):
        out[:, pl.ds(pl.multiple_of((z ^ j) * width, HEAD_DIM), width)] = refs[j][...]


def join_heads(z, pieces):
    rows, width = pieces[0].shape
    slots = len(pieces)
    blk = min(rows, 256)
    return pl.pallas_call(
        functools.partial(join_kernel, slots, width),
        out_shape=jax.ShapeDtypeStruct((rows, slots * width), bf16),
        grid_spec=pltpu.PrefetchScalarGridSpec(
            num_scalar_prefetch=1,
            grid=(rows // blk,),
            in_specs=[pl.BlockSpec((blk, width), lambda i, *_: (i, 0))] * slots,
            out_specs=pl.BlockSpec((blk, slots * width), lambda i, *_: (i, 0)),
        ),
    )(z, *pieces)


def split_kernel(slots, width, z_ref, x, *outs):
    z = z_ref[0]
    for j in range(slots):
        outs[j][...] = x[:, pl.ds(pl.multiple_of((z ^ j) * width, HEAD_DIM), width)]


def split_heads(z, x, slots):
    rows, local = x.shape
    width = local // slots
    blk = min(rows, 256)
    return pl.pallas_call(
        functools.partial(split_kernel, slots, width),
        out_shape=[jax.ShapeDtypeStruct((rows, width), bf16)] * slots,
        grid_spec=pltpu.PrefetchScalarGridSpec(
            num_scalar_prefetch=1,
            grid=(rows // blk,),
            in_specs=[pl.BlockSpec((blk, local), lambda i, *_: (i, 0))],
            out_specs=[pl.BlockSpec((blk, width), lambda i, *_: (i, 0))] * slots,
        ),
    )(z, x)


def row_places(slots, masks, rows, z, me):
    count = rows // len(masks)
    for j in range(slots):
        for k, m in enumerate(masks):
            yield j, k * count, pl.multiple_of((z ^ j) * rows + (me ^ m) * count, count), count


def key_bias(total, length):
    pos = lax.broadcasted_iota(jnp.int32, (1, total), 1)
    return jnp.where(pos < length, 0.0, masked_score).astype(f32)


def diag_mask(size):
    r = lax.broadcasted_iota(jnp.int32, (size, size), 0)
    c = lax.broadcasted_iota(jnp.int32, (size, size), 1)
    return c <= r


def attend_kernel(slots, masks, rows, blk, scal, *refs):
    pieces, outs = refs[:slots], refs[slots : 2 * slots]
    o32, lse, qkv, o16, sem = refs[2 * slots :]
    z, me, length = scal[0], scal[1], scal[2]
    total = slots * rows
    copies = []
    for t, (j, at, to, n) in enumerate(row_places(slots, masks, rows, z, me)):
        cp = pltpu.make_async_copy(pieces[j].at[pl.ds(at, n)], qkv.at[pl.ds(to, n)], sem.at[t])
        cp.start()
        copies.append(cp)
    bias = key_bias(total, length)
    causal = diag_mask(blk)
    for cp in copies:
        cp.wait()
    factor = HEAD_DIM**-0.5 * LOG2E
    for i in range(total // blk):
        lo = i * blk
        q = qkv[lo : lo + blk, :HEAD_DIM]
        s = dot_nt(q, qkv[lo : lo + blk, HEAD_DIM : 2 * HEAD_DIM]) * factor
        s = jnp.where(causal, s + bias[:, lo : lo + blk], masked_score)
        top = jnp.max(s, axis=1, keepdims=True)
        if i:
            before = dot_nt(q, qkv[:lo, HEAD_DIM : 2 * HEAD_DIM]) * factor + bias[:, :lo]
            top = jnp.maximum(top, jnp.max(before, axis=1, keepdims=True))
        p = jnp.exp2(s - top)
        mass = jnp.sum(p, axis=1, keepdims=True)
        acc = dot(p.astype(bf16), qkv[lo : lo + blk, 2 * HEAD_DIM :])
        if i:
            p = jnp.exp2(before - top)
            mass = mass + jnp.sum(p, axis=1, keepdims=True)
            acc = acc + dot(p.astype(bf16), qkv[:lo, 2 * HEAD_DIM :])
        acc = acc / mass
        o32[lo : lo + blk, :] = acc
        o16[lo : lo + blk, :] = acc.astype(bf16)
        lse[lo : lo + blk, :] = top + jnp.log(mass) * LOG2E
    copies = []
    for t, (j, at, to, n) in enumerate(row_places(slots, masks, rows, z, me)):
        cp = pltpu.make_async_copy(o16.at[pl.ds(to, n)], outs[j].at[pl.ds(at, n)], sem.at[t])
        cp.start()
        copies.append(cp)
    for cp in copies:
        cp.wait()


def attend(scal, pieces, masks):
    slots = len(pieces)
    rows = pieces[0].shape[0]
    total = slots * rows
    hbm = pl.BlockSpec(memory_space=pl.ANY)
    vmem = pl.BlockSpec(memory_space=pltpu.VMEM)
    out = pl.pallas_call(
        functools.partial(attend_kernel, slots, masks, rows, 256),
        out_shape=[jax.ShapeDtypeStruct((rows, HEAD_DIM), bf16)] * slots
        + [
            jax.ShapeDtypeStruct((total, HEAD_DIM), f32),
            jax.ShapeDtypeStruct((total, 1), f32),
        ],
        in_specs=[pl.BlockSpec(memory_space=pltpu.SMEM)] + [hbm] * slots,
        out_specs=[hbm] * slots + [vmem, vmem],
        scratch_shapes=[
            pltpu.VMEM((total, 3 * HEAD_DIM), bf16),
            pltpu.VMEM((total, HEAD_DIM), bf16),
            pltpu.SemaphoreType.DMA((slots * len(masks),)),
        ],
        cost_estimate=BRIEF,
        name="attend",
    )(scal, *pieces)
    return out[:slots], (out[slots], out[slots + 1])


def attend_back_kernel(slots, masks, rows, blk, micros, scal, *refs):
    pieces = [refs[m * slots : (m + 1) * slots] for m in range(micros)]
    refs = refs[micros * slots :]
    kept = [refs[2 * m : 2 * m + 2] for m in range(micros)]
    dos, outs = refs[2 * micros : 2 * micros + slots], refs[2 * micros + slots :][:slots]
    qkv, do, o32, lse, dkv, grad, sem = refs[2 * micros + 2 * slots :]
    micro = pl.program_id(0)
    z, me, length = scal[0], scal[1], scal[2 + micro]
    total = slots * rows
    runs = slots * len(masks)
    places = list(row_places(slots, masks, rows, z, me))
    base = micro * rows

    def incoming(m):
        out = []
        for t, (j, at, to, n) in enumerate(places):
            from_, to_ = pl.ds(at, n), pl.ds(to, n)
            out.append(pltpu.make_async_copy(pieces[m][j].at[from_], qkv.at[to_], sem.at[t]))
            far = pl.ds(pl.multiple_of(base + at, n), n)
            out.append(pltpu.make_async_copy(dos[j].at[far], do.at[to_], sem.at[runs + t]))
        out.append(pltpu.make_async_copy(kept[m][0], o32, sem.at[2 * runs]))
        out.append(pltpu.make_async_copy(kept[m][1], lse, sem.at[2 * runs + 1]))
        return out

    for m in range(micros):

        @pl.when(micro == m)
        def _(m=m):
            copies = incoming(m)
            for cp in copies:
                cp.start()
            for cp in copies:
                cp.wait()

    bias = key_bias(total, length)
    causal = diag_mask(blk)
    dkv[...] = jnp.zeros_like(dkv)
    scale = HEAD_DIM**-0.5
    factor = scale * LOG2E
    D = HEAD_DIM
    for i in range(total // blk):
        lo = i * blk
        q, dy = qkv[lo : lo + blk, :D], do[lo : lo + blk, :]
        delta = jnp.sum(dy.astype(f32) * o32[lo : lo + blk, :], axis=1, keepdims=True)
        level = lse[lo : lo + blk, :]
        dq = None
        for start, stop in ((lo, lo + blk), (0, lo)):
            if start == stop:
                continue
            keys, vals = qkv[start:stop, D : 2 * D], qkv[start:stop, 2 * D :]
            s = dot_nt(q, keys) * factor + bias[:, start:stop]
            if start == lo:
                s = jnp.where(causal, s, masked_score)
            p = jnp.exp2(s - level)
            ds = (p * (dot_nt(dy, vals) - delta)).astype(bf16)
            part = dot(ds, keys)
            dq = part if dq is None else dq + part
            dkv[start:stop, :D] += dot_t(ds, q)
            dkv[start:stop, D:] += dot_t(p.astype(bf16), dy)
        grad[lo : lo + blk, :D] = (dq * scale).astype(bf16)
    grad[:, D : 2 * D] = (dkv[:, :D] * scale).astype(bf16)
    grad[:, 2 * D :] = dkv[:, D:].astype(bf16)
    copies = []
    for t, (j, at, to, n) in enumerate(places):
        far = pl.ds(pl.multiple_of(base + at, n), n)
        cp = pltpu.make_async_copy(grad.at[pl.ds(to, n)], outs[j].at[far], sem.at[t])
        cp.start()
        copies.append(cp)
    for cp in copies:
        cp.wait()


def attend_back(scal, pieces, kept, dos, masks):
    micros, slots = len(pieces), len(dos)
    rows = dos[0].shape[0] // micros
    total = slots * rows
    hbm = pl.BlockSpec(memory_space=pl.ANY)
    return pl.pallas_call(
        functools.partial(attend_back_kernel, slots, masks, rows, 256, micros),
        out_shape=[jax.ShapeDtypeStruct((micros * rows, 3 * HEAD_DIM), bf16)] * slots,
        grid=(micros,),
        in_specs=[pl.BlockSpec(memory_space=pltpu.SMEM)] + [hbm] * ((micros + 1) * slots + 2 * micros),
        out_specs=[hbm] * slots,
        scratch_shapes=[
            pltpu.VMEM((total, 3 * HEAD_DIM), bf16),
            pltpu.VMEM((total, HEAD_DIM), bf16),
            pltpu.VMEM((total, HEAD_DIM), f32),
            pltpu.VMEM((total, 1), f32),
            pltpu.VMEM((total, 2 * HEAD_DIM), f32),
            pltpu.VMEM((total, 3 * HEAD_DIM), bf16),
            pltpu.SemaphoreType.DMA((2 * slots * len(masks) + 2,)),
        ],
        cost_estimate=BRIEF,
        name="attend_back",
    )(scal, *[p for ps in pieces for p in ps], *[k for ks in kept for k in ks], *dos)


def mlp_back_kernel(n, *refs):
    grads, dw, gates, ups = refs[: 2 * n], refs[2 * n], refs[2 * n + 1 :][:n], refs[3 * n + 1 :][:n]
    tok, outs, tok_out = refs[4 * n + 1], refs[4 * n + 2 : 6 * n + 2], refs[6 * n + 2]
    w = dw[...]
    half = grads[0].shape[0]
    for i, x in enumerate(grads):
        m, t = i // 2, slice(i % 2 * half, (i % 2 + 1) * half)
        a = dot_nt(x[...], w)
        g, u = gates[m][t, :], ups[m][t, :]
        s = jax.nn.sigmoid(g)
        outs[m][t, :] = (a * u * s * (1.0 + g * (1.0 - s))).astype(bf16)
        outs[n + m][t, :] = (a * g * s).astype(bf16)
    tok_out[0] = tok[0]


def mlp_back(line, grads, down_weight, gates, ups):
    n = len(gates)
    half, width = grads[0].shape
    rows = 2 * half
    ff = down_weight.shape[0]
    t = min(ff, 256)
    tall = pl.BlockSpec((rows, t), lambda i: (0, i))
    smem = pl.BlockSpec(memory_space=pltpu.SMEM)
    full = jax.ShapeDtypeStruct((rows, ff), bf16)
    *out, line.token = pl.pallas_call(
        functools.partial(mlp_back_kernel, n),
        out_shape=[full] * (2 * n) + [jax.ShapeDtypeStruct((1,), jnp.int32)],
        grid=(ff // t,),
        in_specs=[pl.BlockSpec((half, width), lambda i: (0, 0))] * (2 * n)
        + [pl.BlockSpec((t, width), lambda i: (i, 0))]
        + [tall] * (2 * n)
        + [smem],
        out_specs=[tall] * (2 * n) + [smem],
        cost_estimate=BRIEF,
        name="mlp_back",
    )(*grads, down_weight, *gates, *ups, line.token)
    return out[:n], out[n:]


def hidden_back_kernel(n, *refs):
    gate_grads, gw, up_grads, uw = refs[:n], refs[n], refs[n + 1 : 2 * n + 1], refs[2 * n + 1]
    tok, keep, send, tok_out = refs[2 * n + 2 :]
    g, u = gw[...], uw[...]
    half = keep.shape[1]
    for m in range(n):
        v = (dot_nt(gate_grads[m][...], g) + dot_nt(up_grads[m][...], u)).astype(bf16)
        keep[m] = v[:half, :]
        send[m] = v[half:, :]
    tok_out[0] = tok[0]


def hidden_back(line, gate_grads, gate_weight, up_grads, up_weight):
    n = len(gate_grads)
    rows, ff = gate_grads[0].shape
    width = gate_weight.shape[0]
    t = min(width, 256)
    all_ = pl.BlockSpec((rows, ff), lambda i: (0, 0), pipeline_mode=pl.Buffered(1))
    tile = pl.BlockSpec((t, ff), lambda i: (i, 0))
    smem = pl.BlockSpec(memory_space=pltpu.SMEM)
    half = jax.ShapeDtypeStruct((n, rows // 2, width), bf16)
    part = pl.BlockSpec((n, rows // 2, t), lambda i: (0, 0, i))
    keep, send, line.token = pl.pallas_call(
        functools.partial(hidden_back_kernel, n),
        out_shape=[half, half, jax.ShapeDtypeStruct((1,), jnp.int32)],
        grid=(width // t,),
        in_specs=[all_] * n + [tile] + [all_] * n + [tile, smem],
        out_specs=[part, part, smem],
        cost_estimate=BRIEF,
        name="hidden_back",
    )(*gate_grads, gate_weight, *up_grads, up_weight, line.token)
    return keep, send


def turn_kernel(n, *refs):
    out, tok_out = refs[n + 1 :]
    at = 0
    for x in refs[:n]:
        out[:, at : at + x.shape[0]] = x[...].T
        at += x.shape[0]
    tok_out[0] = refs[n][0]


def turn(line, pieces, m=0, count=1):
    counts = [x.shape[0] // count for x in pieces]
    rows, cols = sum(counts), pieces[0].shape[1]
    t = min(cols, 512)
    smem = pl.BlockSpec(memory_space=pltpu.SMEM)
    out, line.token = pl.pallas_call(
        functools.partial(turn_kernel, len(pieces)),
        out_shape=[
            jax.ShapeDtypeStruct((cols, rows), pieces[0].dtype),
            jax.ShapeDtypeStruct((1,), jnp.int32),
        ],
        grid=(cols // t,),
        in_specs=[pl.BlockSpec((n, t), lambda i: (m, i)) for n in counts] + [smem],
        out_specs=[pl.BlockSpec((t, rows), lambda i: (i, 0)), smem],
        cost_estimate=BRIEF,
        name="turn",
    )(*pieces, line.token)
    return out


def gathered_attend(piece, pos, length):
    rows, local = piece.shape[0], piece.shape[1] // 3
    heads = local // HEAD_DIM
    q = piece[:, :local].reshape(rows, heads, HEAD_DIM)
    kv = lax.all_gather(piece[:, local:], SEQ, axis=0, tiled=True)
    n = kv.shape[0]
    k = kv[:, :local].reshape(n, heads, HEAD_DIM)
    v = kv[:, local:].reshape(n, heads, HEAD_DIM)
    base = jnp.arange(n // rows, dtype=jnp.int32) * rows
    own = pos - lax.axis_index(SEQ) * rows
    key_pos = (base[:, None] + own[None, :]).reshape(n)
    allowed = (key_pos[None, :] <= pos[:, None]) & (key_pos[None, :] < length)
    allowed = allowed[:, None, :]
    s = jnp.einsum(TO_KEYS, q, k, preferred_element_type=f32) * HEAD_DIM**-0.5
    s = jnp.where(allowed, s, masked_score)
    top = jnp.max(s, axis=-1, keepdims=True)
    w = jnp.where(allowed, jnp.exp(s - top), 0.0)
    mass = jnp.sum(w, axis=-1, keepdims=True)
    mixed = jnp.einsum(TO_ROWS, w.astype(bf16), v, preferred_element_type=f32) / mass
    return mixed.reshape(rows, local).astype(bf16), (q, k, v, allowed, mixed, top + jnp.log(mass))


def gathered_back(kept, dy):
    q, k, v, allowed, mixed, level = kept
    rows, heads, _ = q.shape
    n = k.shape[0]
    dy = dy.reshape(rows, heads, HEAD_DIM)
    scale = HEAD_DIM**-0.5
    delta = jnp.sum(dy.astype(f32) * mixed, axis=-1, keepdims=True)
    s = jnp.einsum(TO_KEYS, q, k, preferred_element_type=f32) * scale
    p = jnp.where(allowed, jnp.exp(s - level), 0.0)
    dp = jnp.einsum(TO_KEYS, dy, v, preferred_element_type=f32)
    ds = (p * (dp - delta)).astype(bf16)
    dq = jnp.einsum(TO_ROWS, ds, k, preferred_element_type=f32) * scale
    dk = jnp.einsum(TO_HEADS, ds, q, preferred_element_type=f32) * scale
    dv = jnp.einsum(TO_HEADS, p.astype(bf16), dy, preferred_element_type=f32)
    local = heads * HEAD_DIM
    dkv = jnp.concatenate([dk.reshape(n, local), dv.reshape(n, local)], axis=1).astype(bf16)
    dkv = lax.psum_scatter(dkv, SEQ, scatter_dimension=0, tiled=True)
    return jnp.concatenate([dq.reshape(rows, local).astype(bf16), dkv.astype(bf16)], axis=1)


class Line:
    def __init__(self, token):
        self.token = token
        self.waits = {}

    def add(self, *tasks):
        for t in tasks:
            self.waits[t] = next(t)[0]

    def mark(self, *arrays):
        for x in arrays:
            x = lax.slice(x, (0,) * x.ndim, (1,) * x.ndim).reshape(1)
            self.token = self.token + (x.astype(f32) > 3.4e38).astype(jnp.int32)

    def step(self, *tasks):
        tasks = [t for t in tasks if t in self.waits]
        if not tasks:
            return []
        held = [self.waits.pop(t) for t in tasks]
        if jax.tree.leaves(held):
            held, self.token = lax.optimization_barrier((held, self.token))
        for t, v in zip(tasks, held):
            try:
                self.waits[t], out = t.send(v)
            except StopIteration as end:
                out = end.value
            self.mark(*jax.tree.leaves(out)[:1])
        return [t for t in tasks if t in self.waits]


def idle(n):
    for _ in range(n):
        yield (), ()


class Place:
    def __init__(self, n_seq):
        self.n = n_seq
        self.dp, self.z = lax.axis_index(DP), lax.axis_index(SEQ)
        self.swap = [(0, 1), (1, 0)]
        self.lo, self.hi = n_seq // 2 - 1, n_seq // 2
        self.mid = [(self.lo, self.hi), (self.hi, self.lo)]
        self.inward = [
            [(i, i + 1), (n_seq - 1 - i, n_seq - 2 - i)] for i in range(n_seq // 2 - 1)
        ]

    def ends(self, pairs):
        return functools.reduce(jnp.logical_or, [self.z == b for _, b in pairs])


def take_half(x, dp, own):
    half = x.shape[1] // 2
    return lax.dynamic_slice_in_dim(x, (dp if own else 1 - dp) * half, half, 1)


def task_a(at, outs, which, x_send, x_keep, grad, cols, out_col):
    half = x_keep.shape[1]
    g = (yield grad, ())[:, cols]
    send = dot_t(x_send, g).astype(bf16)
    got = yield lax.ppermute(send, DP, at.swap), send
    s = (dot_t(x_keep, g) + got.astype(f32)).astype(bf16)
    for pairs in at.inward:
        got = yield lax.ppermute(s, SEQ, pairs), s
        s = add_low(s, got)
    got = yield lax.ppermute(s, SEQ, at.mid), s
    s = add_low(s, got)
    for pairs in reversed(at.inward):
        pairs = [(b, a) for a, b in pairs]
        got = yield lax.ppermute(s, SEQ, pairs), s
        s = jnp.where(at.ends(pairs), got, s)
    outs[which] = lax.dynamic_update_slice(outs[which], s.astype(f32), (at.dp * half, out_col))
    got = yield lax.ppermute(s, DP, at.swap), s
    outs[which] = lax.dynamic_update_slice(
        outs[which], got.astype(f32), ((1 - at.dp) * half, out_col)
    )
    return ()


def task_b(at, outs, which, x, grad, cols, out_col):
    g = (yield grad, ())[:, cols]
    s = dot_t(x, g).astype(bf16)
    for pairs in at.inward:
        got = yield lax.ppermute(s, SEQ, pairs), s
        s = add_low(s, got)
    h = s.shape[1] // 2
    first = at.z == at.lo
    send = jnp.where(first, s[:, h:], s[:, :h])
    keep = jnp.where(first, s[:, :h], s[:, h:])
    got = yield lax.ppermute(send, SEQ, at.mid), (send, keep)
    keep = add_low(keep, got)
    n = at.n
    pairs = [(d * n + k, (1 - d) * n + k) for d in (0, 1) for k in (at.lo, at.hi)]
    got = yield lax.ppermute(keep, (DP, SEQ), pairs), keep
    keep = add_low(keep, got)
    got = yield lax.ppermute(keep, SEQ, at.mid), keep
    s = jnp.concatenate([jnp.where(first, keep, got), jnp.where(first, got, keep)], axis=1)
    for pairs in reversed(at.inward):
        pairs = [(b, a) for a, b in pairs]
        got = yield lax.ppermute(s, SEQ, pairs), s
        s = jnp.where(at.ends(pairs), got, s)
    outs[which] = lax.dynamic_update_slice(outs[which], s.astype(f32), (0, out_col))
    return None


class Round:
    def __init__(self):
        self.refs, self.loads, self.keys = [], {}, {}

    def ref(self, array):
        for i, r in enumerate(self.refs):
            if r is array:
                return i
        self.refs.append(array)
        return len(self.refs) - 1

    def load(self, name, array, rows, cols=None):
        cols = (0, array.shape[1]) if cols is None else cols
        self.loads[name] = ((rows[1], cols[1]), ((self.ref(array), rows, cols, 0, 0),))

    def load_down(self, name, arrays, cols):
        n = arrays[0].shape[0]
        parts = tuple((self.ref(x), (0, n), cols, i * n, 0) for i, x in enumerate(arrays))
        self.loads[name] = ((n * len(arrays), cols[1]), parts)

    def load_across(self, name, arrays, rows):
        n = arrays[0].shape[1]
        parts = tuple((self.ref(x), rows, (0, n), 0, i * n) for i, x in enumerate(arrays))
        self.loads[name] = ((rows[1], n * len(arrays)), parts)


def first_row(first, count, dp):
    if isinstance(first, int):
        return first
    own, base = first
    return pl.multiple_of(base + (dp if own else 1 - dp) * count, count)


def round_kernel(kind, loads, n_in, pieces, extras, stores, scal, tok, *refs):
    ins = refs[:n_in]
    outs = refs[n_in + 1 : n_in + 1 + bool(pieces) + bool(extras) + len(stores)]
    refs[n_in][0] = tok[0]
    scratch = refs[n_in + 1 + len(outs) :]
    bufs = dict(zip([l[0] for l in loads], scratch))
    rest = list(scratch[len(loads) :])
    out_bufs = {}
    for name, _ in pieces + extras:
        out_bufs[name] = rest.pop(0)
    f_bufs = [rest.pop(0) for _ in stores]
    in_sem, out_sem = rest
    dp, z, n = scal[0], scal[1], scal[2]
    outer = (z == 0) | (z == n - 1)
    first = z == n // 2 - 1
    waits = {}
    t = 0
    for name, _, parts in loads:
        waits[name] = []
        for i, (r0, rows), (c0, cols), to_row, to_col in parts:
            src = ins[i].at[pl.ds(first_row(r0, rows, dp), rows), pl.ds(c0, cols)]
            dst = bufs[name].at[pl.ds(to_row, rows), pl.ds(to_col, cols)]
            cp = pltpu.make_async_copy(src, dst, in_sem.at[t])
            cp.start()
            waits[name].append(cp)
            t += 1

    def get(name):
        for cp in waits.pop(name, ()):
            cp.wait()
        return bufs[name]

    done = []
    slot = [0]

    def ship(src, dst):
        cp = pltpu.make_async_copy(src, dst, out_sem.at[slot[0]])
        slot[0] += 1
        cp.start()
        done.append(cp)

    where_out = {}
    k = 0
    for group in (pieces, extras):
        if group:
            at = 0
            for name, rows in group:
                where_out[name] = outs[k].at[pl.ds(at, rows)]
                at += rows
            k += 1

    def emit(name):
        if name in where_out:
            ship(out_bufs[name], where_out[name])

    def tiles(rows):
        t = min(rows, 256)
        return [slice(i, i + t) for i in range(0, rows, t)]

    have = lambda *names: all(n in bufs for n in names)
    low = lambda a, b: (a.astype(f32) + b.astype(f32)).astype(bf16)
    finals = {}
    if kind == "X":
        if have("a4r"):
            got, own, out = get("a4r"), get("a4o"), out_bufs["a4"]
            for t in tiles(out.shape[0]):
                out[t, :] = jnp.where(outer, got[t, :], own[t, :])
            emit("a4")
            finals["a4"] = out
        if have("b2r"):
            got, own, out = get("b2r"), get("b2o"), out_bufs["b2"]
            for t in tiles(out.shape[0]):
                out[t, :] = low(own[t, :], got[t, :])
            emit("b2")
        if have("a0g"):
            g, x, out = get("a0g"), get("a0x"), out_bufs["a0"]
            for t in tiles(out.shape[0]):
                out[t, :] = dot(x[t, :], g[...]).astype(bf16)
            emit("a0")
    if kind == "O":
        a_in, a_out = have("s1g"), have("s3r")
        if a_in:
            g, x, got, s1 = get("s1g"), get("s1x"), get("s1r"), out_bufs["s1"]
            for t in tiles(s1.shape[0]):
                s1[t, :] = (dot(x[t, :], g[...]) + got[t, :].astype(f32)).astype(bf16)
            emit("s1")
        if a_in or a_out:
            out = out_bufs["a"]
            n_in = s1.shape[0] if a_in else 0
            n_out = bufs["s3r"].shape[0] if a_out else 0
            if a_out:
                own, got = get("s3o"), get("s3r")
            for t in tiles(out.shape[0]):
                v = s1[t, :] if t.start < n_in else None
                if t.start < n_out:
                    u = low(own[t, :], got[t, :])
                    v = u if v is None else jnp.where(outer, v, u)
                out[t, :] = v
            emit("a")
        b_in, b_out = have("t0g"), have("t4r")
        if b_in:
            g, x, t0 = get("t0g"), get("t0x"), out_bufs["t0"]
            for t in tiles(t0.shape[0]):
                t0[t, :] = dot(x[t, :], g[...]).astype(bf16)
            emit("t0")
        if b_in or b_out:
            out = out_bufs["b"]
            n_in = t0.shape[0] if b_in else 0
            h = bufs["t4r"].shape[0] if b_out else 0
            if b_out:
                own, got = get("t4o"), get("t4r")
            for o in tiles(out.shape[0]):
                v = t0[o, :] if o.start < n_in else None
                if o.start < 2 * h:
                    back = h if o.start >= h else 0
                    t = slice(o.start - back, o.stop - back)
                    mine = jnp.logical_not(first) if back else first
                    u = jnp.where(mine, own[t, :], got[t, :])
                    v = u if v is None else jnp.where(outer, v, u)
                out[o, :] = v
            emit("b")
        if have("af"):
            finals["af"] = get("af")
    if kind == "M":
        if have("a2r"):
            own, got, out = get("a2o"), get("a2r"), out_bufs["a2"]
            for t in tiles(out.shape[0]):
                out[t, :] = low(own[t, :], got[t, :])
            emit("a2")
        if have("b3r"):
            own, got, out = get("b3o"), get("b3r"), out_bufs["b3"]
            for t in tiles(out.shape[0]):
                out[t, :] = low(own[t, :], got[t, :])
            emit("b3")
        if have("b1o"):
            own, got, out, keep = get("b1o"), get("ob"), out_bufs["b1"], out_bufs["keep"]
            h = out.shape[0]
            for t in tiles(h):
                o = slice(h + t.start, h + t.stop)
                top, bottom = low(own[t, :], got[t, :]), low(own[o, :], got[o, :])
                out[t, :] = jnp.where(first, bottom, top)
                keep[t, :] = jnp.where(first, top, bottom)
            emit("b1")
            emit("keep")
        if have("fino"):
            own, got = get("fino"), get("ob")
            finals["fin"] = (got, own)
    for i, (name, r0, rows, col) in enumerate(stores):
        src, buf = finals[name], f_bufs[i]
        for t in tiles(buf.shape[0]):
            if name == "fin":
                buf[t, :] = jnp.where(outer, src[0][t, :], src[1][t, :]).astype(f32)
            else:
                buf[t, :] = src[t, :].astype(f32)
        dst = outs[len(outs) - len(stores) + i]
        ship(buf, dst.at[pl.ds(first_row(r0, rows, dp), rows), pl.ds(col, buf.shape[1])])
    for cp in done:
        cp.wait()


class Rounds:
    def __init__(self, at, outs, line):
        self.at, self.outs, self.line = at, outs, line
        self.a, self.b = {}, {}
        self.got = {}
        self.r = 0
        self.swap_outer = [(0, 1), (1, 0), (2, 3), (3, 2)]
        self.scal = jnp.stack([at.dp, at.z, jnp.int32(at.n)]).astype(jnp.int32)

    def piece(self, kind, r, name, own=False, some=None):
        sent, got, table = self.got[kind, r]
        at = 0
        for k, rows in table:
            if k == name:
                return (sent if own else got), (at, rows if some is None else some)
            at += rows

    def run(self, kind, b, pieces, extras, stores, flops):
        rows = {n: r for n, r in pieces + extras}
        w = self.width
        loads = tuple((k,) + v for k, v in b.loads.items())
        any_ = pl.BlockSpec(memory_space=pl.ANY)
        smem = pl.BlockSpec(memory_space=pltpu.SMEM)
        shapes, aliases = [jax.ShapeDtypeStruct((1,), jnp.int32)], {}
        if pieces:
            shapes.append(jax.ShapeDtypeStruct((sum(r for _, r in pieces), w), bf16))
        if extras:
            shapes.append(jax.ShapeDtypeStruct((sum(r for _, r in extras), w), bf16))
        for which, *_ in stores:
            aliases[2 + len(b.refs) + len(aliases)] = len(shapes)
            shapes.append(jax.ShapeDtypeStruct(self.outs[which].shape, f32))
        scratch = [pltpu.VMEM(shape, bf16) for _, shape, _ in loads]
        scratch += [pltpu.VMEM((rows[n], w), bf16) for n, _ in pieces + extras]
        scratch += [pltpu.VMEM((r, w), f32) for _, _, _, r, _ in stores]
        n_out = len(pieces) + len(extras) + len(stores)
        n_load = sum(len(parts) for _, _, parts in loads)
        scratch += [pltpu.SemaphoreType.DMA((n_load,)), pltpu.SemaphoreType.DMA((n_out,))]
        moved = sum(m * n * 2 for _, (m, n), _ in loads) + sum(rows.values()) * w * 2
        moved += sum(r * w * 4 for _, _, _, r, _ in stores)
        n_in = len(b.refs) + len(stores)
        out = pl.pallas_call(
            functools.partial(
                round_kernel, kind, loads, n_in, tuple(pieces), tuple(extras),
                tuple(s[1:] for s in stores),
            ),
            out_shape=shapes,
            in_specs=[smem, smem] + [any_] * n_in,
            out_specs=[smem] + [any_] * (len(shapes) - 1),
            input_output_aliases=aliases,
            scratch_shapes=scratch,
            cost_estimate=BRIEF,
            name="round_" + kind.lower(),
        )(self.scal, self.line.token, *b.refs, *[self.outs[s[0]] for s in stores])
        self.line.token, *out = out
        for which, *_ in reversed(stores):
            self.outs[which] = out.pop()
        extra = out.pop() if extras else None
        if pieces:
            axis, pairs = {
                "X": (DP, self.at.swap), "O": (SEQ, self.swap_outer), "M": (SEQ, self.at.mid),
            }[kind]
            self.got[kind, self.r] = (out[0], lax.ppermute(out[0], axis, pairs), pieces)
        return extra

    def step_x(self):
        r, A, B = self.r, self.a, self.b
        b, pieces, stores, flops = Round(), [], [], 0
        if r in A:
            c = A[r]
            half, tok = c["rows"][1] // 2, sum(x.shape[1] for x in c["x"])
            b.load_down("a0g", c["grad"], c["cols"])
            b.load_across("a0x", c["x"], ((False, c["rows"][0]), half))
            pieces.append(("a0", half))
            flops += 2 * half * tok * c["cols"][1]
        if r - 6 in A:
            c = A[r - 6]
            rows = c["rows"][1] // 2
            b.load("a4r", *self.piece("O", r - 2, "a", False, rows))
            b.load("a4o", *self.piece("O", r - 2, "a", True, rows))
            pieces.append(("a4", rows))
            stores.append((c["which"], "a4", (True, c["rows"][0]), rows, c["col"]))
        if r - 3 in B:
            c = B[r - 3]
            b.load("b2r", *self.piece("M", r - 2, "b1"))
            b.load("b2o", *c["keep"])
            pieces.append(("b2", b.loads["b2r"][0][0]))
        if pieces:
            self.run("X", b, pieces, [], stores, flops)

    def step_o(self):
        r, A, B = self.r, self.a, self.b
        b, pieces, extras, stores, flops = Round(), [], [], [], 0
        if r - 1 in A:
            c = A[r - 1]
            half, tok = c["rows"][1] // 2, sum(x.shape[1] for x in c["x"])
            b.load_down("s1g", c["grad"], c["cols"])
            b.load_across("s1x", c["x"], ((True, c["rows"][0]), half))
            b.load("s1r", *self.piece("X", r - 1, "a0"))
            extras.append(("s1", half))
            flops += 2 * half * tok * c["cols"][1]
        if r - 4 in A:
            b.load("s3o", *self.piece("M", r - 2, "a2", True))
            b.load("s3r", *self.piece("M", r - 2, "a2"))
        if r - 1 in A or r - 4 in A:
            sizes = [A[k]["rows"][1] // 2 for k in (r - 1, r - 4) if k in A]
            pieces.append(("a", max(sizes)))
        if r in B:
            c = B[r]
            rows, tok = c["rows"][1], sum(x.shape[1] for x in c["x"])
            b.load_down("t0g", c["grad"], c["cols"])
            b.load_across("t0x", c["x"], c["rows"])
            extras.append(("t0", rows))
            flops += 2 * rows * tok * c["cols"][1]
        if r - 6 in B:
            b.load("t4o", *self.piece("M", r - 2, "b3", True))
            b.load("t4r", *self.piece("M", r - 2, "b3"))
        if r in B or r - 6 in B:
            pieces.append(("b", max(B[k]["rows"][1] for k in (r, r - 6) if k in B)))
        if r - 7 in A:
            c = A.pop(r - 7)
            b.load("af", *self.piece("X", r - 1, "a4"))
            first = (False, c["rows"][0])
            stores.append((c["which"], "af", first, b.loads["af"][0][0], c["col"]))
        if pieces or stores:
            extra = self.run("O", b, pieces, extras, stores, flops)
            at = 0
            for name, n in extras:
                (A[r - 1] if name == "s1" else B[r])[name] = (extra, (at, n))
                at += n

    def step_m(self):
        r, A, B = self.r, self.a, self.b
        b, pieces, extras, stores = Round(), [], [], []
        if r - 2 in A:
            rows = A[r - 2]["rows"][1] // 2
            b.load("a2o", *A[r - 2]["s1"])
            b.load("a2r", *self.piece("O", r - 1, "a", False, rows))
            pieces.append(("a2", rows))
        if r - 1 in B or r - 7 in B:
            b.load("ob", *self.piece("O", r - 1, "b"))
        if r - 1 in B:
            h = B[r - 1]["rows"][1] // 2
            b.load("b1o", *B[r - 1]["t0"])
            pieces.append(("b1", h))
            extras.append(("keep", h))
        if r - 4 in B:
            b.load("b3o", *self.piece("X", r - 1, "b2", True))
            b.load("b3r", *self.piece("X", r - 1, "b2"))
            pieces.append(("b3", b.loads["b3r"][0][0]))
        if r - 7 in B:
            c = B.pop(r - 7)
            b.load("fino", *self.piece("O", r - 1, "b", True, c["rows"][1]))
            stores.append((c["which"], "fin", c["rows"][0], c["rows"][1], c["col"]))
        if pieces or stores:
            extra = self.run("M", b, pieces, extras, stores, 0)
            if extras:
                B[r - 1]["keep"] = (extra, (0, h))


def blank_kernel(*outs):
    pass


def blanks(shapes):
    return pl.pallas_call(
        blank_kernel,
        out_shape=[jax.ShapeDtypeStruct(s, f32) for s in shapes],
        out_specs=[pl.BlockSpec(memory_space=pl.ANY)] * len(shapes),
    )()


def gather_steps(x, n, axis=0, wait=0):
    got = None
    for b in reversed(bits_of(n)):
        if got is not None:
            x = jnp.concatenate([x, got], axis=axis)
        got = lax.ppermute(x, MP, xor_perm(n, b))
        if wait:
            yield (), x
            yield from idle(wait - 1)
            got = yield got, ()
        else:
            got = yield got, x
    return [x, got]


def joined(pieces, axis=0):
    return jnp.concatenate(pieces, axis=axis)


def scatter_steps(x, n, axis=0, wait=0):
    for b in bits_of(n):
        if isinstance(x, tuple):
            keep, send = x
        else:
            half = x.shape[axis] // 2
            keep = lax.slice_in_dim(x, 0, half, axis=axis)
            send = lax.slice_in_dim(x, half, 2 * half, axis=axis)
        got = lax.ppermute(send, MP, xor_perm(n, b))
        if wait:
            yield (), (send, keep)
            yield from idle(wait - 1)
            got = yield got, ()
        else:
            got = yield got, (send, keep)
        x = keep.astype(f32) + got.astype(f32)
        if 2 * b < n:
            x = x.astype(bf16)
    return x.astype(f32)


def sum_rows_steps(x, n):
    masks = row_masks(n)
    for b in bits_of(n):
        got = yield lax.ppermute(x, MP, xor_perm(n, b)), x
        got = got.reshape(x.shape[:-1] + (n, -1))
        order = [masks.index(m ^ b) for m in masks]
        got = jnp.stack([got[..., k, :] for k in order], axis=-2)
        x = x + got.reshape(x.shape)
    return x


def exchange_steps(pieces, n):
    rows = pieces[0].shape[0]
    held = {(j, 0): p for j, p in enumerate(pieces)}
    for b in bits_of(n):
        far = [k for k in held if k[0] & b]
        sent = jnp.concatenate([held.pop(k) for k in far], axis=0)
        got = yield lax.ppermute(sent, SEQ, xor_perm(n, b)), sent
        for t, (to, source) in enumerate(far):
            held[to ^ b, source ^ b] = got[t * rows : (t + 1) * rows]
    return [held[0, j] for j in range(n)]


class Layer:
    pass


def forward_task(c, m):
    f = c.fwd[m]
    own = c.tokens[m]
    length = c.lengths[m, 0]
    x = f.x = yield from gather_steps(own, c.n_mp)
    proj = dot(joined(x), c.qkv_weight)
    local = c.local
    squares = jnp.stack(
        [jnp.sum(jnp.square(proj[:, t * local : (t + 1) * local]), axis=1) for t in (0, 1)], axis=0
    )
    squares = yield from sum_rows_steps(squares, c.n_mp)
    inv = lax.rsqrt(squares / c.width + epsilon).T
    pieces = rope_call(c.slots, c.z_arr, proj, inv, c.cos, c.sin, c.qg, c.kg)
    if c.by_heads:
        scal = jnp.stack([c.z, c.me, length]).astype(jnp.int32)
        f.pieces = yield from exchange_steps(pieces, c.n_seq)
        mixed, f.kept = attend(scal, f.pieces, c.masks)
        mixed = yield from exchange_steps(mixed, c.n_seq)
        mixed = join_heads(c.z_arr, mixed)
    else:
        mixed, f.kept = gathered_attend(pieces[0], c.pos, length)
    attended = yield from scatter_steps(dot(mixed, c.o_weight).astype(bf16), c.n_mp)
    attn_inv = inv_rms(attended)
    hidden = own.astype(f32) + attended * attn_inv * c.attn_gain
    mlp_in = yield from gather_steps(hidden.astype(bf16), c.n_mp)
    f.mlp_in = mlp_in
    rows_in = joined(mlp_in)
    f.gate, f.up = dot(rows_in, c.gate_weight), dot(rows_in, c.up_weight)
    f.act = (f.gate * jax.nn.sigmoid(f.gate) * f.up).astype(bf16)
    mlp_out = yield from scatter_steps(dot(f.act, c.down_weight).astype(bf16), c.n_mp)
    mlp_inv = inv_rms(mlp_out)
    f.layer = (hidden + mlp_out * mlp_inv * c.mlp_gain).astype(bf16)
    f.seeds = c.cotangent[m].astype(f32) * (c.own_pos < length).astype(f32)[:, None]
    mlp_grad, gain_rows = norm_backward(mlp_out, mlp_inv, c.mlp_gain, f.seeds)
    f.mlp_gain = jnp.sum(gain_rows, axis=0)
    f.mlp_grad = yield from gather_steps(mlp_grad.astype(bf16), c.n_mp)
    f.proj, f.inv, f.mixed, f.attended, f.attn_inv = proj, inv, mixed, attended, attn_inv
    return ()


def backward_task(c):
    n, rows, fwd = len(c.fwd), c.rows, c.fwd
    yield (), ()
    gates = mlp_back(
        c.line, [x for f in fwd for x in f.mlp_grad], c.down_weight, [f.gate for f in fwd], [f.up for f in fwd]
    )
    for f, f.gate_grad, f.up_grad in zip(fwd, *gates):
        pass
    yield (), ()
    back = hidden_back(c.line, gates[0], c.gate_weight, gates[1], c.up_weight)
    back = yield from scatter_steps(back, c.n_mp, 1, c.far)
    hidden_grad, attn_grad = [], []
    for m, f in enumerate(fwd):
        hidden_grad.append(f.seeds + back[m])
        e, gain_rows = norm_backward(f.attended, f.attn_inv, c.attn_gain, hidden_grad[m])
        f.attn_gain = jnp.sum(gain_rows, axis=0)
        attn_grad.append(e.astype(bf16))
    attn_grad = yield from gather_steps(jnp.stack(attn_grad), c.n_mp, 1, c.far)
    c.attn_grad = [x.reshape(-1, c.width) for x in attn_grad]
    dy = [dot_nt(x, c.o_weight).astype(bf16).reshape(n, -1, c.local) for x in c.attn_grad]
    dy = joined(dy, 1).reshape(n * rows, c.local)
    if not c.rounds:
        c.attn_grad_all = joined(attn_grad, 1).reshape(n * rows, c.width)
    if c.by_heads:
        dys = split_heads(c.z_arr, dy, c.slots)
        dys = yield from exchange_steps(dys, c.n_seq)
        scal = jnp.concatenate([jnp.stack([c.z, c.me]), c.lengths[:, 0]]).astype(jnp.int32)
        grads = attend_back(scal, [f.pieces for f in fwd], [f.kept for f in fwd], dys, c.masks)
        grads = yield from exchange_steps(grads, c.n_seq)
    else:
        grads = [gathered_back(f.kept, dy[m * rows : (m + 1) * rows]) for m, f in enumerate(fwd)]
        grads = [jnp.concatenate(grads, axis=0)]
    tables = (c.cos, c.sin, c.qg, c.kg)
    cross = []
    for m, f in enumerate(fwd):
        e, f.gains = cross_call(c.slots, m, c.z_arr, grads, f.proj, f.inv, *tables)
        cross.append(e.T)
    cross = yield from sum_rows_steps(jnp.concatenate(cross, axis=0), c.n_mp)
    for m, f in enumerate(fwd):
        e = cross[2 * m : 2 * m + 2].T
        f.qkv_grad = raw_call(
            c.slots, c.width, m, c.z_arr, grads, f.proj, f.inv, e, *tables
        )
    yield (), [f.qkv_grad for f in fwd]
    back = jnp.stack([dot_nt(f.qkv_grad, c.qkv_weight).astype(bf16) for f in fwd])
    back = yield from scatter_steps(back, c.n_mp, 1, c.far)
    c.input_grad = jnp.stack(hidden_grad) + back
    return c.input_grad


def turning_task(c):
    yield (), ()
    c.attn_grad_t = []
    for m in range(len(c.fwd)):
        c.attn_grad_t.append(turn(c.line, c.attn_grad, m, len(c.fwd)))
        yield (), ()


def gains_task(c):
    yield (), ()
    gains = sum(f.gains for f in c.fwd)
    gains = lax.dynamic_update_slice(jnp.zeros((2, c.width), f32), gains, (0, c.me * c.local))
    gains = jnp.concatenate(
        [gains, sum(f.attn_gain for f in c.fwd)[None], sum(f.mlp_gain for f in c.fwd)[None]], axis=0
    )
    for name, n in ((MP, c.n_mp), (SEQ, c.n_seq), (DP, c.n_dp)):
        for b in bits_of(n):
            got = lax.ppermute(gains, name, xor_perm(n, b))
            yield (), gains
            if c.rounds:
                yield from idle(0)
            got = yield got, ()
            gains = gains + got
    c.gains = gains
    return gains


def per_device(
    n_dp, n_seq, n_mp,
    tokens, lengths, cotangent, q_weight, k_weight, v_weight, o_weight, q_gain, k_gain,
    attn_gain, gate_weight, up_weight, down_weight, mlp_gain,
):
    c = Layer()
    micros, own_rows, width = tokens.shape
    rows = own_rows * n_mp
    local = q_weight.shape[1]
    heads = local // HEAD_DIM
    ff = gate_weight.shape[1]
    me, z = lax.axis_index(MP), lax.axis_index(SEQ)
    c.tokens, c.lengths, c.cotangent, c.o_weight = tokens, lengths, cotangent, o_weight
    c.gate_weight, c.up_weight, c.down_weight = gate_weight, up_weight, down_weight
    c.attn_gain, c.mlp_gain = attn_gain, mlp_gain
    c.n_dp, c.n_seq, c.n_mp, c.rows, c.width, c.local = n_dp, n_seq, n_mp, rows, width, local
    c.me, c.z, c.masks = me, z, row_masks(n_mp)
    c.by_heads = heads == n_seq
    c.slots = n_seq if c.by_heads else 1
    c.z_arr = z.astype(jnp.int32).reshape(1)
    c.qkv_weight = jnp.concatenate([q_weight, k_weight, v_weight], axis=1)
    c.qg = lax.dynamic_slice_in_dim(q_gain, me * local, local)[None]
    c.kg = lax.dynamic_slice_in_dim(k_gain, me * local, local)[None]
    block = jnp.asarray(c.masks, jnp.int32) ^ me
    steps = jnp.arange(own_rows, dtype=jnp.int32)
    c.pos = z * rows + (block[:, None] * own_rows + steps).reshape(-1)
    c.own_pos = z * rows + me * own_rows + steps
    frequency = rope_base ** (-(jnp.arange(HALF, dtype=f32) * 2.0 / HEAD_DIM))
    angles = c.pos.astype(f32)[:, None] * frequency[None, :]
    cos, sin = jnp.cos(angles), jnp.sin(angles)
    c.cos = jnp.concatenate([cos, cos], axis=1)
    c.sin = jnp.concatenate([-sin, sin], axis=1)
    c.fwd = [Layer() for _ in range(micros)]

    at = Place(n_seq)
    c.rounds = rounds = n_seq == 4
    line = c.line = Line(jnp.zeros((1,), jnp.int32))
    fw = [forward_task(c, m) for m in range(micros)]
    line.add(*fw)
    def turned(m, name):
        f = c.fwd[m]
        rows_ = getattr(f, name)
        setattr(f, name + "_t", turn(line, rows_ if isinstance(rows_, list) else [rows_]))

    extra = {"a": (0, "x"), "b": (1, "x"), "c": (0, "act"), "d": (1, "act"), "e": (0, "mlp_in"), "f": (1, "mlp_in")}
    order = ORDER if (micros, n_mp, c.by_heads) == (2, 4, True) and rounds else ""
    for act in order:
        if act in extra:
            turned(*extra[act])
        else:
            line.step(fw[int(act)])
    while any(t in line.waits for t in fw):
        for t in fw:
            line.step(t)

    c.far = 0
    each = lambda name: [getattr(f, name) for f in c.fwd]
    outs = list(blanks(
        [(ff, width), (width, ff), (width, ff)]
        + [(width, local)] * 3
        + [(width, local) if rounds else (local, width)]
    ))
    back, gains = backward_task(c), gains_task(c)
    side = []
    line.add(back)

    stack = lambda lists: [x for pieces in lists for x in pieces]
    both = lambda name: jnp.concatenate(each(name), axis=0)
    both2 = lambda name: jnp.concatenate(stack(each(name)), axis=0)

    def work(key):
        if rounds:
            return {
                "down": lambda: (each("act_t"), stack(each("mlp_grad"))),
                "gate": lambda: (each("mlp_in_t"), each("gate_grad")),
                "up": lambda: (each("mlp_in_t"), each("up_grad")),
                "o": lambda: (c.attn_grad_t, each("mixed")),
                "qkv": lambda: (each("x_t"), each("qkv_grad")),
            }[key]()
        return {
            "down": lambda: (both("act"), both2("mlp_grad")),
            "gate": lambda: (both2("mlp_in"), both("gate_grad")),
            "up": lambda: (both2("mlp_in"), both("up_grad")),
            "o": lambda: (both("mixed"), c.attn_grad_all),
            "qkv": lambda: (both2("x"), both("qkv_grad")),
        }[key]()

    done, live = {}, []
    if rounds:
        reducer = Rounds(at, outs, line)
        reducer.width = local // 2

    def rows_of(key):
        if key not in done:
            done[key] = work(key)
        return done[key]

    def one_round(new_a, new_b, script=""):
        if rounds:
            for new, table in ((new_a, reducer.a), (new_b, reducer.b)):
                if new is not None:
                    key, which, first, n, col, span = new
                    x, grad = rows_of(key)
                    table[reducer.r] = dict(
                        x=x, grad=grad, cols=(first, n), which=which, col=col, rows=span
                    )
            for act in script:
                if act in "XOM":
                    getattr(reducer, "step_" + act.lower())()
                else:
                    line.step({"c": back, "t": turning, "g": gains}[act])
            reducer.r += 1
            return
        for new, kind in ((new_a, "a"), (new_b, "b")):
            if new is not None:
                key, which, first, n, col, _ = new
                x, grad = rows_of(key)
                if kind == "a":
                    if key + "/" not in done:
                        done[key + "/"] = (take_half(x, at.dp, False), take_half(x, at.dp, True))
                    t = task_a(at, outs, which, *done[key + "/"], grad, slice(first, first + n), col)
                else:
                    t = task_b(at, outs, which, x, grad, slice(first, first + n), col)
                line.add(t)
                live.append(t)
        live[:] = line.step(*live)
        for t in side:
            line.step(t)

    unit = local // 2
    cut = lambda key, which, n, u=unit, first=0, parts=1: [
        (key, which, first + t, u, t, (k * (width // parts), width // parts))
        for t in range(0, n, u)
        for k in range(parts)
    ]
    ready = {
        "down": lambda: True,
        "gate": lambda: all(hasattr(f, "up_grad") for f in c.fwd),
        "o": lambda: len(c.attn_grad_t) == micros if rounds else hasattr(c, "attn_grad_all"),
        "qkv": lambda: all(hasattr(f, "qkv_grad") for f in c.fwd),
    }
    ready["up"] = ready["gate"]
    todo = cut("down", 0, width) + cut("gate", 1, ff) + cut("up", 2, ff)
    todo += cut("o", 6, local) if rounds else cut("o", 6, width, width // 2)
    for t in range(3):
        todo += cut("qkv", 3 + t, local, first=t * local, parts=2 if rounds and t else 1)
    c.attn_grad_t = []
    if rounds:
        for m in range(micros):
            for name in ("x", "act", "mlp_in"):
                if not hasattr(c.fwd[m], name + "_t"):
                    turned(m, name)
        turning = turning_task(c)
        line.add(turning)
    else:
        side = [back]
    count_a = len(todo) // 2

    def take():
        for i, chunk in enumerate(todo):
            if ready[chunk[0]]():
                return todo.pop(i)
        return None

    gains_on = False
    r = taken_a = 0
    while todo or any(t in line.waits for t in (back, gains)) or (
        reducer.a or reducer.b if rounds else live
    ):
        late = ready["qkv"]()
        if late and not gains_on and not (rounds and todo):
            gains_on = True
            side.append(gains)
            line.add(gains)
        new_a = take() if taken_a < count_a else None
        taken_a += new_a is not None
        script = SCRIPT[r] if r < len(SCRIPT) else "XgOcMg"
        lone = rounds and r < len(SCRIPT) and script[-1:] == "-"
        new_b = None if lone else take()
        one_round(new_a, new_b, script.strip("-") if rounds else "")
        r += 1
    return (
        jnp.stack(each("layer")),
        c.input_grad,
        outs[3],
        outs[4],
        outs[5],
        outs[6].T if rounds else outs[6],
        c.gains[0],
        c.gains[1],
        c.gains[2],
        outs[1],
        outs[2],
        outs[0],
        c.gains[3],
    )


SCRIPT = (
    "XOc",
    "XcOM",
    "XcOM",
    "XcOM",
    "XOcM",
    "XOcM",
    "XOMc",
    "XOtMtc",
    "XOcM",
    "XcOMc",
    "XOMc",
)

ORDER = "000011011ab010001011010" "10ce1101d0f1011"


def solution(mesh):
    n_dp, n_seq, n_mp = (mesh.shape[a] for a in (DP, SEQ, MP))
    assert n_dp == 2
    rows = P(None, (DP, SEQ, MP), None)
    cols, flat, all_ = P(None, MP), P(MP, None), P()
    return jax.shard_map(
        functools.partial(per_device, n_dp, n_seq, n_mp),
        mesh=mesh,
        in_specs=(rows, P(None, DP), rows, cols, cols, cols, flat, all_, all_, all_, cols, cols, flat, all_),
        out_specs=(rows, rows, cols, cols, cols, flat, all_, all_, all_, cols, cols, flat, all_),
        check_vma=False,
    )
```

```python
import functools

import jax
import jax.numpy as jnp
from jax import lax
from jax.experimental import pallas as pl
from jax.experimental.pallas import tpu as pltpu
from jax.sharding import PartitionSpec as P

HEAD_DIM = 128
HALF = HEAD_DIM // 2
DP, SEQ, MP = "dp", "seq", "mp"
TO_KEYS, TO_ROWS, TO_HEADS = "shd,khd->shk", "shk,khd->shd", "shk,shd->khd"
epsilon = 1e-06
rope_base = 500000.0
masked_score = -1e30
LOG2E = 1.4426950408889634

f32 = jnp.float32
bf16 = jnp.bfloat16


def add_low(a, b):
    return (a.astype(f32) + b.astype(f32)).astype(bf16)


def bits_of(n):
    out = []
    b = 1
    while b < n:
        out.append(b)
        b *= 2
    return out


def xor_perm(n, b):
    return [(i, i ^ b) for i in range(n)]


def row_masks(n):
    masks = [0]
    for b in reversed(bits_of(n)):
        masks = masks + [m | b for m in masks]
    return masks


def inv_rms(v):
    return lax.rsqrt(jnp.mean(v * v, axis=-1, keepdims=True) + epsilon)


def norm_backward(source, inverse, gain_vec, upstream):
    normed = source * inverse
    weighted = upstream * gain_vec
    back = inverse * (weighted - normed * jnp.mean(weighted * normed, axis=-1, keepdims=True))
    return back, upstream * normed


def dot_t(a, b):
    return lax.dot_general(a, b, (((0,), (0,)), ((), ())), preferred_element_type=f32)


def dot_nt(a, b):
    return lax.dot_general(a, b, (((1,), (1,)), ((), ())), preferred_element_type=f32)


def dot(a, b):
    return jnp.dot(a, b, preferred_element_type=f32)


def rope_kernel(slots, width, local, z_ref, proj, inv, cos, sin, qg, kg, *outs):
    z = z_ref[0]
    c, s = cos[...], sin[...]
    for j in range(slots):
        base = (z ^ j) * width if slots > 1 else 0
        for h in range(width // HEAD_DIM):
            at = base + h * HEAD_DIM
            at = pl.multiple_of(at, HEAD_DIM) if slots > 1 else at
            for part, gain in ((0, qg), (1, kg)):
                raw = proj[:, pl.ds(part * local + at, HEAD_DIM)]
                v = raw * inv[:, part : part + 1] * gain[:, pl.ds(at, HEAD_DIM)]
                v = v * c + pltpu.roll(v, HALF, 1) * s
                lo = part * width + h * HEAD_DIM
                outs[j][:, lo : lo + HEAD_DIM] = v.astype(bf16)
            lo = 2 * width + h * HEAD_DIM
            outs[j][:, lo : lo + HEAD_DIM] = proj[:, pl.ds(2 * local + at, HEAD_DIM)].astype(bf16)


def rope_call(slots, z, proj, inv, cos, sin, qg, kg):
    rows, local = proj.shape[0], proj.shape[1] // 3
    width = local // slots
    blk = min(rows, 256)
    row = lambda n: pl.BlockSpec((blk, n), lambda i, *_: (i, 0))
    vec = pl.BlockSpec((1, local), lambda i, *_: (0, 0))
    return pl.pallas_call(
        functools.partial(rope_kernel, slots, width, local),
        out_shape=[jax.ShapeDtypeStruct((rows, 3 * width), bf16)] * slots,
        grid_spec=pltpu.PrefetchScalarGridSpec(
            num_scalar_prefetch=1,
            grid=(rows // blk,),
            in_specs=[row(3 * local), row(2), row(HEAD_DIM), row(HEAD_DIM), vec, vec],
            out_specs=[row(3 * width)] * slots,
        ),
        cost_estimate=pl.CostEstimate(
            flops=rows * local * 12, bytes_accessed=rows * local * 18, transcendentals=0
        ),
    )(z, proj, inv, cos, sin, qg, kg)


def unrope(grad, c, s):
    g = grad.astype(f32)
    return g * c - pltpu.roll(g, HALF, 1) * s


def cross_kernel(slots, width, local, z_ref, *refs):
    grads = refs[:slots]
    proj, inv, cos, sin, qg, kg, cross, gains = refs[slots:]
    z = z_ref[0]
    c, s = cos[...], sin[...]

    @pl.when(pl.program_id(0) == 0)
    def _():
        gains[...] = jnp.zeros_like(gains)

    for part, gain in ((0, qg), (1, kg)):
        total = None
        for j in range(slots):
            base = (z ^ j) * width if slots > 1 else 0
            for h in range(width // HEAD_DIM):
                at = base + h * HEAD_DIM
                at = pl.multiple_of(at, HEAD_DIM) if slots > 1 else at
                lo = part * width + h * HEAD_DIM
                g = unrope(grads[j][:, lo : lo + HEAD_DIM], c, s)
                gr = g * proj[:, pl.ds(part * local + at, HEAD_DIM)]
                w = gr * gain[:, pl.ds(at, HEAD_DIM)]
                total = w if total is None else total + w
                col = jnp.sum(gr * inv[:, part : part + 1], axis=0, keepdims=True)
                gains[part : part + 1, pl.ds(at, HEAD_DIM)] += col
        cross[:, part : part + 1] = jnp.sum(total, axis=1, keepdims=True)


def raw_kernel(slots, width, local, d, z_ref, *refs):
    grads = refs[:slots]
    proj, inv, cross, cos, sin, qg, kg, out = refs[slots:]
    z = z_ref[0]
    c, s = cos[...], sin[...]
    for j in range(slots):
        base = (z ^ j) * width if slots > 1 else 0
        for h in range(width // HEAD_DIM):
            at = base + h * HEAD_DIM
            at = pl.multiple_of(at, HEAD_DIM) if slots > 1 else at
            for part, gain in ((0, qg), (1, kg)):
                lo = part * width + h * HEAD_DIM
                g = unrope(grads[j][:, lo : lo + HEAD_DIM], c, s)
                r = inv[:, part : part + 1]
                w = g * gain[:, pl.ds(at, HEAD_DIM)] * r
                k = r * r * r * (cross[:, part : part + 1] * (1.0 / d))
                w = w - proj[:, pl.ds(part * local + at, HEAD_DIM)] * k
                out[:, pl.ds(part * local + at, HEAD_DIM)] = w.astype(bf16)
            lo = 2 * width + h * HEAD_DIM
            out[:, pl.ds(2 * local + at, HEAD_DIM)] = grads[j][:, lo : lo + HEAD_DIM]


def cross_call(slots, m, z, grads, proj, inv, cos, sin, qg, kg):
    rows, local = proj.shape[0], proj.shape[1] // 3
    width = local // slots
    blk = min(rows, 256)
    far = lambda n: pl.BlockSpec((blk, n), lambda i, *_: (i + m * (rows // blk), 0))
    row = lambda n: pl.BlockSpec((blk, n), lambda i, *_: (i, 0))
    vec = pl.BlockSpec((1, local), lambda i, *_: (0, 0))
    return pl.pallas_call(
        functools.partial(cross_kernel, slots, width, local),
        out_shape=[
            jax.ShapeDtypeStruct((rows, 2), f32),
            jax.ShapeDtypeStruct((2, local), f32),
        ],
        grid_spec=pltpu.PrefetchScalarGridSpec(
            num_scalar_prefetch=1,
            grid=(rows // blk,),
            in_specs=[far(3 * width)] * slots
            + [row(3 * local), row(2), row(HEAD_DIM), row(HEAD_DIM), vec, vec],
            out_specs=[row(2), pl.BlockSpec((2, local), lambda i, *_: (0, 0))],
        ),
        cost_estimate=pl.CostEstimate(
            flops=rows * local * 20, bytes_accessed=rows * local * 18, transcendentals=0
        ),
    )(z, *grads, proj, inv, cos, sin, qg, kg)


def raw_call(slots, d, m, z, grads, proj, inv, cross, cos, sin, qg, kg):
    rows, local = proj.shape[0], proj.shape[1] // 3
    width = local // slots
    blk = min(rows, 256)
    far = lambda n: pl.BlockSpec((blk, n), lambda i, *_: (i + m * (rows // blk), 0))
    row = lambda n: pl.BlockSpec((blk, n), lambda i, *_: (i, 0))
    vec = pl.BlockSpec((1, local), lambda i, *_: (0, 0))
    return pl.pallas_call(
        functools.partial(raw_kernel, slots, width, local, d),
        out_shape=jax.ShapeDtypeStruct((rows, 3 * local), bf16),
        grid_spec=pltpu.PrefetchScalarGridSpec(
            num_scalar_prefetch=1,
            grid=(rows // blk,),
            in_specs=[far(3 * width)] * slots
            + [row(3 * local), row(2), row(2), row(HEAD_DIM), row(HEAD_DIM), vec, vec],
            out_specs=row(3 * local),
        ),
        cost_estimate=pl.CostEstimate(
            flops=rows * local * 20, bytes_accessed=rows * local * 24, transcendentals=0
        ),
    )(z, *grads, proj, inv, cross, cos, sin, qg, kg)


def join_kernel(slots, width, z_ref, *refs):
    z = z_ref[0]
    out = refs[slots]
    for j in range(slots):
        out[:, pl.ds(pl.multiple_of((z ^ j) * width, HEAD_DIM), width)] = refs[j][...]


def join_heads(z, pieces):
    rows, width = pieces[0].shape
    slots = len(pieces)
    blk = min(rows, 256)
    return pl.pallas_call(
        functools.partial(join_kernel, slots, width),
        out_shape=jax.ShapeDtypeStruct((rows, slots * width), bf16),
        grid_spec=pltpu.PrefetchScalarGridSpec(
            num_scalar_prefetch=1,
            grid=(rows // blk,),
            in_specs=[pl.BlockSpec((blk, width), lambda i, *_: (i, 0))] * slots,
            out_specs=pl.BlockSpec((blk, slots * width), lambda i, *_: (i, 0)),
        ),
    )(z, *pieces)


def split_kernel(slots, width, z_ref, x, *outs):
    z = z_ref[0]
    for j in range(slots):
        outs[j][...] = x[:, pl.ds(pl.multiple_of((z ^ j) * width, HEAD_DIM), width)]


def split_heads(z, x, slots):
    rows, local = x.shape
    width = local // slots
    blk = min(rows, 256)
    return pl.pallas_call(
        functools.partial(split_kernel, slots, width),
        out_shape=[jax.ShapeDtypeStruct((rows, width), bf16)] * slots,
        grid_spec=pltpu.PrefetchScalarGridSpec(
            num_scalar_prefetch=1,
            grid=(rows // blk,),
            in_specs=[pl.BlockSpec((blk, local), lambda i, *_: (i, 0))],
            out_specs=[pl.BlockSpec((blk, width), lambda i, *_: (i, 0))] * slots,
        ),
    )(z, x)


def exchange(pieces, n):
    return [p if j == 0 else lax.ppermute(p, SEQ, xor_perm(n, j)) for j, p in enumerate(pieces)]


def row_places(slots, masks, rows, z, me):
    count = rows // len(masks)
    for j in range(slots):
        for k, m in enumerate(masks):
            yield j, k * count, pl.multiple_of((z ^ j) * rows + (me ^ m) * count, count), count


def key_bias(total, length):
    pos = lax.broadcasted_iota(jnp.int32, (1, total), 1)
    return jnp.where(pos < length, 0.0, masked_score).astype(f32)


def diag_mask(size):
    r = lax.broadcasted_iota(jnp.int32, (size, size), 0)
    c = lax.broadcasted_iota(jnp.int32, (size, size), 1)
    return c <= r


def attend_kernel(slots, masks, rows, blk, scal, *refs):
    pieces, outs = refs[:slots], refs[slots : 2 * slots]
    o32, lse, qkv, o16, sem = refs[2 * slots :]
    z, me, length = scal[0], scal[1], scal[2]
    total = slots * rows
    copies = []
    for t, (j, at, to, n) in enumerate(row_places(slots, masks, rows, z, me)):
        cp = pltpu.make_async_copy(pieces[j].at[pl.ds(at, n)], qkv.at[pl.ds(to, n)], sem.at[t])
        cp.start()
        copies.append(cp)
    bias = key_bias(total, length)
    causal = diag_mask(blk)
    for cp in copies:
        cp.wait()
    factor = HEAD_DIM**-0.5 * LOG2E
    for i in range(total // blk):
        lo = i * blk
        q = qkv[lo : lo + blk, :HEAD_DIM]
        s = dot_nt(q, qkv[lo : lo + blk, HEAD_DIM : 2 * HEAD_DIM]) * factor
        s = jnp.where(causal, s + bias[:, lo : lo + blk], masked_score)
        top = jnp.max(s, axis=1, keepdims=True)
        if i:
            before = dot_nt(q, qkv[:lo, HEAD_DIM : 2 * HEAD_DIM]) * factor + bias[:, :lo]
            top = jnp.maximum(top, jnp.max(before, axis=1, keepdims=True))
        p = jnp.exp2(s - top)
        mass = jnp.sum(p, axis=1, keepdims=True)
        acc = dot(p.astype(bf16), qkv[lo : lo + blk, 2 * HEAD_DIM :])
        if i:
            p = jnp.exp2(before - top)
            mass = mass + jnp.sum(p, axis=1, keepdims=True)
            acc = acc + dot(p.astype(bf16), qkv[:lo, 2 * HEAD_DIM :])
        acc = acc / mass
        o32[lo : lo + blk, :] = acc
        o16[lo : lo + blk, :] = acc.astype(bf16)
        lse[lo : lo + blk, :] = top + jnp.log(mass) * LOG2E
    copies = []
    for t, (j, at, to, n) in enumerate(row_places(slots, masks, rows, z, me)):
        cp = pltpu.make_async_copy(o16.at[pl.ds(to, n)], outs[j].at[pl.ds(at, n)], sem.at[t])
        cp.start()
        copies.append(cp)
    for cp in copies:
        cp.wait()


def attend(scal, pieces, masks):
    slots = len(pieces)
    rows = pieces[0].shape[0]
    total = slots * rows
    hbm = pl.BlockSpec(memory_space=pl.ANY)
    vmem = pl.BlockSpec(memory_space=pltpu.VMEM)
    out = pl.pallas_call(
        functools.partial(attend_kernel, slots, masks, rows, 256),
        out_shape=[jax.ShapeDtypeStruct((rows, HEAD_DIM), bf16)] * slots
        + [
            jax.ShapeDtypeStruct((total, HEAD_DIM), f32),
            jax.ShapeDtypeStruct((total, 1), f32),
        ],
        in_specs=[pl.BlockSpec(memory_space=pltpu.SMEM)] + [hbm] * slots,
        out_specs=[hbm] * slots + [vmem, vmem],
        scratch_shapes=[
            pltpu.VMEM((total, 3 * HEAD_DIM), bf16),
            pltpu.VMEM((total, HEAD_DIM), bf16),
            pltpu.SemaphoreType.DMA((slots * len(masks),)),
        ],
        cost_estimate=pl.CostEstimate(
            flops=total * total * HEAD_DIM * 4,
            bytes_accessed=total * HEAD_DIM * 12,
            transcendentals=total * total // 2,
        ),
        name="attend",
    )(scal, *pieces)
    return out[:slots], (out[slots], out[slots + 1])


def attend_back_kernel(slots, masks, rows, blk, micros, scal, *refs):
    pieces = [refs[m * slots : (m + 1) * slots] for m in range(micros)]
    refs = refs[micros * slots :]
    kept = [refs[2 * m : 2 * m + 2] for m in range(micros)]
    dos, outs = refs[2 * micros : 2 * micros + slots], refs[2 * micros + slots :][:slots]
    qkv, do, o32, lse, dkv, grad, sem = refs[2 * micros + 2 * slots :]
    micro = pl.program_id(0)
    z, me, length = scal[0], scal[1], scal[2 + micro]
    total = slots * rows
    runs = slots * len(masks)
    places = list(row_places(slots, masks, rows, z, me))
    base = micro * rows

    def incoming(m):
        out = []
        for t, (j, at, to, n) in enumerate(places):
            from_, to_ = pl.ds(at, n), pl.ds(to, n)
            out.append(pltpu.make_async_copy(pieces[m][j].at[from_], qkv.at[to_], sem.at[t]))
            far = pl.ds(pl.multiple_of(base + at, n), n)
            out.append(pltpu.make_async_copy(dos[j].at[far], do.at[to_], sem.at[runs + t]))
        out.append(pltpu.make_async_copy(kept[m][0], o32, sem.at[2 * runs]))
        out.append(pltpu.make_async_copy(kept[m][1], lse, sem.at[2 * runs + 1]))
        return out

    for m in range(micros):

        @pl.when(micro == m)
        def _(m=m):
            copies = incoming(m)
            for cp in copies:
                cp.start()
            for cp in copies:
                cp.wait()

    bias = key_bias(total, length)
    causal = diag_mask(blk)
    dkv[...] = jnp.zeros_like(dkv)
    scale = HEAD_DIM**-0.5
    factor = scale * LOG2E
    D = HEAD_DIM
    for i in range(total // blk):
        lo = i * blk
        q, dy = qkv[lo : lo + blk, :D], do[lo : lo + blk, :]
        delta = jnp.sum(dy.astype(f32) * o32[lo : lo + blk, :], axis=1, keepdims=True)
        level = lse[lo : lo + blk, :]
        dq = None
        for start, stop in ((lo, lo + blk), (0, lo)):
            if start == stop:
                continue
            keys, vals = qkv[start:stop, D : 2 * D], qkv[start:stop, 2 * D :]
            s = dot_nt(q, keys) * factor + bias[:, start:stop]
            if start == lo:
                s = jnp.where(causal, s, masked_score)
            p = jnp.exp2(s - level)
            ds = (p * (dot_nt(dy, vals) - delta)).astype(bf16)
            part = dot(ds, keys)
            dq = part if dq is None else dq + part
            dkv[start:stop, :D] += dot_t(ds, q)
            dkv[start:stop, D:] += dot_t(p.astype(bf16), dy)
        grad[lo : lo + blk, :D] = (dq * scale).astype(bf16)
    grad[:, D : 2 * D] = (dkv[:, :D] * scale).astype(bf16)
    grad[:, 2 * D :] = dkv[:, D:].astype(bf16)
    copies = []
    for t, (j, at, to, n) in enumerate(places):
        far = pl.ds(pl.multiple_of(base + at, n), n)
        cp = pltpu.make_async_copy(grad.at[pl.ds(to, n)], outs[j].at[far], sem.at[t])
        cp.start()
        copies.append(cp)
    for cp in copies:
        cp.wait()


def attend_back(scal, pieces, kept, dos, masks):
    micros, slots = len(pieces), len(dos)
    rows = dos[0].shape[0] // micros
    total = slots * rows
    hbm = pl.BlockSpec(memory_space=pl.ANY)
    return pl.pallas_call(
        functools.partial(attend_back_kernel, slots, masks, rows, 256, micros),
        out_shape=[jax.ShapeDtypeStruct((micros * rows, 3 * HEAD_DIM), bf16)] * slots,
        grid=(micros,),
        in_specs=[pl.BlockSpec(memory_space=pltpu.SMEM)] + [hbm] * ((micros + 1) * slots + 2 * micros),
        out_specs=[hbm] * slots,
        scratch_shapes=[
            pltpu.VMEM((total, 3 * HEAD_DIM), bf16),
            pltpu.VMEM((total, HEAD_DIM), bf16),
            pltpu.VMEM((total, HEAD_DIM), f32),
            pltpu.VMEM((total, 1), f32),
            pltpu.VMEM((total, 2 * HEAD_DIM), f32),
            pltpu.VMEM((total, 3 * HEAD_DIM), bf16),
            pltpu.SemaphoreType.DMA((2 * slots * len(masks) + 2,)),
        ],
        cost_estimate=pl.CostEstimate(
            flops=micros * total * total * HEAD_DIM * 10,
            bytes_accessed=micros * total * HEAD_DIM * 24,
            transcendentals=micros * total * total // 2,
        ),
        name="attend_back",
    )(scal, *[p for ps in pieces for p in ps], *[k for ks in kept for k in ks], *dos)


def mlp_back_kernel(n, *refs):
    grads, dw, gates, ups = refs[: 2 * n], refs[2 * n], refs[2 * n + 1 :][:n], refs[3 * n + 1 :][:n]
    tok, outs, tok_out = refs[4 * n + 1], refs[4 * n + 2 : 6 * n + 2], refs[6 * n + 2]
    w = dw[...]
    half = grads[0].shape[0]
    for i, x in enumerate(grads):
        m, t = i // 2, slice(i % 2 * half, (i % 2 + 1) * half)
        a = dot_nt(x[...], w)
        g, u = gates[m][t, :], ups[m][t, :]
        s = jax.nn.sigmoid(g)
        outs[m][t, :] = (a * u * s * (1.0 + g * (1.0 - s))).astype(bf16)
        outs[n + m][t, :] = (a * g * s).astype(bf16)
    tok_out[0] = tok[0]


def mlp_back(line, grads, down_weight, gates, ups):
    n = len(gates)
    half, width = grads[0].shape
    rows = 2 * half
    ff = down_weight.shape[0]
    t = min(ff, 256)
    tall = pl.BlockSpec((rows, t), lambda i: (0, i))
    smem = pl.BlockSpec(memory_space=pltpu.SMEM)
    full = jax.ShapeDtypeStruct((rows, ff), bf16)
    *out, line.token = pl.pallas_call(
        functools.partial(mlp_back_kernel, n),
        out_shape=[full] * (2 * n) + [jax.ShapeDtypeStruct((1,), jnp.int32)],
        grid=(ff // t,),
        in_specs=[pl.BlockSpec((half, width), lambda i: (0, 0))] * (2 * n)
        + [pl.BlockSpec((t, width), lambda i: (i, 0))]
        + [tall] * (2 * n)
        + [smem],
        out_specs=[tall] * (2 * n) + [smem],
        cost_estimate=pl.CostEstimate(
            flops=2 * n * rows * width * ff,
            bytes_accessed=2 * width * ff + n * (2 * rows * width + 12 * rows * ff),
            transcendentals=n * rows * ff,
        ),
        name="mlp_back",
    )(*grads, down_weight, *gates, *ups, line.token)
    return out[:n], out[n:]


def hidden_back_kernel(n, *refs):
    gate_grads, gw, up_grads, uw = refs[:n], refs[n], refs[n + 1 : 2 * n + 1], refs[2 * n + 1]
    tok, keep, send, tok_out = refs[2 * n + 2 :]
    g, u = gw[...], uw[...]
    half = keep.shape[1]
    for m in range(n):
        v = (dot_nt(gate_grads[m][...], g) + dot_nt(up_grads[m][...], u)).astype(bf16)
        keep[m] = v[:half, :]
        send[m] = v[half:, :]
    tok_out[0] = tok[0]


def hidden_back(line, gate_grads, gate_weight, up_grads, up_weight):
    n = len(gate_grads)
    rows, ff = gate_grads[0].shape
    width = gate_weight.shape[0]
    t = min(width, 256)
    all_ = pl.BlockSpec((rows, ff), lambda i: (0, 0), pipeline_mode=pl.Buffered(1))
    tile = pl.BlockSpec((t, ff), lambda i: (i, 0))
    smem = pl.BlockSpec(memory_space=pltpu.SMEM)
    half = jax.ShapeDtypeStruct((n, rows // 2, width), bf16)
    part = pl.BlockSpec((n, rows // 2, t), lambda i: (0, 0, i))
    keep, send, line.token = pl.pallas_call(
        functools.partial(hidden_back_kernel, n),
        out_shape=[half, half, jax.ShapeDtypeStruct((1,), jnp.int32)],
        grid=(width // t,),
        in_specs=[all_] * n + [tile] + [all_] * n + [tile, smem],
        out_specs=[part, part, smem],
        cost_estimate=pl.CostEstimate(
            flops=4 * n * rows * width * ff,
            bytes_accessed=4 * width * ff + n * (4 * rows * ff + 2 * rows * width),
            transcendentals=0,
        ),
        name="hidden_back",
    )(*gate_grads, gate_weight, *up_grads, up_weight, line.token)
    return keep, send


def turn_kernel(n, *refs):
    out, tok_out = refs[n + 1 :]
    at = 0
    for x in refs[:n]:
        out[:, at : at + x.shape[0]] = x[...].T
        at += x.shape[0]
    tok_out[0] = refs[n][0]


def turn(line, pieces, m=0, count=1):
    counts = [x.shape[0] // count for x in pieces]
    rows, cols = sum(counts), pieces[0].shape[1]
    t = min(cols, 512)
    smem = pl.BlockSpec(memory_space=pltpu.SMEM)
    out, line.token = pl.pallas_call(
        functools.partial(turn_kernel, len(pieces)),
        out_shape=[
            jax.ShapeDtypeStruct((cols, rows), pieces[0].dtype),
            jax.ShapeDtypeStruct((1,), jnp.int32),
        ],
        grid=(cols // t,),
        in_specs=[pl.BlockSpec((n, t), lambda i: (m, i)) for n in counts] + [smem],
        out_specs=[pl.BlockSpec((t, rows), lambda i: (i, 0)), smem],
        cost_estimate=pl.CostEstimate(flops=0, bytes_accessed=4 * rows * cols, transcendentals=0),
        name="turn",
    )(*pieces, line.token)
    return out


def gathered_attend(piece, pos, length):
    rows, local = piece.shape[0], piece.shape[1] // 3
    heads = local // HEAD_DIM
    q = piece[:, :local].reshape(rows, heads, HEAD_DIM)
    kv = lax.all_gather(piece[:, local:], SEQ, axis=0, tiled=True)
    n = kv.shape[0]
    k = kv[:, :local].reshape(n, heads, HEAD_DIM)
    v = kv[:, local:].reshape(n, heads, HEAD_DIM)
    base = jnp.arange(n // rows, dtype=jnp.int32) * rows
    own = pos - lax.axis_index(SEQ) * rows
    key_pos = (base[:, None] + own[None, :]).reshape(n)
    allowed = (key_pos[None, :] <= pos[:, None]) & (key_pos[None, :] < length)
    allowed = allowed[:, None, :]
    s = jnp.einsum(TO_KEYS, q, k, preferred_element_type=f32) * HEAD_DIM**-0.5
    s = jnp.where(allowed, s, masked_score)
    top = jnp.max(s, axis=-1, keepdims=True)
    w = jnp.where(allowed, jnp.exp(s - top), 0.0)
    mass = jnp.sum(w, axis=-1, keepdims=True)
    mixed = jnp.einsum(TO_ROWS, w.astype(bf16), v, preferred_element_type=f32) / mass
    return mixed.reshape(rows, local).astype(bf16), (q, k, v, allowed, mixed, top + jnp.log(mass))


def gathered_back(kept, dy):
    q, k, v, allowed, mixed, level = kept
    rows, heads, _ = q.shape
    n = k.shape[0]
    dy = dy.reshape(rows, heads, HEAD_DIM)
    scale = HEAD_DIM**-0.5
    delta = jnp.sum(dy.astype(f32) * mixed, axis=-1, keepdims=True)
    s = jnp.einsum(TO_KEYS, q, k, preferred_element_type=f32) * scale
    p = jnp.where(allowed, jnp.exp(s - level), 0.0)
    dp = jnp.einsum(TO_KEYS, dy, v, preferred_element_type=f32)
    ds = (p * (dp - delta)).astype(bf16)
    dq = jnp.einsum(TO_ROWS, ds, k, preferred_element_type=f32) * scale
    dk = jnp.einsum(TO_HEADS, ds, q, preferred_element_type=f32) * scale
    dv = jnp.einsum(TO_HEADS, p.astype(bf16), dy, preferred_element_type=f32)
    local = heads * HEAD_DIM
    dkv = jnp.concatenate([dk.reshape(n, local), dv.reshape(n, local)], axis=1).astype(bf16)
    dkv = lax.psum_scatter(dkv, SEQ, scatter_dimension=0, tiled=True)
    return jnp.concatenate([dq.reshape(rows, local).astype(bf16), dkv.astype(bf16)], axis=1)


class Line:
    def __init__(self, token):
        self.token = token
        self.waits = {}

    def add(self, *tasks):
        for t in tasks:
            self.waits[t] = next(t)[0]

    def mark(self, *arrays):
        for x in arrays:
            x = lax.slice(x, (0,) * x.ndim, (1,) * x.ndim).reshape(1)
            self.token = self.token + (x.astype(f32) > 3.4e38).astype(jnp.int32)

    def step(self, *tasks):
        tasks = [t for t in tasks if t in self.waits]
        if not tasks:
            return []
        held = [self.waits.pop(t) for t in tasks]
        if jax.tree.leaves(held):
            held, self.token = lax.optimization_barrier((held, self.token))
        for t, v in zip(tasks, held):
            try:
                self.waits[t], out = t.send(v)
            except StopIteration as end:
                out = end.value
            self.mark(*jax.tree.leaves(out)[:1])
        return [t for t in tasks if t in self.waits]


def idle(n):
    for _ in range(n):
        yield (), ()


class Place:
    def __init__(self, n_seq):
        self.n = n_seq
        self.dp, self.z = lax.axis_index(DP), lax.axis_index(SEQ)
        self.swap = [(0, 1), (1, 0)]
        self.lo, self.hi = n_seq // 2 - 1, n_seq // 2
        self.mid = [(self.lo, self.hi), (self.hi, self.lo)]
        self.inward = [
            [(i, i + 1), (n_seq - 1 - i, n_seq - 2 - i)] for i in range(n_seq // 2 - 1)
        ]

    def ends(self, pairs):
        return functools.reduce(jnp.logical_or, [self.z == b for _, b in pairs])


def take_half(x, dp, own):
    half = x.shape[1] // 2
    return lax.dynamic_slice_in_dim(x, (dp if own else 1 - dp) * half, half, 1)


def task_a(at, outs, which, x_send, x_keep, grad, cols, out_col):
    half = x_keep.shape[1]
    g = (yield grad, ())[:, cols]
    send = dot_t(x_send, g).astype(bf16)
    got = yield lax.ppermute(send, DP, at.swap), send
    s = (dot_t(x_keep, g) + got.astype(f32)).astype(bf16)
    for pairs in at.inward:
        got = yield lax.ppermute(s, SEQ, pairs), s
        s = add_low(s, got)
    got = yield lax.ppermute(s, SEQ, at.mid), s
    s = add_low(s, got)
    for pairs in reversed(at.inward):
        pairs = [(b, a) for a, b in pairs]
        got = yield lax.ppermute(s, SEQ, pairs), s
        s = jnp.where(at.ends(pairs), got, s)
    outs[which] = lax.dynamic_update_slice(outs[which], s.astype(f32), (at.dp * half, out_col))
    got = yield lax.ppermute(s, DP, at.swap), s
    outs[which] = lax.dynamic_update_slice(
        outs[which], got.astype(f32), ((1 - at.dp) * half, out_col)
    )
    return ()


def task_b(at, outs, which, x, grad, cols, out_col):
    g = (yield grad, ())[:, cols]
    s = dot_t(x, g).astype(bf16)
    for pairs in at.inward:
        got = yield lax.ppermute(s, SEQ, pairs), s
        s = add_low(s, got)
    h = s.shape[1] // 2
    first = at.z == at.lo
    send = jnp.where(first, s[:, h:], s[:, :h])
    keep = jnp.where(first, s[:, :h], s[:, h:])
    got = yield lax.ppermute(send, SEQ, at.mid), (send, keep)
    keep = add_low(keep, got)
    n = at.n
    pairs = [(d * n + k, (1 - d) * n + k) for d in (0, 1) for k in (at.lo, at.hi)]
    got = yield lax.ppermute(keep, (DP, SEQ), pairs), keep
    keep = add_low(keep, got)
    got = yield lax.ppermute(keep, SEQ, at.mid), keep
    s = jnp.concatenate([jnp.where(first, keep, got), jnp.where(first, got, keep)], axis=1)
    for pairs in reversed(at.inward):
        pairs = [(b, a) for a, b in pairs]
        got = yield lax.ppermute(s, SEQ, pairs), s
        s = jnp.where(at.ends(pairs), got, s)
    outs[which] = lax.dynamic_update_slice(outs[which], s.astype(f32), (0, out_col))
    return None


class Round:
    def __init__(self):
        self.refs, self.loads, self.keys = [], {}, {}

    def ref(self, array):
        for i, r in enumerate(self.refs):
            if r is array:
                return i
        self.refs.append(array)
        return len(self.refs) - 1

    def load(self, name, array, rows, cols=None):
        cols = (0, array.shape[1]) if cols is None else cols
        self.loads[name] = ((rows[1], cols[1]), ((self.ref(array), rows, cols, 0, 0),))

    def load_down(self, name, arrays, cols):
        n = arrays[0].shape[0]
        parts = tuple((self.ref(x), (0, n), cols, i * n, 0) for i, x in enumerate(arrays))
        self.loads[name] = ((n * len(arrays), cols[1]), parts)

    def load_across(self, name, arrays, rows):
        n = arrays[0].shape[1]
        parts = tuple((self.ref(x), rows, (0, n), 0, i * n) for i, x in enumerate(arrays))
        self.loads[name] = ((rows[1], n * len(arrays)), parts)


def first_row(first, count, dp):
    if isinstance(first, int):
        return first
    own, base = first
    return pl.multiple_of(base + (dp if own else 1 - dp) * count, count)


def round_kernel(kind, loads, n_in, pieces, extras, stores, scal, tok, *refs):
    ins = refs[:n_in]
    outs = refs[n_in + 1 : n_in + 1 + bool(pieces) + bool(extras) + len(stores)]
    refs[n_in][0] = tok[0]
    scratch = refs[n_in + 1 + len(outs) :]
    bufs = dict(zip([l[0] for l in loads], scratch))
    rest = list(scratch[len(loads) :])
    out_bufs = {}
    for name, _ in pieces + extras:
        out_bufs[name] = rest.pop(0)
    f_bufs = [rest.pop(0) for _ in stores]
    in_sem, out_sem = rest
    dp, z, n = scal[0], scal[1], scal[2]
    outer = (z == 0) | (z == n - 1)
    first = z == n // 2 - 1
    waits = {}
    t = 0
    for name, _, parts in loads:
        waits[name] = []
        for i, (r0, rows), (c0, cols), to_row, to_col in parts:
            src = ins[i].at[pl.ds(first_row(r0, rows, dp), rows), pl.ds(c0, cols)]
            dst = bufs[name].at[pl.ds(to_row, rows), pl.ds(to_col, cols)]
            cp = pltpu.make_async_copy(src, dst, in_sem.at[t])
            cp.start()
            waits[name].append(cp)
            t += 1

    def get(name):
        for cp in waits.pop(name, ()):
            cp.wait()
        return bufs[name]

    done = []
    slot = [0]

    def ship(src, dst):
        cp = pltpu.make_async_copy(src, dst, out_sem.at[slot[0]])
        slot[0] += 1
        cp.start()
        done.append(cp)

    where_out = {}
    k = 0
    for group in (pieces, extras):
        if group:
            at = 0
            for name, rows in group:
                where_out[name] = outs[k].at[pl.ds(at, rows)]
                at += rows
            k += 1

    def emit(name):
        if name in where_out:
            ship(out_bufs[name], where_out[name])

    def tiles(rows):
        t = min(rows, 256)
        return [slice(i, i + t) for i in range(0, rows, t)]

    have = lambda *names: all(n in bufs for n in names)
    low = lambda a, b: (a.astype(f32) + b.astype(f32)).astype(bf16)
    finals = {}
    if kind == "X":
        if have("a4r"):
            got, own, out = get("a4r"), get("a4o"), out_bufs["a4"]
            for t in tiles(out.shape[0]):
                out[t, :] = jnp.where(outer, got[t, :], own[t, :])
            emit("a4")
            finals["a4"] = out
        if have("b2r"):
            got, own, out = get("b2r"), get("b2o"), out_bufs["b2"]
            for t in tiles(out.shape[0]):
                out[t, :] = low(own[t, :], got[t, :])
            emit("b2")
        if have("a0g"):
            g, x, out = get("a0g"), get("a0x"), out_bufs["a0"]
            for t in tiles(out.shape[0]):
                out[t, :] = dot(x[t, :], g[...]).astype(bf16)
            emit("a0")
    if kind == "O":
        a_in, a_out = have("s1g"), have("s3r")
        if a_in:
            g, x, got, s1 = get("s1g"), get("s1x"), get("s1r"), out_bufs["s1"]
            for t in tiles(s1.shape[0]):
                s1[t, :] = (dot(x[t, :], g[...]) + got[t, :].astype(f32)).astype(bf16)
            emit("s1")
        if a_in or a_out:
            out = out_bufs["a"]
            n_in = s1.shape[0] if a_in else 0
            n_out = bufs["s3r"].shape[0] if a_out else 0
            if a_out:
                own, got = get("s3o"), get("s3r")
            for t in tiles(out.shape[0]):
                v = s1[t, :] if t.start < n_in else None
                if t.start < n_out:
                    u = low(own[t, :], got[t, :])
                    v = u if v is None else jnp.where(outer, v, u)
                out[t, :] = v
            emit("a")
        b_in, b_out = have("t0g"), have("t4r")
        if b_in:
            g, x, t0 = get("t0g"), get("t0x"), out_bufs["t0"]
            for t in tiles(t0.shape[0]):
                t0[t, :] = dot(x[t, :], g[...]).astype(bf16)
            emit("t0")
        if b_in or b_out:
            out = out_bufs["b"]
            n_in = t0.shape[0] if b_in else 0
            h = bufs["t4r"].shape[0] if b_out else 0
            if b_out:
                own, got = get("t4o"), get("t4r")
            for o in tiles(out.shape[0]):
                v = t0[o, :] if o.start < n_in else None
                if o.start < 2 * h:
                    back = h if o.start >= h else 0
                    t = slice(o.start - back, o.stop - back)
                    mine = jnp.logical_not(first) if back else first
                    u = jnp.where(mine, own[t, :], got[t, :])
                    v = u if v is None else jnp.where(outer, v, u)
                out[o, :] = v
            emit("b")
        if have("af"):
            finals["af"] = get("af")
    if kind == "M":
        if have("a2r"):
            own, got, out = get("a2o"), get("a2r"), out_bufs["a2"]
            for t in tiles(out.shape[0]):
                out[t, :] = low(own[t, :], got[t, :])
            emit("a2")
        if have("b3r"):
            own, got, out = get("b3o"), get("b3r"), out_bufs["b3"]
            for t in tiles(out.shape[0]):
                out[t, :] = low(own[t, :], got[t, :])
            emit("b3")
        if have("b1o"):
            own, got, out, keep = get("b1o"), get("ob"), out_bufs["b1"], out_bufs["keep"]
            h = out.shape[0]
            for t in tiles(h):
                o = slice(h + t.start, h + t.stop)
                top, bottom = low(own[t, :], got[t, :]), low(own[o, :], got[o, :])
                out[t, :] = jnp.where(first, bottom, top)
                keep[t, :] = jnp.where(first, top, bottom)
            emit("b1")
            emit("keep")
        if have("fino"):
            own, got = get("fino"), get("ob")
            finals["fin"] = (got, own)
    for i, (name, r0, rows, col) in enumerate(stores):
        src, buf = finals[name], f_bufs[i]
        for t in tiles(buf.shape[0]):
            if name == "fin":
                buf[t, :] = jnp.where(outer, src[0][t, :], src[1][t, :]).astype(f32)
            else:
                buf[t, :] = src[t, :].astype(f32)
        dst = outs[len(outs) - len(stores) + i]
        ship(buf, dst.at[pl.ds(first_row(r0, rows, dp), rows), pl.ds(col, buf.shape[1])])
    for cp in done:
        cp.wait()


class Rounds:
    def __init__(self, at, outs, line):
        self.at, self.outs, self.line = at, outs, line
        self.a, self.b = {}, {}
        self.got = {}
        self.r = 0
        self.swap_outer = [(0, 1), (1, 0), (2, 3), (3, 2)]
        self.scal = jnp.stack([at.dp, at.z, jnp.int32(at.n)]).astype(jnp.int32)

    def piece(self, kind, r, name, own=False, some=None):
        sent, got, table = self.got[kind, r]
        at = 0
        for k, rows in table:
            if k == name:
                return (sent if own else got), (at, rows if some is None else some)
            at += rows

    def run(self, kind, b, pieces, extras, stores, flops):
        rows = {n: r for n, r in pieces + extras}
        w = self.width
        loads = tuple((k,) + v for k, v in b.loads.items())
        any_ = pl.BlockSpec(memory_space=pl.ANY)
        smem = pl.BlockSpec(memory_space=pltpu.SMEM)
        shapes, aliases = [jax.ShapeDtypeStruct((1,), jnp.int32)], {}
        if pieces:
            shapes.append(jax.ShapeDtypeStruct((sum(r for _, r in pieces), w), bf16))
        if extras:
            shapes.append(jax.ShapeDtypeStruct((sum(r for _, r in extras), w), bf16))
        for which, *_ in stores:
            aliases[2 + len(b.refs) + len(aliases)] = len(shapes)
            shapes.append(jax.ShapeDtypeStruct(self.outs[which].shape, f32))
        scratch = [pltpu.VMEM(shape, bf16) for _, shape, _ in loads]
        scratch += [pltpu.VMEM((rows[n], w), bf16) for n, _ in pieces + extras]
        scratch += [pltpu.VMEM((r, w), f32) for _, _, _, r, _ in stores]
        n_out = len(pieces) + len(extras) + len(stores)
        n_load = sum(len(parts) for _, _, parts in loads)
        scratch += [pltpu.SemaphoreType.DMA((n_load,)), pltpu.SemaphoreType.DMA((n_out,))]
        moved = sum(m * n * 2 for _, (m, n), _ in loads) + sum(rows.values()) * w * 2
        moved += sum(r * w * 4 for _, _, _, r, _ in stores)
        n_in = len(b.refs) + len(stores)
        out = pl.pallas_call(
            functools.partial(
                round_kernel, kind, loads, n_in, tuple(pieces), tuple(extras),
                tuple(s[1:] for s in stores),
            ),
            out_shape=shapes,
            in_specs=[smem, smem] + [any_] * n_in,
            out_specs=[smem] + [any_] * (len(shapes) - 1),
            input_output_aliases=aliases,
            scratch_shapes=scratch,
            cost_estimate=pl.CostEstimate(flops=flops, bytes_accessed=moved, transcendentals=0),
            name="round_" + kind.lower(),
        )(self.scal, self.line.token, *b.refs, *[self.outs[s[0]] for s in stores])
        self.line.token, *out = out
        for which, *_ in reversed(stores):
            self.outs[which] = out.pop()
        extra = out.pop() if extras else None
        if pieces:
            axis, pairs = {
                "X": (DP, self.at.swap), "O": (SEQ, self.swap_outer), "M": (SEQ, self.at.mid),
            }[kind]
            self.got[kind, self.r] = (out[0], lax.ppermute(out[0], axis, pairs), pieces)
        return extra

    def step_x(self):
        r, A, B = self.r, self.a, self.b
        b, pieces, stores, flops = Round(), [], [], 0
        if r in A:
            c = A[r]
            half, tok = c["rows"][1] // 2, sum(x.shape[1] for x in c["x"])
            b.load_down("a0g", c["grad"], c["cols"])
            b.load_across("a0x", c["x"], ((False, c["rows"][0]), half))
            pieces.append(("a0", half))
            flops += 2 * half * tok * c["cols"][1]
        if r - 6 in A:
            c = A[r - 6]
            rows = c["rows"][1] // 2
            b.load("a4r", *self.piece("O", r - 2, "a", False, rows))
            b.load("a4o", *self.piece("O", r - 2, "a", True, rows))
            pieces.append(("a4", rows))
            stores.append((c["which"], "a4", (True, c["rows"][0]), rows, c["col"]))
        if r - 3 in B:
            c = B[r - 3]
            b.load("b2r", *self.piece("M", r - 2, "b1"))
            b.load("b2o", *c["keep"])
            pieces.append(("b2", b.loads["b2r"][0][0]))
        if pieces:
            self.run("X", b, pieces, [], stores, flops)

    def step_o(self):
        r, A, B = self.r, self.a, self.b
        b, pieces, extras, stores, flops = Round(), [], [], [], 0
        if r - 1 in A:
            c = A[r - 1]
            half, tok = c["rows"][1] // 2, sum(x.shape[1] for x in c["x"])
            b.load_down("s1g", c["grad"], c["cols"])
            b.load_across("s1x", c["x"], ((True, c["rows"][0]), half))
            b.load("s1r", *self.piece("X", r - 1, "a0"))
            extras.append(("s1", half))
            flops += 2 * half * tok * c["cols"][1]
        if r - 4 in A:
            b.load("s3o", *self.piece("M", r - 2, "a2", True))
            b.load("s3r", *self.piece("M", r - 2, "a2"))
        if r - 1 in A or r - 4 in A:
            sizes = [A[k]["rows"][1] // 2 for k in (r - 1, r - 4) if k in A]
            pieces.append(("a", max(sizes)))
        if r in B:
            c = B[r]
            rows, tok = c["rows"][1], sum(x.shape[1] for x in c["x"])
            b.load_down("t0g", c["grad"], c["cols"])
            b.load_across("t0x", c["x"], c["rows"])
            extras.append(("t0", rows))
            flops += 2 * rows * tok * c["cols"][1]
        if r - 6 in B:
            b.load("t4o", *self.piece("M", r - 2, "b3", True))
            b.load("t4r", *self.piece("M", r - 2, "b3"))
        if r in B or r - 6 in B:
            pieces.append(("b", max(B[k]["rows"][1] for k in (r, r - 6) if k in B)))
        if r - 7 in A:
            c = A.pop(r - 7)
            b.load("af", *self.piece("X", r - 1, "a4"))
            first = (False, c["rows"][0])
            stores.append((c["which"], "af", first, b.loads["af"][0][0], c["col"]))
        if pieces or stores:
            extra = self.run("O", b, pieces, extras, stores, flops)
            at = 0
            for name, n in extras:
                (A[r - 1] if name == "s1" else B[r])[name] = (extra, (at, n))
                at += n

    def step_m(self):
        r, A, B = self.r, self.a, self.b
        b, pieces, extras, stores = Round(), [], [], []
        if r - 2 in A:
            rows = A[r - 2]["rows"][1] // 2
            b.load("a2o", *A[r - 2]["s1"])
            b.load("a2r", *self.piece("O", r - 1, "a", False, rows))
            pieces.append(("a2", rows))
        if r - 1 in B or r - 7 in B:
            b.load("ob", *self.piece("O", r - 1, "b"))
        if r - 1 in B:
            h = B[r - 1]["rows"][1] // 2
            b.load("b1o", *B[r - 1]["t0"])
            pieces.append(("b1", h))
            extras.append(("keep", h))
        if r - 4 in B:
            b.load("b3o", *self.piece("X", r - 1, "b2", True))
            b.load("b3r", *self.piece("X", r - 1, "b2"))
            pieces.append(("b3", b.loads["b3r"][0][0]))
        if r - 7 in B:
            c = B.pop(r - 7)
            b.load("fino", *self.piece("O", r - 1, "b", True, c["rows"][1]))
            stores.append((c["which"], "fin", c["rows"][0], c["rows"][1], c["col"]))
        if pieces or stores:
            extra = self.run("M", b, pieces, extras, stores, 0)
            if extras:
                B[r - 1]["keep"] = (extra, (0, h))


def blank_kernel(*outs):
    pass


def blanks(shapes):
    return pl.pallas_call(
        blank_kernel,
        out_shape=[jax.ShapeDtypeStruct(s, f32) for s in shapes],
        out_specs=[pl.BlockSpec(memory_space=pl.ANY)] * len(shapes),
    )()


def gather_steps(x, n, axis=0, wait=0):
    got = None
    for b in reversed(bits_of(n)):
        if got is not None:
            x = jnp.concatenate([x, got], axis=axis)
        got = lax.ppermute(x, MP, xor_perm(n, b))
        if wait:
            yield (), x
            yield from idle(wait - 1)
            got = yield got, ()
        else:
            got = yield got, x
    return [x, got]


def joined(pieces, axis=0):
    return jnp.concatenate(pieces, axis=axis)


def scatter_steps(x, n, axis=0, wait=0):
    for b in bits_of(n):
        if isinstance(x, tuple):
            keep, send = x
        else:
            half = x.shape[axis] // 2
            keep = lax.slice_in_dim(x, 0, half, axis=axis)
            send = lax.slice_in_dim(x, half, 2 * half, axis=axis)
        got = lax.ppermute(send, MP, xor_perm(n, b))
        if wait:
            yield (), (send, keep)
            yield from idle(wait - 1)
            got = yield got, ()
        else:
            got = yield got, (send, keep)
        x = keep.astype(f32) + got.astype(f32)
        if 2 * b < n:
            x = x.astype(bf16)
    return x.astype(f32)


def sum_rows_steps(x, n):
    masks = row_masks(n)
    for b in bits_of(n):
        got = yield lax.ppermute(x, MP, xor_perm(n, b)), x
        got = got.reshape(x.shape[:-1] + (n, -1))
        order = [masks.index(m ^ b) for m in masks]
        got = jnp.stack([got[..., k, :] for k in order], axis=-2)
        x = x + got.reshape(x.shape)
    return x


def exchange_steps(pieces, n):
    got = yield exchange(pieces, n)[1:], pieces[1:]
    return [pieces[0]] + list(got)


class Layer:
    pass


def forward_task(c, m):
    f = c.fwd[m]
    own = c.tokens[m]
    length = c.lengths[m, 0]
    x = f.x = yield from gather_steps(own, c.n_mp)
    proj = dot(joined(x), c.qkv_weight)
    local = c.local
    squares = jnp.stack(
        [jnp.sum(jnp.square(proj[:, t * local : (t + 1) * local]), axis=1) for t in (0, 1)], axis=0
    )
    squares = yield from sum_rows_steps(squares, c.n_mp)
    inv = lax.rsqrt(squares / c.width + epsilon).T
    pieces = rope_call(c.slots, c.z_arr, proj, inv, c.cos, c.sin, c.qg, c.kg)
    if c.by_heads:
        scal = jnp.stack([c.z, c.me, length]).astype(jnp.int32)
        f.pieces = yield from exchange_steps(pieces, c.n_seq)
        mixed, f.kept = attend(scal, f.pieces, c.masks)
        mixed = yield from exchange_steps(mixed, c.n_seq)
        mixed = join_heads(c.z_arr, mixed)
    else:
        mixed, f.kept = gathered_attend(pieces[0], c.pos, length)
    attended = yield from scatter_steps(dot(mixed, c.o_weight).astype(bf16), c.n_mp)
    attn_inv = inv_rms(attended)
    hidden = own.astype(f32) + attended * attn_inv * c.attn_gain
    mlp_in = yield from gather_steps(hidden.astype(bf16), c.n_mp)
    f.mlp_in = mlp_in
    rows_in = joined(mlp_in)
    f.gate, f.up = dot(rows_in, c.gate_weight), dot(rows_in, c.up_weight)
    f.act = (f.gate * jax.nn.sigmoid(f.gate) * f.up).astype(bf16)
    mlp_out = yield from scatter_steps(dot(f.act, c.down_weight).astype(bf16), c.n_mp)
    mlp_inv = inv_rms(mlp_out)
    f.layer = (hidden + mlp_out * mlp_inv * c.mlp_gain).astype(bf16)
    f.seeds = c.cotangent[m].astype(f32) * (c.own_pos < length).astype(f32)[:, None]
    mlp_grad, gain_rows = norm_backward(mlp_out, mlp_inv, c.mlp_gain, f.seeds)
    f.mlp_gain = jnp.sum(gain_rows, axis=0)
    f.mlp_grad = yield from gather_steps(mlp_grad.astype(bf16), c.n_mp)
    f.proj, f.inv, f.mixed, f.attended, f.attn_inv = proj, inv, mixed, attended, attn_inv
    return ()


def backward_task(c):
    n, rows, fwd = len(c.fwd), c.rows, c.fwd
    yield (), ()
    gates = mlp_back(
        c.line, [x for f in fwd for x in f.mlp_grad], c.down_weight, [f.gate for f in fwd], [f.up for f in fwd]
    )
    for f, f.gate_grad, f.up_grad in zip(fwd, *gates):
        pass
    yield (), ()
    back = hidden_back(c.line, gates[0], c.gate_weight, gates[1], c.up_weight)
    back = yield from scatter_steps(back, c.n_mp, 1, c.far)
    hidden_grad, attn_grad = [], []
    for m, f in enumerate(fwd):
        hidden_grad.append(f.seeds + back[m])
        e, gain_rows = norm_backward(f.attended, f.attn_inv, c.attn_gain, hidden_grad[m])
        f.attn_gain = jnp.sum(gain_rows, axis=0)
        attn_grad.append(e.astype(bf16))
    attn_grad = yield from gather_steps(jnp.stack(attn_grad), c.n_mp, 1, c.far)
    c.attn_grad = [x.reshape(-1, c.width) for x in attn_grad]
    dy = [dot_nt(x, c.o_weight).astype(bf16).reshape(n, -1, c.local) for x in c.attn_grad]
    dy = joined(dy, 1).reshape(n * rows, c.local)
    if not c.rounds:
        c.attn_grad_all = joined(attn_grad, 1).reshape(n * rows, c.width)
    if c.by_heads:
        dys = split_heads(c.z_arr, dy, c.slots)
        dys = yield from exchange_steps(dys, c.n_seq)
        scal = jnp.concatenate([jnp.stack([c.z, c.me]), c.lengths[:, 0]]).astype(jnp.int32)
        grads = attend_back(scal, [f.pieces for f in fwd], [f.kept for f in fwd], dys, c.masks)
        grads = yield from exchange_steps(grads, c.n_seq)
    else:
        grads = [gathered_back(f.kept, dy[m * rows : (m + 1) * rows]) for m, f in enumerate(fwd)]
        grads = [jnp.concatenate(grads, axis=0)]
    tables = (c.cos, c.sin, c.qg, c.kg)
    cross = []
    for m, f in enumerate(fwd):
        e, f.gains = cross_call(c.slots, m, c.z_arr, grads, f.proj, f.inv, *tables)
        cross.append(e.T)
    cross = yield from sum_rows_steps(jnp.concatenate(cross, axis=0), c.n_mp)
    for m, f in enumerate(fwd):
        e = cross[2 * m : 2 * m + 2].T
        f.qkv_grad = raw_call(
            c.slots, c.width, m, c.z_arr, grads, f.proj, f.inv, e, *tables
        )
    yield (), [f.qkv_grad for f in fwd]
    back = jnp.stack([dot_nt(f.qkv_grad, c.qkv_weight).astype(bf16) for f in fwd])
    back = yield from scatter_steps(back, c.n_mp, 1, c.far)
    c.input_grad = jnp.stack(hidden_grad) + back
    return c.input_grad


def turning_task(c):
    yield (), ()
    c.attn_grad_t = []
    for m in range(len(c.fwd)):
        c.attn_grad_t.append(turn(c.line, c.attn_grad, m, len(c.fwd)))
        yield (), ()


def gains_task(c):
    yield (), ()
    gains = sum(f.gains for f in c.fwd)
    gains = lax.dynamic_update_slice(jnp.zeros((2, c.width), f32), gains, (0, c.me * c.local))
    gains = jnp.concatenate(
        [gains, sum(f.attn_gain for f in c.fwd)[None], sum(f.mlp_gain for f in c.fwd)[None]], axis=0
    )
    for name, n in ((MP, c.n_mp), (SEQ, c.n_seq), (DP, c.n_dp)):
        for b in bits_of(n):
            got = lax.ppermute(gains, name, xor_perm(n, b))
            got = yield got, gains
            gains = gains + got
    c.gains = gains
    return gains


def per_device(
    n_dp, n_seq, n_mp,
    tokens, lengths, cotangent, q_weight, k_weight, v_weight, o_weight, q_gain, k_gain,
    attn_gain, gate_weight, up_weight, down_weight, mlp_gain,
):
    c = Layer()
    micros, own_rows, width = tokens.shape
    rows = own_rows * n_mp
    local = q_weight.shape[1]
    heads = local // HEAD_DIM
    ff = gate_weight.shape[1]
    me, z = lax.axis_index(MP), lax.axis_index(SEQ)
    c.tokens, c.lengths, c.cotangent, c.o_weight = tokens, lengths, cotangent, o_weight
    c.gate_weight, c.up_weight, c.down_weight = gate_weight, up_weight, down_weight
    c.attn_gain, c.mlp_gain = attn_gain, mlp_gain
    c.n_dp, c.n_seq, c.n_mp, c.rows, c.width, c.local = n_dp, n_seq, n_mp, rows, width, local
    c.me, c.z, c.masks = me, z, row_masks(n_mp)
    c.by_heads = heads == n_seq
    c.slots = n_seq if c.by_heads else 1
    c.z_arr = z.astype(jnp.int32).reshape(1)
    c.qkv_weight = jnp.concatenate([q_weight, k_weight, v_weight], axis=1)
    c.qg = lax.dynamic_slice_in_dim(q_gain, me * local, local)[None]
    c.kg = lax.dynamic_slice_in_dim(k_gain, me * local, local)[None]
    block = jnp.asarray(c.masks, jnp.int32) ^ me
    steps = jnp.arange(own_rows, dtype=jnp.int32)
    c.pos = z * rows + (block[:, None] * own_rows + steps).reshape(-1)
    c.own_pos = z * rows + me * own_rows + steps
    frequency = rope_base ** (-(jnp.arange(HALF, dtype=f32) * 2.0 / HEAD_DIM))
    angles = c.pos.astype(f32)[:, None] * frequency[None, :]
    cos, sin = jnp.cos(angles), jnp.sin(angles)
    c.cos = jnp.concatenate([cos, cos], axis=1)
    c.sin = jnp.concatenate([-sin, sin], axis=1)
    c.fwd = [Layer() for _ in range(micros)]

    at = Place(n_seq)
    c.rounds = rounds = n_seq == 4
    line = c.line = Line(jnp.zeros((1,), jnp.int32))
    fw = [forward_task(c, m) for m in range(micros)]
    line.add(*fw)
    def turned(m, name):
        f = c.fwd[m]
        rows_ = getattr(f, name)
        setattr(f, name + "_t", turn(line, rows_ if isinstance(rows_, list) else [rows_]))

    extra = {"a": (0, "x"), "b": (1, "x"), "c": (0, "act"), "d": (1, "act"), "e": (0, "mlp_in"), "f": (1, "mlp_in")}
    order = ORDER if (micros, n_mp, c.by_heads) == (2, 4, True) and rounds else ""
    for act in order:
        if act in extra:
            turned(*extra[act])
        else:
            line.step(fw[int(act)])
    while any(t in line.waits for t in fw):
        for t in fw:
            line.step(t)

    c.far = 0
    each = lambda name: [getattr(f, name) for f in c.fwd]
    outs = list(blanks(
        [(ff, width), (width, ff), (width, ff)]
        + [(width, local)] * 3
        + [(width, local) if rounds else (local, width)]
    ))
    back, gains = backward_task(c), gains_task(c)
    side = []
    line.add(back)

    stack = lambda lists: [x for pieces in lists for x in pieces]
    both = lambda name: jnp.concatenate(each(name), axis=0)
    both2 = lambda name: jnp.concatenate(stack(each(name)), axis=0)

    def work(key):
        if rounds:
            return {
                "down": lambda: (each("act_t"), stack(each("mlp_grad"))),
                "gate": lambda: (each("mlp_in_t"), each("gate_grad")),
                "up": lambda: (each("mlp_in_t"), each("up_grad")),
                "o": lambda: (c.attn_grad_t, each("mixed")),
                "qkv": lambda: (each("x_t"), each("qkv_grad")),
            }[key]()
        return {
            "down": lambda: (both("act"), both2("mlp_grad")),
            "gate": lambda: (both2("mlp_in"), both("gate_grad")),
            "up": lambda: (both2("mlp_in"), both("up_grad")),
            "o": lambda: (both("mixed"), c.attn_grad_all),
            "qkv": lambda: (both2("x"), both("qkv_grad")),
        }[key]()

    done, live = {}, []
    if rounds:
        reducer = Rounds(at, outs, line)
        reducer.width = local // 2

    def rows_of(key):
        if key not in done:
            done[key] = work(key)
        return done[key]

    def one_round(new_a, new_b, script=""):
        if rounds:
            for new, table in ((new_a, reducer.a), (new_b, reducer.b)):
                if new is not None:
                    key, which, first, n, col, span = new
                    x, grad = rows_of(key)
                    table[reducer.r] = dict(
                        x=x, grad=grad, cols=(first, n), which=which, col=col, rows=span
                    )
            for act in script:
                if act in "XOM":
                    getattr(reducer, "step_" + act.lower())()
                else:
                    line.step({"c": back, "t": turning, "g": gains}[act])
            reducer.r += 1
            return
        for new, kind in ((new_a, "a"), (new_b, "b")):
            if new is not None:
                key, which, first, n, col, _ = new
                x, grad = rows_of(key)
                if kind == "a":
                    if key + "/" not in done:
                        done[key + "/"] = (take_half(x, at.dp, False), take_half(x, at.dp, True))
                    t = task_a(at, outs, which, *done[key + "/"], grad, slice(first, first + n), col)
                else:
                    t = task_b(at, outs, which, x, grad, slice(first, first + n), col)
                line.add(t)
                live.append(t)
        live[:] = line.step(*live)
        for t in side:
            line.step(t)

    unit = local // 2
    cut = lambda key, which, n, u=unit, first=0, parts=1: [
        (key, which, first + t, u, t, (k * (width // parts), width // parts))
        for t in range(0, n, u)
        for k in range(parts)
    ]
    ready = {
        "down": lambda: True,
        "gate": lambda: all(hasattr(f, "up_grad") for f in c.fwd),
        "o": lambda: len(c.attn_grad_t) == micros if rounds else hasattr(c, "attn_grad_all"),
        "qkv": lambda: all(hasattr(f, "qkv_grad") for f in c.fwd),
    }
    ready["up"] = ready["gate"]
    todo = cut("down", 0, width) + cut("gate", 1, ff) + cut("up", 2, ff)
    todo += cut("o", 6, local) if rounds else cut("o", 6, width, width // 2)
    for t in range(3):
        todo += cut("qkv", 3 + t, local, first=t * local, parts=2 if rounds and t else 1)
    c.attn_grad_t = []
    if rounds:
        for m in range(micros):
            for name in ("x", "act", "mlp_in"):
                if not hasattr(c.fwd[m], name + "_t"):
                    turned(m, name)
        turning = turning_task(c)
        line.add(turning)
    else:
        side = [back]
    count_a = len(todo) // 2

    def take():
        for i, chunk in enumerate(todo):
            if ready[chunk[0]]():
                return todo.pop(i)
        return None

    gains_on = False
    r = taken_a = 0
    while todo or any(t in line.waits for t in (back, gains)) or (
        reducer.a or reducer.b if rounds else live
    ):
        late = ready["qkv"]()
        if late and not gains_on and not (rounds and todo):
            gains_on = True
            side.append(gains)
            line.add(gains)
        new_a = take() if taken_a < count_a else None
        taken_a += new_a is not None
        script = SCRIPT[r] if r < len(SCRIPT) else "XgOcMg"
        lone = rounds and r < len(SCRIPT) and script[-1:] == "-"
        new_b = None if lone else take()
        one_round(new_a, new_b, script.strip("-") if rounds else "")
        r += 1
    return (
        jnp.stack(each("layer")),
        c.input_grad,
        outs[3],
        outs[4],
        outs[5],
        outs[6].T if rounds else outs[6],
        c.gains[0],
        c.gains[1],
        c.gains[2],
        outs[1],
        outs[2],
        outs[0],
        c.gains[3],
    )


SCRIPT = (
    "XOc",
    "XcOM",
    "XcOM",
    "XcOM",
    "XOcM",
    "XOcM",
    "XOMc",
    "XOtMtc",
    "XOcM",
    "XcOMc",
    "XOMc",
)

ORDER = "00001111ab00010101010ce1101d0f1011"


def solution(mesh):
    n_dp, n_seq, n_mp = (mesh.shape[a] for a in (DP, SEQ, MP))
    assert n_dp == 2
    rows = P(None, (DP, SEQ, MP), None)
    cols, flat, all_ = P(None, MP), P(MP, None), P()
    return jax.shard_map(
        functools.partial(per_device, n_dp, n_seq, n_mp),
        mesh=mesh,
        in_specs=(rows, P(None, DP), rows, cols, cols, cols, flat, all_, all_, all_, cols, cols, flat, all_),
        out_specs=(rows, rows, cols, cols, cols, flat, all_, all_, all_, cols, cols, flat, all_),
        check_vma=False,
    )
```

```python
import functools

import jax
import jax.numpy as jnp
from jax import lax
from jax.experimental import pallas as pl
from jax.experimental.pallas import tpu as pltpu
from jax.sharding import PartitionSpec as P

HEAD_DIM = 128
HALF = HEAD_DIM // 2
DP, SEQ, MP = "dp", "seq", "mp"
TO_KEYS, TO_ROWS, TO_HEADS = "shd,khd->shk", "shk,khd->shd", "shk,shd->khd"
epsilon = 1e-06
rope_base = 500000.0
masked_score = -1e30
LOG2E = 1.4426950408889634

f32 = jnp.float32
bf16 = jnp.bfloat16


def add_low(a, b):
    return (a.astype(f32) + b.astype(f32)).astype(bf16)


def bits_of(n):
    out = []
    b = 1
    while b < n:
        out.append(b)
        b *= 2
    return out


def xor_perm(n, b):
    return [(i, i ^ b) for i in range(n)]


def row_masks(n):
    masks = [0]
    for b in reversed(bits_of(n)):
        masks = masks + [m | b for m in masks]
    return masks


def inv_rms(v):
    return lax.rsqrt(jnp.mean(v * v, axis=-1, keepdims=True) + epsilon)


def norm_backward(source, inverse, gain_vec, upstream):
    normed = source * inverse
    weighted = upstream * gain_vec
    back = inverse * (weighted - normed * jnp.mean(weighted * normed, axis=-1, keepdims=True))
    return back, upstream * normed


def dot_t(a, b):
    return lax.dot_general(a, b, (((0,), (0,)), ((), ())), preferred_element_type=f32)


def dot_nt(a, b):
    return lax.dot_general(a, b, (((1,), (1,)), ((), ())), preferred_element_type=f32)


def dot(a, b):
    return jnp.dot(a, b, preferred_element_type=f32)


def rope_kernel(slots, width, local, z_ref, proj, inv, cos, sin, qg, kg, *outs):
    z = z_ref[0]
    c, s = cos[...], sin[...]
    for j in range(slots):
        base = (z ^ j) * width if slots > 1 else 0
        for h in range(width // HEAD_DIM):
            at = base + h * HEAD_DIM
            at = pl.multiple_of(at, HEAD_DIM) if slots > 1 else at
            for part, gain in ((0, qg), (1, kg)):
                raw = proj[:, pl.ds(part * local + at, HEAD_DIM)]
                v = raw * inv[:, part : part + 1] * gain[:, pl.ds(at, HEAD_DIM)]
                v = v * c + pltpu.roll(v, HALF, 1) * s
                lo = part * width + h * HEAD_DIM
                outs[j][:, lo : lo + HEAD_DIM] = v.astype(bf16)
            lo = 2 * width + h * HEAD_DIM
            outs[j][:, lo : lo + HEAD_DIM] = proj[:, pl.ds(2 * local + at, HEAD_DIM)].astype(bf16)


def rope_call(slots, z, proj, inv, cos, sin, qg, kg):
    rows, local = proj.shape[0], proj.shape[1] // 3
    width = local // slots
    blk = min(rows, 256)
    row = lambda n: pl.BlockSpec((blk, n), lambda i, *_: (i, 0))
    vec = pl.BlockSpec((1, local), lambda i, *_: (0, 0))
    return pl.pallas_call(
        functools.partial(rope_kernel, slots, width, local),
        out_shape=[jax.ShapeDtypeStruct((rows, 3 * width), bf16)] * slots,
        grid_spec=pltpu.PrefetchScalarGridSpec(
            num_scalar_prefetch=1,
            grid=(rows // blk,),
            in_specs=[row(3 * local), row(2), row(HEAD_DIM), row(HEAD_DIM), vec, vec],
            out_specs=[row(3 * width)] * slots,
        ),
        cost_estimate=pl.CostEstimate(
            flops=rows * local * 12, bytes_accessed=rows * local * 18, transcendentals=0
        ),
    )(z, proj, inv, cos, sin, qg, kg)


def unrope(grad, c, s):
    g = grad.astype(f32)
    return g * c - pltpu.roll(g, HALF, 1) * s


def cross_kernel(slots, width, local, z_ref, *refs):
    grads = refs[:slots]
    proj, inv, cos, sin, qg, kg, cross, gains = refs[slots:]
    z = z_ref[0]
    c, s = cos[...], sin[...]

    @pl.when(pl.program_id(0) == 0)
    def _():
        gains[...] = jnp.zeros_like(gains)

    for part, gain in ((0, qg), (1, kg)):
        total = None
        for j in range(slots):
            base = (z ^ j) * width if slots > 1 else 0
            for h in range(width // HEAD_DIM):
                at = base + h * HEAD_DIM
                at = pl.multiple_of(at, HEAD_DIM) if slots > 1 else at
                lo = part * width + h * HEAD_DIM
                g = unrope(grads[j][:, lo : lo + HEAD_DIM], c, s)
                gr = g * proj[:, pl.ds(part * local + at, HEAD_DIM)]
                w = gr * gain[:, pl.ds(at, HEAD_DIM)]
                total = w if total is None else total + w
                col = jnp.sum(gr * inv[:, part : part + 1], axis=0, keepdims=True)
                gains[part : part + 1, pl.ds(at, HEAD_DIM)] += col
        cross[:, part : part + 1] = jnp.sum(total, axis=1, keepdims=True)


def raw_kernel(slots, width, local, d, z_ref, *refs):
    grads = refs[:slots]
    proj, inv, cross, cos, sin, qg, kg, out = refs[slots:]
    z = z_ref[0]
    c, s = cos[...], sin[...]
    for j in range(slots):
        base = (z ^ j) * width if slots > 1 else 0
        for h in range(width // HEAD_DIM):
            at = base + h * HEAD_DIM
            at = pl.multiple_of(at, HEAD_DIM) if slots > 1 else at
            for part, gain in ((0, qg), (1, kg)):
                lo = part * width + h * HEAD_DIM
                g = unrope(grads[j][:, lo : lo + HEAD_DIM], c, s)
                r = inv[:, part : part + 1]
                w = g * gain[:, pl.ds(at, HEAD_DIM)] * r
                k = r * r * r * (cross[:, part : part + 1] * (1.0 / d))
                w = w - proj[:, pl.ds(part * local + at, HEAD_DIM)] * k
                out[:, pl.ds(part * local + at, HEAD_DIM)] = w.astype(bf16)
            lo = 2 * width + h * HEAD_DIM
            out[:, pl.ds(2 * local + at, HEAD_DIM)] = grads[j][:, lo : lo + HEAD_DIM]


def cross_call(slots, m, z, grads, proj, inv, cos, sin, qg, kg):
    rows, local = proj.shape[0], proj.shape[1] // 3
    width = local // slots
    blk = min(rows, 256)
    far = lambda n: pl.BlockSpec((blk, n), lambda i, *_: (i + m * (rows // blk), 0))
    row = lambda n: pl.BlockSpec((blk, n), lambda i, *_: (i, 0))
    vec = pl.BlockSpec((1, local), lambda i, *_: (0, 0))
    return pl.pallas_call(
        functools.partial(cross_kernel, slots, width, local),
        out_shape=[
            jax.ShapeDtypeStruct((rows, 2), f32),
            jax.ShapeDtypeStruct((2, local), f32),
        ],
        grid_spec=pltpu.PrefetchScalarGridSpec(
            num_scalar_prefetch=1,
            grid=(rows // blk,),
            in_specs=[far(3 * width)] * slots
            + [row(3 * local), row(2), row(HEAD_DIM), row(HEAD_DIM), vec, vec],
            out_specs=[row(2), pl.BlockSpec((2, local), lambda i, *_: (0, 0))],
        ),
        cost_estimate=pl.CostEstimate(
            flops=rows * local * 20, bytes_accessed=rows * local * 18, transcendentals=0
        ),
    )(z, *grads, proj, inv, cos, sin, qg, kg)


def raw_call(slots, d, m, z, grads, proj, inv, cross, cos, sin, qg, kg):
    rows, local = proj.shape[0], proj.shape[1] // 3
    width = local // slots
    blk = min(rows, 256)
    far = lambda n: pl.BlockSpec((blk, n), lambda i, *_: (i + m * (rows // blk), 0))
    row = lambda n: pl.BlockSpec((blk, n), lambda i, *_: (i, 0))
    vec = pl.BlockSpec((1, local), lambda i, *_: (0, 0))
    return pl.pallas_call(
        functools.partial(raw_kernel, slots, width, local, d),
        out_shape=jax.ShapeDtypeStruct((rows, 3 * local), bf16),
        grid_spec=pltpu.PrefetchScalarGridSpec(
            num_scalar_prefetch=1,
            grid=(rows // blk,),
            in_specs=[far(3 * width)] * slots
            + [row(3 * local), row(2), row(2), row(HEAD_DIM), row(HEAD_DIM), vec, vec],
            out_specs=row(3 * local),
        ),
        cost_estimate=pl.CostEstimate(
            flops=rows * local * 20, bytes_accessed=rows * local * 24, transcendentals=0
        ),
    )(z, *grads, proj, inv, cross, cos, sin, qg, kg)


def join_kernel(slots, width, z_ref, *refs):
    z = z_ref[0]
    out = refs[slots]
    for j in range(slots):
        out[:, pl.ds(pl.multiple_of((z ^ j) * width, HEAD_DIM), width)] = refs[j][...]


def join_heads(z, pieces):
    rows, width = pieces[0].shape
    slots = len(pieces)
    blk = min(rows, 256)
    return pl.pallas_call(
        functools.partial(join_kernel, slots, width),
        out_shape=jax.ShapeDtypeStruct((rows, slots * width), bf16),
        grid_spec=pltpu.PrefetchScalarGridSpec(
            num_scalar_prefetch=1,
            grid=(rows // blk,),
            in_specs=[pl.BlockSpec((blk, width), lambda i, *_: (i, 0))] * slots,
            out_specs=pl.BlockSpec((blk, slots * width), lambda i, *_: (i, 0)),
        ),
    )(z, *pieces)


def split_kernel(slots, width, z_ref, x, *outs):
    z = z_ref[0]
    for j in range(slots):
        outs[j][...] = x[:, pl.ds(pl.multiple_of((z ^ j) * width, HEAD_DIM), width)]


def split_heads(z, x, slots):
    rows, local = x.shape
    width = local // slots
    blk = min(rows, 256)
    return pl.pallas_call(
        functools.partial(split_kernel, slots, width),
        out_shape=[jax.ShapeDtypeStruct((rows, width), bf16)] * slots,
        grid_spec=pltpu.PrefetchScalarGridSpec(
            num_scalar_prefetch=1,
            grid=(rows // blk,),
            in_specs=[pl.BlockSpec((blk, local), lambda i, *_: (i, 0))],
            out_specs=[pl.BlockSpec((blk, width), lambda i, *_: (i, 0))] * slots,
        ),
    )(z, x)


def exchange(pieces, n):
    return [p if j == 0 else lax.ppermute(p, SEQ, xor_perm(n, j)) for j, p in enumerate(pieces)]


def row_places(slots, masks, rows, z, me):
    count = rows // len(masks)
    for j in range(slots):
        for k, m in enumerate(masks):
            yield j, k * count, pl.multiple_of((z ^ j) * rows + (me ^ m) * count, count), count


def key_bias(total, length):
    pos = lax.broadcasted_iota(jnp.int32, (1, total), 1)
    return jnp.where(pos < length, 0.0, masked_score).astype(f32)


def diag_mask(size):
    r = lax.broadcasted_iota(jnp.int32, (size, size), 0)
    c = lax.broadcasted_iota(jnp.int32, (size, size), 1)
    return c <= r


def attend_kernel(slots, masks, rows, blk, scal, *refs):
    pieces, outs = refs[:slots], refs[slots : 2 * slots]
    o32, lse, qkv, o16, sem = refs[2 * slots :]
    z, me, length = scal[0], scal[1], scal[2]
    total = slots * rows
    copies = []
    for t, (j, at, to, n) in enumerate(row_places(slots, masks, rows, z, me)):
        cp = pltpu.make_async_copy(pieces[j].at[pl.ds(at, n)], qkv.at[pl.ds(to, n)], sem.at[t])
        cp.start()
        copies.append(cp)
    bias = key_bias(total, length)
    causal = diag_mask(blk)
    for cp in copies:
        cp.wait()
    factor = HEAD_DIM**-0.5 * LOG2E
    for i in range(total // blk):
        lo = i * blk
        q = qkv[lo : lo + blk, :HEAD_DIM]
        s = dot_nt(q, qkv[lo : lo + blk, HEAD_DIM : 2 * HEAD_DIM]) * factor
        s = jnp.where(causal, s + bias[:, lo : lo + blk], masked_score)
        top = jnp.max(s, axis=1, keepdims=True)
        if i:
            before = dot_nt(q, qkv[:lo, HEAD_DIM : 2 * HEAD_DIM]) * factor + bias[:, :lo]
            top = jnp.maximum(top, jnp.max(before, axis=1, keepdims=True))
        p = jnp.exp2(s - top)
        mass = jnp.sum(p, axis=1, keepdims=True)
        acc = dot(p.astype(bf16), qkv[lo : lo + blk, 2 * HEAD_DIM :])
        if i:
            p = jnp.exp2(before - top)
            mass = mass + jnp.sum(p, axis=1, keepdims=True)
            acc = acc + dot(p.astype(bf16), qkv[:lo, 2 * HEAD_DIM :])
        acc = acc / mass
        o32[lo : lo + blk, :] = acc
        o16[lo : lo + blk, :] = acc.astype(bf16)
        lse[lo : lo + blk, :] = top + jnp.log(mass) * LOG2E
    copies = []
    for t, (j, at, to, n) in enumerate(row_places(slots, masks, rows, z, me)):
        cp = pltpu.make_async_copy(o16.at[pl.ds(to, n)], outs[j].at[pl.ds(at, n)], sem.at[t])
        cp.start()
        copies.append(cp)
    for cp in copies:
        cp.wait()


def attend(scal, pieces, masks):
    slots = len(pieces)
    rows = pieces[0].shape[0]
    total = slots * rows
    hbm = pl.BlockSpec(memory_space=pl.ANY)
    vmem = pl.BlockSpec(memory_space=pltpu.VMEM)
    out = pl.pallas_call(
        functools.partial(attend_kernel, slots, masks, rows, 256),
        out_shape=[jax.ShapeDtypeStruct((rows, HEAD_DIM), bf16)] * slots
        + [
            jax.ShapeDtypeStruct((total, HEAD_DIM), f32),
            jax.ShapeDtypeStruct((total, 1), f32),
        ],
        in_specs=[pl.BlockSpec(memory_space=pltpu.SMEM)] + [hbm] * slots,
        out_specs=[hbm] * slots + [vmem, vmem],
        scratch_shapes=[
            pltpu.VMEM((total, 3 * HEAD_DIM), bf16),
            pltpu.VMEM((total, HEAD_DIM), bf16),
            pltpu.SemaphoreType.DMA((slots * len(masks),)),
        ],
        cost_estimate=pl.CostEstimate(
            flops=total * total * HEAD_DIM * 4,
            bytes_accessed=total * HEAD_DIM * 12,
            transcendentals=total * total // 2,
        ),
        name="attend",
    )(scal, *pieces)
    return out[:slots], (out[slots], out[slots + 1])


def attend_back_kernel(slots, masks, rows, blk, micros, scal, *refs):
    pieces = [refs[m * slots : (m + 1) * slots] for m in range(micros)]
    refs = refs[micros * slots :]
    kept = [refs[2 * m : 2 * m + 2] for m in range(micros)]
    dos, outs = refs[2 * micros : 2 * micros + slots], refs[2 * micros + slots :][:slots]
    qkv, do, o32, lse, dkv, grad, sem = refs[2 * micros + 2 * slots :]
    micro = pl.program_id(0)
    z, me, length = scal[0], scal[1], scal[2 + micro]
    total = slots * rows
    runs = slots * len(masks)
    places = list(row_places(slots, masks, rows, z, me))
    base = micro * rows

    def incoming(m):
        out = []
        for t, (j, at, to, n) in enumerate(places):
            from_, to_ = pl.ds(at, n), pl.ds(to, n)
            out.append(pltpu.make_async_copy(pieces[m][j].at[from_], qkv.at[to_], sem.at[t]))
            far = pl.ds(pl.multiple_of(base + at, n), n)
            out.append(pltpu.make_async_copy(dos[j].at[far], do.at[to_], sem.at[runs + t]))
        out.append(pltpu.make_async_copy(kept[m][0], o32, sem.at[2 * runs]))
        out.append(pltpu.make_async_copy(kept[m][1], lse, sem.at[2 * runs + 1]))
        return out

    for m in range(micros):

        @pl.when(micro == m)
        def _(m=m):
            copies = incoming(m)
            for cp in copies:
                cp.start()
            for cp in copies:
                cp.wait()

    bias = key_bias(total, length)
    causal = diag_mask(blk)
    dkv[...] = jnp.zeros_like(dkv)
    scale = HEAD_DIM**-0.5
    factor = scale * LOG2E
    D = HEAD_DIM
    for i in range(total // blk):
        lo = i * blk
        q, dy = qkv[lo : lo + blk, :D], do[lo : lo + blk, :]
        delta = jnp.sum(dy.astype(f32) * o32[lo : lo + blk, :], axis=1, keepdims=True)
        level = lse[lo : lo + blk, :]
        dq = None
        for start, stop in ((lo, lo + blk), (0, lo)):
            if start == stop:
                continue
            keys, vals = qkv[start:stop, D : 2 * D], qkv[start:stop, 2 * D :]
            s = dot_nt(q, keys) * factor + bias[:, start:stop]
            if start == lo:
                s = jnp.where(causal, s, masked_score)
            p = jnp.exp2(s - level)
            ds = (p * (dot_nt(dy, vals) - delta)).astype(bf16)
            part = dot(ds, keys)
            dq = part if dq is None else dq + part
            dkv[start:stop, :D] += dot_t(ds, q)
            dkv[start:stop, D:] += dot_t(p.astype(bf16), dy)
        grad[lo : lo + blk, :D] = (dq * scale).astype(bf16)
    grad[:, D : 2 * D] = (dkv[:, :D] * scale).astype(bf16)
    grad[:, 2 * D :] = dkv[:, D:].astype(bf16)
    copies = []
    for t, (j, at, to, n) in enumerate(places):
        far = pl.ds(pl.multiple_of(base + at, n), n)
        cp = pltpu.make_async_copy(grad.at[pl.ds(to, n)], outs[j].at[far], sem.at[t])
        cp.start()
        copies.append(cp)
    for cp in copies:
        cp.wait()


def attend_back(scal, pieces, kept, dos, masks):
    micros, slots = len(pieces), len(dos)
    rows = dos[0].shape[0] // micros
    total = slots * rows
    hbm = pl.BlockSpec(memory_space=pl.ANY)
    return pl.pallas_call(
        functools.partial(attend_back_kernel, slots, masks, rows, 256, micros),
        out_shape=[jax.ShapeDtypeStruct((micros * rows, 3 * HEAD_DIM), bf16)] * slots,
        grid=(micros,),
        in_specs=[pl.BlockSpec(memory_space=pltpu.SMEM)] + [hbm] * ((micros + 1) * slots + 2 * micros),
        out_specs=[hbm] * slots,
        scratch_shapes=[
            pltpu.VMEM((total, 3 * HEAD_DIM), bf16),
            pltpu.VMEM((total, HEAD_DIM), bf16),
            pltpu.VMEM((total, HEAD_DIM), f32),
            pltpu.VMEM((total, 1), f32),
            pltpu.VMEM((total, 2 * HEAD_DIM), f32),
            pltpu.VMEM((total, 3 * HEAD_DIM), bf16),
            pltpu.SemaphoreType.DMA((2 * slots * len(masks) + 2,)),
        ],
        cost_estimate=pl.CostEstimate(
            flops=micros * total * total * HEAD_DIM * 10,
            bytes_accessed=micros * total * HEAD_DIM * 24,
            transcendentals=micros * total * total // 2,
        ),
        name="attend_back",
    )(scal, *[p for ps in pieces for p in ps], *[k for ks in kept for k in ks], *dos)


def mlp_back_kernel(n, *refs):
    grads, dw, gates, ups = refs[: 2 * n], refs[2 * n], refs[2 * n + 1 :][:n], refs[3 * n + 1 :][:n]
    tok, outs, tok_out = refs[4 * n + 1], refs[4 * n + 2 : 6 * n + 2], refs[6 * n + 2]
    w = dw[...]
    half = grads[0].shape[0]
    for i, x in enumerate(grads):
        m, t = i // 2, slice(i % 2 * half, (i % 2 + 1) * half)
        a = dot_nt(x[...], w)
        g, u = gates[m][t, :], ups[m][t, :]
        s = jax.nn.sigmoid(g)
        outs[m][t, :] = (a * u * s * (1.0 + g * (1.0 - s))).astype(bf16)
        outs[n + m][t, :] = (a * g * s).astype(bf16)
    tok_out[0] = tok[0]


def mlp_back(line, grads, down_weight, gates, ups):
    n = len(gates)
    half, width = grads[0].shape
    rows = 2 * half
    ff = down_weight.shape[0]
    t = min(ff, 256)
    tall = pl.BlockSpec((rows, t), lambda i: (0, i))
    smem = pl.BlockSpec(memory_space=pltpu.SMEM)
    full = jax.ShapeDtypeStruct((rows, ff), bf16)
    *out, line.token = pl.pallas_call(
        functools.partial(mlp_back_kernel, n),
        out_shape=[full] * (2 * n) + [jax.ShapeDtypeStruct((1,), jnp.int32)],
        grid=(ff // t,),
        in_specs=[pl.BlockSpec((half, width), lambda i: (0, 0))] * (2 * n)
        + [pl.BlockSpec((t, width), lambda i: (i, 0))]
        + [tall] * (2 * n)
        + [smem],
        out_specs=[tall] * (2 * n) + [smem],
        cost_estimate=pl.CostEstimate(
            flops=2 * n * rows * width * ff,
            bytes_accessed=2 * width * ff + n * (2 * rows * width + 12 * rows * ff),
            transcendentals=n * rows * ff,
        ),
        name="mlp_back",
    )(*grads, down_weight, *gates, *ups, line.token)
    return out[:n], out[n:]


def hidden_back_kernel(n, *refs):
    gate_grads, gw, up_grads, uw = refs[:n], refs[n], refs[n + 1 : 2 * n + 1], refs[2 * n + 1]
    tok, keep, send, tok_out = refs[2 * n + 2 :]
    g, u = gw[...], uw[...]
    half = keep.shape[1]
    for m in range(n):
        v = (dot_nt(gate_grads[m][...], g) + dot_nt(up_grads[m][...], u)).astype(bf16)
        keep[m] = v[:half, :]
        send[m] = v[half:, :]
    tok_out[0] = tok[0]


def hidden_back(line, gate_grads, gate_weight, up_grads, up_weight):
    n = len(gate_grads)
    rows, ff = gate_grads[0].shape
    width = gate_weight.shape[0]
    t = min(width, 256)
    all_ = pl.BlockSpec((rows, ff), lambda i: (0, 0), pipeline_mode=pl.Buffered(1))
    tile = pl.BlockSpec((t, ff), lambda i: (i, 0))
    smem = pl.BlockSpec(memory_space=pltpu.SMEM)
    half = jax.ShapeDtypeStruct((n, rows // 2, width), bf16)
    part = pl.BlockSpec((n, rows // 2, t), lambda i: (0, 0, i))
    keep, send, line.token = pl.pallas_call(
        functools.partial(hidden_back_kernel, n),
        out_shape=[half, half, jax.ShapeDtypeStruct((1,), jnp.int32)],
        grid=(width // t,),
        in_specs=[all_] * n + [tile] + [all_] * n + [tile, smem],
        out_specs=[part, part, smem],
        cost_estimate=pl.CostEstimate(
            flops=4 * n * rows * width * ff,
            bytes_accessed=4 * width * ff + n * (4 * rows * ff + 2 * rows * width),
            transcendentals=0,
        ),
        name="hidden_back",
    )(*gate_grads, gate_weight, *up_grads, up_weight, line.token)
    return keep, send


def turn_kernel(n, *refs):
    out, tok_out = refs[n + 1 :]
    at = 0
    for x in refs[:n]:
        out[:, at : at + x.shape[0]] = x[...].T
        at += x.shape[0]
    tok_out[0] = refs[n][0]


def turn(line, pieces, m=0, count=1):
    counts = [x.shape[0] // count for x in pieces]
    rows, cols = sum(counts), pieces[0].shape[1]
    t = min(cols, 512)
    smem = pl.BlockSpec(memory_space=pltpu.SMEM)
    out, line.token = pl.pallas_call(
        functools.partial(turn_kernel, len(pieces)),
        out_shape=[
            jax.ShapeDtypeStruct((cols, rows), pieces[0].dtype),
            jax.ShapeDtypeStruct((1,), jnp.int32),
        ],
        grid=(cols // t,),
        in_specs=[pl.BlockSpec((n, t), lambda i: (m, i)) for n in counts] + [smem],
        out_specs=[pl.BlockSpec((t, rows), lambda i: (i, 0)), smem],
        cost_estimate=pl.CostEstimate(flops=0, bytes_accessed=4 * rows * cols, transcendentals=0),
        name="turn",
    )(*pieces, line.token)
    return out


def gathered_attend(piece, pos, length):
    rows, local = piece.shape[0], piece.shape[1] // 3
    heads = local // HEAD_DIM
    q = piece[:, :local].reshape(rows, heads, HEAD_DIM)
    kv = lax.all_gather(piece[:, local:], SEQ, axis=0, tiled=True)
    n = kv.shape[0]
    k = kv[:, :local].reshape(n, heads, HEAD_DIM)
    v = kv[:, local:].reshape(n, heads, HEAD_DIM)
    base = jnp.arange(n // rows, dtype=jnp.int32) * rows
    own = pos - lax.axis_index(SEQ) * rows
    key_pos = (base[:, None] + own[None, :]).reshape(n)
    allowed = (key_pos[None, :] <= pos[:, None]) & (key_pos[None, :] < length)
    allowed = allowed[:, None, :]
    s = jnp.einsum(TO_KEYS, q, k, preferred_element_type=f32) * HEAD_DIM**-0.5
    s = jnp.where(allowed, s, masked_score)
    top = jnp.max(s, axis=-1, keepdims=True)
    w = jnp.where(allowed, jnp.exp(s - top), 0.0)
    mass = jnp.sum(w, axis=-1, keepdims=True)
    mixed = jnp.einsum(TO_ROWS, w.astype(bf16), v, preferred_element_type=f32) / mass
    return mixed.reshape(rows, local).astype(bf16), (q, k, v, allowed, mixed, top + jnp.log(mass))


def gathered_back(kept, dy):
    q, k, v, allowed, mixed, level = kept
    rows, heads, _ = q.shape
    n = k.shape[0]
    dy = dy.reshape(rows, heads, HEAD_DIM)
    scale = HEAD_DIM**-0.5
    delta = jnp.sum(dy.astype(f32) * mixed, axis=-1, keepdims=True)
    s = jnp.einsum(TO_KEYS, q, k, preferred_element_type=f32) * scale
    p = jnp.where(allowed, jnp.exp(s - level), 0.0)
    dp = jnp.einsum(TO_KEYS, dy, v, preferred_element_type=f32)
    ds = (p * (dp - delta)).astype(bf16)
    dq = jnp.einsum(TO_ROWS, ds, k, preferred_element_type=f32) * scale
    dk = jnp.einsum(TO_HEADS, ds, q, preferred_element_type=f32) * scale
    dv = jnp.einsum(TO_HEADS, p.astype(bf16), dy, preferred_element_type=f32)
    local = heads * HEAD_DIM
    dkv = jnp.concatenate([dk.reshape(n, local), dv.reshape(n, local)], axis=1).astype(bf16)
    dkv = lax.psum_scatter(dkv, SEQ, scatter_dimension=0, tiled=True)
    return jnp.concatenate([dq.reshape(rows, local).astype(bf16), dkv.astype(bf16)], axis=1)


class Line:
    def __init__(self, token):
        self.token = token
        self.waits = {}

    def add(self, *tasks):
        for t in tasks:
            self.waits[t] = next(t)[0]

    def mark(self, *arrays):
        for x in arrays:
            x = lax.slice(x, (0,) * x.ndim, (1,) * x.ndim).reshape(1)
            self.token = self.token + (x.astype(f32) > 3.4e38).astype(jnp.int32)

    def step(self, *tasks):
        tasks = [t for t in tasks if t in self.waits]
        if not tasks:
            return []
        held = [self.waits.pop(t) for t in tasks]
        if jax.tree.leaves(held):
            held, self.token = lax.optimization_barrier((held, self.token))
        for t, v in zip(tasks, held):
            try:
                self.waits[t], out = t.send(v)
            except StopIteration as end:
                out = end.value
            self.mark(*jax.tree.leaves(out)[:1])
        return [t for t in tasks if t in self.waits]


def idle(n):
    for _ in range(n):
        yield (), ()


class Place:
    def __init__(self, n_seq):
        self.n = n_seq
        self.dp, self.z = lax.axis_index(DP), lax.axis_index(SEQ)
        self.swap = [(0, 1), (1, 0)]
        self.lo, self.hi = n_seq // 2 - 1, n_seq // 2
        self.mid = [(self.lo, self.hi), (self.hi, self.lo)]
        self.inward = [
            [(i, i + 1), (n_seq - 1 - i, n_seq - 2 - i)] for i in range(n_seq // 2 - 1)
        ]

    def ends(self, pairs):
        return functools.reduce(jnp.logical_or, [self.z == b for _, b in pairs])


def take_half(x, dp, own):
    half = x.shape[1] // 2
    return lax.dynamic_slice_in_dim(x, (dp if own else 1 - dp) * half, half, 1)


def task_a(at, outs, which, x_send, x_keep, grad, cols, out_col):
    half = x_keep.shape[1]
    g = (yield grad, ())[:, cols]
    send = dot_t(x_send, g).astype(bf16)
    got = yield lax.ppermute(send, DP, at.swap), send
    s = (dot_t(x_keep, g) + got.astype(f32)).astype(bf16)
    for pairs in at.inward:
        got = yield lax.ppermute(s, SEQ, pairs), s
        s = add_low(s, got)
    got = yield lax.ppermute(s, SEQ, at.mid), s
    s = add_low(s, got)
    for pairs in reversed(at.inward):
        pairs = [(b, a) for a, b in pairs]
        got = yield lax.ppermute(s, SEQ, pairs), s
        s = jnp.where(at.ends(pairs), got, s)
    outs[which] = lax.dynamic_update_slice(outs[which], s.astype(f32), (at.dp * half, out_col))
    got = yield lax.ppermute(s, DP, at.swap), s
    outs[which] = lax.dynamic_update_slice(
        outs[which], got.astype(f32), ((1 - at.dp) * half, out_col)
    )
    return ()


def task_b(at, outs, which, x, grad, cols, out_col):
    g = (yield grad, ())[:, cols]
    s = dot_t(x, g).astype(bf16)
    for pairs in at.inward:
        got = yield lax.ppermute(s, SEQ, pairs), s
        s = add_low(s, got)
    h = s.shape[1] // 2
    first = at.z == at.lo
    send = jnp.where(first, s[:, h:], s[:, :h])
    keep = jnp.where(first, s[:, :h], s[:, h:])
    got = yield lax.ppermute(send, SEQ, at.mid), (send, keep)
    keep = add_low(keep, got)
    n = at.n
    pairs = [(d * n + k, (1 - d) * n + k) for d in (0, 1) for k in (at.lo, at.hi)]
    got = yield lax.ppermute(keep, (DP, SEQ), pairs), keep
    keep = add_low(keep, got)
    got = yield lax.ppermute(keep, SEQ, at.mid), keep
    s = jnp.concatenate([jnp.where(first, keep, got), jnp.where(first, got, keep)], axis=1)
    for pairs in reversed(at.inward):
        pairs = [(b, a) for a, b in pairs]
        got = yield lax.ppermute(s, SEQ, pairs), s
        s = jnp.where(at.ends(pairs), got, s)
    outs[which] = lax.dynamic_update_slice(outs[which], s.astype(f32), (0, out_col))
    return None


class Round:
    def __init__(self):
        self.refs, self.loads, self.keys = [], {}, {}

    def ref(self, array):
        for i, r in enumerate(self.refs):
            if r is array:
                return i
        self.refs.append(array)
        return len(self.refs) - 1

    def load(self, name, array, rows, cols=None):
        cols = (0, array.shape[1]) if cols is None else cols
        self.loads[name] = ((rows[1], cols[1]), ((self.ref(array), rows, cols, 0, 0),))

    def load_down(self, name, arrays, cols):
        n = arrays[0].shape[0]
        parts = tuple((self.ref(x), (0, n), cols, i * n, 0) for i, x in enumerate(arrays))
        self.loads[name] = ((n * len(arrays), cols[1]), parts)

    def load_across(self, name, arrays, rows):
        n = arrays[0].shape[1]
        parts = tuple((self.ref(x), rows, (0, n), 0, i * n) for i, x in enumerate(arrays))
        self.loads[name] = ((rows[1], n * len(arrays)), parts)


def first_row(first, count, dp):
    if isinstance(first, int):
        return first
    own, base = first
    return pl.multiple_of(base + (dp if own else 1 - dp) * count, count)


def round_kernel(kind, loads, n_in, pieces, extras, stores, scal, tok, *refs):
    ins = refs[:n_in]
    outs = refs[n_in + 1 : n_in + 1 + bool(pieces) + bool(extras) + len(stores)]
    refs[n_in][0] = tok[0]
    scratch = refs[n_in + 1 + len(outs) :]
    bufs = dict(zip([l[0] for l in loads], scratch))
    rest = list(scratch[len(loads) :])
    out_bufs = {}
    for name, _ in pieces + extras:
        out_bufs[name] = rest.pop(0)
    f_bufs = [rest.pop(0) for _ in stores]
    in_sem, out_sem = rest
    dp, z, n = scal[0], scal[1], scal[2]
    outer = (z == 0) | (z == n - 1)
    first = z == n // 2 - 1
    waits = {}
    t = 0
    for name, _, parts in loads:
        waits[name] = []
        for i, (r0, rows), (c0, cols), to_row, to_col in parts:
            src = ins[i].at[pl.ds(first_row(r0, rows, dp), rows), pl.ds(c0, cols)]
            dst = bufs[name].at[pl.ds(to_row, rows), pl.ds(to_col, cols)]
            cp = pltpu.make_async_copy(src, dst, in_sem.at[t])
            cp.start()
            waits[name].append(cp)
            t += 1

    def get(name):
        for cp in waits.pop(name, ()):
            cp.wait()
        return bufs[name]

    done = []
    slot = [0]

    def ship(src, dst):
        cp = pltpu.make_async_copy(src, dst, out_sem.at[slot[0]])
        slot[0] += 1
        cp.start()
        done.append(cp)

    where_out = {}
    k = 0
    for group in (pieces, extras):
        if group:
            at = 0
            for name, rows in group:
                where_out[name] = outs[k].at[pl.ds(at, rows)]
                at += rows
            k += 1

    def emit(name):
        if name in where_out:
            ship(out_bufs[name], where_out[name])

    def tiles(rows):
        t = min(rows, 256)
        return [slice(i, i + t) for i in range(0, rows, t)]

    have = lambda *names: all(n in bufs for n in names)
    low = lambda a, b: (a.astype(f32) + b.astype(f32)).astype(bf16)
    finals = {}
    if kind == "X":
        if have("a4r"):
            got, own, out = get("a4r"), get("a4o"), out_bufs["a4"]
            for t in tiles(out.shape[0]):
                out[t, :] = jnp.where(outer, got[t, :], own[t, :])
            emit("a4")
            finals["a4"] = out
        if have("b2r"):
            got, own, out = get("b2r"), get("b2o"), out_bufs["b2"]
            for t in tiles(out.shape[0]):
                out[t, :] = low(own[t, :], got[t, :])
            emit("b2")
        if have("a0g"):
            g, x, out = get("a0g"), get("a0x"), out_bufs["a0"]
            for t in tiles(out.shape[0]):
                out[t, :] = dot(x[t, :], g[...]).astype(bf16)
            emit("a0")
    if kind == "O":
        a_in, a_out = have("s1g"), have("s3r")
        if a_in:
            g, x, got, s1 = get("s1g"), get("s1x"), get("s1r"), out_bufs["s1"]
            for t in tiles(s1.shape[0]):
                s1[t, :] = (dot(x[t, :], g[...]) + got[t, :].astype(f32)).astype(bf16)
            emit("s1")
        if a_in or a_out:
            out = out_bufs["a"]
            n_in = s1.shape[0] if a_in else 0
            n_out = bufs["s3r"].shape[0] if a_out else 0
            if a_out:
                own, got = get("s3o"), get("s3r")
            for t in tiles(out.shape[0]):
                v = s1[t, :] if t.start < n_in else None
                if t.start < n_out:
                    u = low(own[t, :], got[t, :])
                    v = u if v is None else jnp.where(outer, v, u)
                out[t, :] = v
            emit("a")
        b_in, b_out = have("t0g"), have("t4r")
        if b_in:
            g, x, t0 = get("t0g"), get("t0x"), out_bufs["t0"]
            for t in tiles(t0.shape[0]):
                t0[t, :] = dot(x[t, :], g[...]).astype(bf16)
            emit("t0")
        if b_in or b_out:
            out = out_bufs["b"]
            n_in = t0.shape[0] if b_in else 0
            h = bufs["t4r"].shape[0] if b_out else 0
            if b_out:
                own, got = get("t4o"), get("t4r")
            for o in tiles(out.shape[0]):
                v = t0[o, :] if o.start < n_in else None
                if o.start < 2 * h:
                    back = h if o.start >= h else 0
                    t = slice(o.start - back, o.stop - back)
                    mine = jnp.logical_not(first) if back else first
                    u = jnp.where(mine, own[t, :], got[t, :])
                    v = u if v is None else jnp.where(outer, v, u)
                out[o, :] = v
            emit("b")
        if have("af"):
            finals["af"] = get("af")
    if kind == "M":
        if have("a2r"):
            own, got, out = get("a2o"), get("a2r"), out_bufs["a2"]
            for t in tiles(out.shape[0]):
                out[t, :] = low(own[t, :], got[t, :])
            emit("a2")
        if have("b3r"):
            own, got, out = get("b3o"), get("b3r"), out_bufs["b3"]
            for t in tiles(out.shape[0]):
                out[t, :] = low(own[t, :], got[t, :])
            emit("b3")
        if have("b1o"):
            own, got, out, keep = get("b1o"), get("ob"), out_bufs["b1"], out_bufs["keep"]
            h = out.shape[0]
            for t in tiles(h):
                o = slice(h + t.start, h + t.stop)
                top, bottom = low(own[t, :], got[t, :]), low(own[o, :], got[o, :])
                out[t, :] = jnp.where(first, bottom, top)
                keep[t, :] = jnp.where(first, top, bottom)
            emit("b1")
            emit("keep")
        if have("fino"):
            own, got = get("fino"), get("ob")
            finals["fin"] = (got, own)
    for i, (name, r0, rows, col) in enumerate(stores):
        src, buf = finals[name], f_bufs[i]
        for t in tiles(buf.shape[0]):
            if name == "fin":
                buf[t, :] = jnp.where(outer, src[0][t, :], src[1][t, :]).astype(f32)
            else:
                buf[t, :] = src[t, :].astype(f32)
        dst = outs[len(outs) - len(stores) + i]
        ship(buf, dst.at[pl.ds(first_row(r0, rows, dp), rows), pl.ds(col, buf.shape[1])])
    for cp in done:
        cp.wait()


class Rounds:
    def __init__(self, at, outs, line):
        self.at, self.outs, self.line = at, outs, line
        self.a, self.b = {}, {}
        self.got = {}
        self.r = 0
        self.swap_outer = [(0, 1), (1, 0), (2, 3), (3, 2)]
        self.scal = jnp.stack([at.dp, at.z, jnp.int32(at.n)]).astype(jnp.int32)

    def piece(self, kind, r, name, own=False, some=None):
        sent, got, table = self.got[kind, r]
        at = 0
        for k, rows in table:
            if k == name:
                return (sent if own else got), (at, rows if some is None else some)
            at += rows

    def run(self, kind, b, pieces, extras, stores, flops):
        rows = {n: r for n, r in pieces + extras}
        w = self.width
        loads = tuple((k,) + v for k, v in b.loads.items())
        any_ = pl.BlockSpec(memory_space=pl.ANY)
        smem = pl.BlockSpec(memory_space=pltpu.SMEM)
        shapes, aliases = [jax.ShapeDtypeStruct((1,), jnp.int32)], {}
        if pieces:
            shapes.append(jax.ShapeDtypeStruct((sum(r for _, r in pieces), w), bf16))
        if extras:
            shapes.append(jax.ShapeDtypeStruct((sum(r for _, r in extras), w), bf16))
        for which, *_ in stores:
            aliases[2 + len(b.refs) + len(aliases)] = len(shapes)
            shapes.append(jax.ShapeDtypeStruct(self.outs[which].shape, f32))
        scratch = [pltpu.VMEM(shape, bf16) for _, shape, _ in loads]
        scratch += [pltpu.VMEM((rows[n], w), bf16) for n, _ in pieces + extras]
        scratch += [pltpu.VMEM((r, w), f32) for _, _, _, r, _ in stores]
        n_out = len(pieces) + len(extras) + len(stores)
        n_load = sum(len(parts) for _, _, parts in loads)
        scratch += [pltpu.SemaphoreType.DMA((n_load,)), pltpu.SemaphoreType.DMA((n_out,))]
        moved = sum(m * n * 2 for _, (m, n), _ in loads) + sum(rows.values()) * w * 2
        moved += sum(r * w * 4 for _, _, _, r, _ in stores)
        n_in = len(b.refs) + len(stores)
        out = pl.pallas_call(
            functools.partial(
                round_kernel, kind, loads, n_in, tuple(pieces), tuple(extras),
                tuple(s[1:] for s in stores),
            ),
            out_shape=shapes,
            in_specs=[smem, smem] + [any_] * n_in,
            out_specs=[smem] + [any_] * (len(shapes) - 1),
            input_output_aliases=aliases,
            scratch_shapes=scratch,
            cost_estimate=pl.CostEstimate(flops=flops, bytes_accessed=moved, transcendentals=0),
            name="round_" + kind.lower(),
        )(self.scal, self.line.token, *b.refs, *[self.outs[s[0]] for s in stores])
        self.line.token, *out = out
        for which, *_ in reversed(stores):
            self.outs[which] = out.pop()
        extra = out.pop() if extras else None
        if pieces:
            axis, pairs = {
                "X": (DP, self.at.swap), "O": (SEQ, self.swap_outer), "M": (SEQ, self.at.mid),
            }[kind]
            self.got[kind, self.r] = (out[0], lax.ppermute(out[0], axis, pairs), pieces)
        return extra

    def step_x(self):
        r, A, B = self.r, self.a, self.b
        b, pieces, stores, flops = Round(), [], [], 0
        if r in A:
            c = A[r]
            half, tok = c["rows"][1] // 2, sum(x.shape[1] for x in c["x"])
            b.load_down("a0g", c["grad"], c["cols"])
            b.load_across("a0x", c["x"], ((False, c["rows"][0]), half))
            pieces.append(("a0", half))
            flops += 2 * half * tok * c["cols"][1]
        if r - 6 in A:
            c = A[r - 6]
            rows = c["rows"][1] // 2
            b.load("a4r", *self.piece("O", r - 2, "a", False, rows))
            b.load("a4o", *self.piece("O", r - 2, "a", True, rows))
            pieces.append(("a4", rows))
            stores.append((c["which"], "a4", (True, c["rows"][0]), rows, c["col"]))
        if r - 3 in B:
            c = B[r - 3]
            b.load("b2r", *self.piece("M", r - 2, "b1"))
            b.load("b2o", *c["keep"])
            pieces.append(("b2", b.loads["b2r"][0][0]))
        if pieces:
            self.run("X", b, pieces, [], stores, flops)

    def step_o(self):
        r, A, B = self.r, self.a, self.b
        b, pieces, extras, stores, flops = Round(), [], [], [], 0
        if r - 1 in A:
            c = A[r - 1]
            half, tok = c["rows"][1] // 2, sum(x.shape[1] for x in c["x"])
            b.load_down("s1g", c["grad"], c["cols"])
            b.load_across("s1x", c["x"], ((True, c["rows"][0]), half))
            b.load("s1r", *self.piece("X", r - 1, "a0"))
            extras.append(("s1", half))
            flops += 2 * half * tok * c["cols"][1]
        if r - 4 in A:
            b.load("s3o", *self.piece("M", r - 2, "a2", True))
            b.load("s3r", *self.piece("M", r - 2, "a2"))
        if r - 1 in A or r - 4 in A:
            sizes = [A[k]["rows"][1] // 2 for k in (r - 1, r - 4) if k in A]
            pieces.append(("a", max(sizes)))
        if r in B:
            c = B[r]
            rows, tok = c["rows"][1], sum(x.shape[1] for x in c["x"])
            b.load_down("t0g", c["grad"], c["cols"])
            b.load_across("t0x", c["x"], c["rows"])
            extras.append(("t0", rows))
            flops += 2 * rows * tok * c["cols"][1]
        if r - 6 in B:
            b.load("t4o", *self.piece("M", r - 2, "b3", True))
            b.load("t4r", *self.piece("M", r - 2, "b3"))
        if r in B or r - 6 in B:
            pieces.append(("b", max(B[k]["rows"][1] for k in (r, r - 6) if k in B)))
        if r - 7 in A:
            c = A.pop(r - 7)
            b.load("af", *self.piece("X", r - 1, "a4"))
            first = (False, c["rows"][0])
            stores.append((c["which"], "af", first, b.loads["af"][0][0], c["col"]))
        if pieces or stores:
            extra = self.run("O", b, pieces, extras, stores, flops)
            at = 0
            for name, n in extras:
                (A[r - 1] if name == "s1" else B[r])[name] = (extra, (at, n))
                at += n

    def step_m(self):
        r, A, B = self.r, self.a, self.b
        b, pieces, extras, stores = Round(), [], [], []
        if r - 2 in A:
            rows = A[r - 2]["rows"][1] // 2
            b.load("a2o", *A[r - 2]["s1"])
            b.load("a2r", *self.piece("O", r - 1, "a", False, rows))
            pieces.append(("a2", rows))
        if r - 1 in B or r - 7 in B:
            b.load("ob", *self.piece("O", r - 1, "b"))
        if r - 1 in B:
            h = B[r - 1]["rows"][1] // 2
            b.load("b1o", *B[r - 1]["t0"])
            pieces.append(("b1", h))
            extras.append(("keep", h))
        if r - 4 in B:
            b.load("b3o", *self.piece("X", r - 1, "b2", True))
            b.load("b3r", *self.piece("X", r - 1, "b2"))
            pieces.append(("b3", b.loads["b3r"][0][0]))
        if r - 7 in B:
            c = B.pop(r - 7)
            b.load("fino", *self.piece("O", r - 1, "b", True, c["rows"][1]))
            stores.append((c["which"], "fin", c["rows"][0], c["rows"][1], c["col"]))
        if pieces or stores:
            extra = self.run("M", b, pieces, extras, stores, 0)
            if extras:
                B[r - 1]["keep"] = (extra, (0, h))


def blank_kernel(*outs):
    pass


def blanks(shapes):
    return pl.pallas_call(
        blank_kernel,
        out_shape=[jax.ShapeDtypeStruct(s, f32) for s in shapes],
        out_specs=[pl.BlockSpec(memory_space=pl.ANY)] * len(shapes),
    )()


def gather_steps(x, n, axis=0, wait=0):
    got = None
    for b in reversed(bits_of(n)):
        if got is not None:
            x = jnp.concatenate([x, got], axis=axis)
        got = lax.ppermute(x, MP, xor_perm(n, b))
        if wait:
            yield (), x
            yield from idle(wait - 1)
            got = yield got, ()
        else:
            got = yield got, x
    return [x, got]


def joined(pieces, axis=0):
    return jnp.concatenate(pieces, axis=axis)


def scatter_steps(x, n, axis=0, wait=0):
    for b in bits_of(n):
        if isinstance(x, tuple):
            keep, send = x
        else:
            half = x.shape[axis] // 2
            keep = lax.slice_in_dim(x, 0, half, axis=axis)
            send = lax.slice_in_dim(x, half, 2 * half, axis=axis)
        got = lax.ppermute(send, MP, xor_perm(n, b))
        if wait:
            yield (), (send, keep)
            yield from idle(wait - 1)
            got = yield got, ()
        else:
            got = yield got, (send, keep)
        x = keep.astype(f32) + got.astype(f32)
        if 2 * b < n:
            x = x.astype(bf16)
    return x.astype(f32)


def sum_rows_steps(x, n):
    masks = row_masks(n)
    for b in bits_of(n):
        got = yield lax.ppermute(x, MP, xor_perm(n, b)), x
        got = got.reshape(x.shape[:-1] + (n, -1))
        order = [masks.index(m ^ b) for m in masks]
        got = jnp.stack([got[..., k, :] for k in order], axis=-2)
        x = x + got.reshape(x.shape)
    return x


def exchange_steps(pieces, n):
    got = yield exchange(pieces, n)[1:], pieces[1:]
    return [pieces[0]] + list(got)


class Layer:
    pass


def forward_task(c, m):
    f = c.fwd[m]
    own = c.tokens[m]
    length = c.lengths[m, 0]
    x = f.x = yield from gather_steps(own, c.n_mp)
    proj = dot(joined(x), c.qkv_weight)
    local = c.local
    squares = jnp.stack(
        [jnp.sum(jnp.square(proj[:, t * local : (t + 1) * local]), axis=1) for t in (0, 1)], axis=0
    )
    squares = yield from sum_rows_steps(squares, c.n_mp)
    inv = lax.rsqrt(squares / c.width + epsilon).T
    pieces = rope_call(c.slots, c.z_arr, proj, inv, c.cos, c.sin, c.qg, c.kg)
    if c.by_heads:
        scal = jnp.stack([c.z, c.me, length]).astype(jnp.int32)
        f.pieces = yield from exchange_steps(pieces, c.n_seq)
        mixed, f.kept = attend(scal, f.pieces, c.masks)
        mixed = yield from exchange_steps(mixed, c.n_seq)
        mixed = join_heads(c.z_arr, mixed)
    else:
        mixed, f.kept = gathered_attend(pieces[0], c.pos, length)
    attended = yield from scatter_steps(dot(mixed, c.o_weight).astype(bf16), c.n_mp)
    attn_inv = inv_rms(attended)
    hidden = own.astype(f32) + attended * attn_inv * c.attn_gain
    mlp_in = yield from gather_steps(hidden.astype(bf16), c.n_mp)
    f.mlp_in = mlp_in
    rows_in = joined(mlp_in)
    f.gate, f.up = dot(rows_in, c.gate_weight), dot(rows_in, c.up_weight)
    f.act = (f.gate * jax.nn.sigmoid(f.gate) * f.up).astype(bf16)
    mlp_out = yield from scatter_steps(dot(f.act, c.down_weight).astype(bf16), c.n_mp)
    mlp_inv = inv_rms(mlp_out)
    f.layer = (hidden + mlp_out * mlp_inv * c.mlp_gain).astype(bf16)
    f.seeds = c.cotangent[m].astype(f32) * (c.own_pos < length).astype(f32)[:, None]
    mlp_grad, gain_rows = norm_backward(mlp_out, mlp_inv, c.mlp_gain, f.seeds)
    f.mlp_gain = jnp.sum(gain_rows, axis=0)
    f.mlp_grad = yield from gather_steps(mlp_grad.astype(bf16), c.n_mp)
    f.proj, f.inv, f.mixed, f.attended, f.attn_inv = proj, inv, mixed, attended, attn_inv
    return ()


def backward_task(c):
    n, rows, fwd = len(c.fwd), c.rows, c.fwd
    yield (), ()
    gates = mlp_back(
        c.line, [x for f in fwd for x in f.mlp_grad], c.down_weight, [f.gate for f in fwd], [f.up for f in fwd]
    )
    for f, f.gate_grad, f.up_grad in zip(fwd, *gates):
        pass
    yield (), ()
    back = hidden_back(c.line, gates[0], c.gate_weight, gates[1], c.up_weight)
    back = yield from scatter_steps(back, c.n_mp, 1, c.far)
    hidden_grad, attn_grad = [], []
    for m, f in enumerate(fwd):
        hidden_grad.append(f.seeds + back[m])
        e, gain_rows = norm_backward(f.attended, f.attn_inv, c.attn_gain, hidden_grad[m])
        f.attn_gain = jnp.sum(gain_rows, axis=0)
        attn_grad.append(e.astype(bf16))
    attn_grad = yield from gather_steps(jnp.stack(attn_grad), c.n_mp, 1, c.far)
    c.attn_grad = [x.reshape(-1, c.width) for x in attn_grad]
    dy = [dot_nt(x, c.o_weight).astype(bf16).reshape(n, -1, c.local) for x in c.attn_grad]
    dy = joined(dy, 1).reshape(n * rows, c.local)
    if not c.rounds:
        c.attn_grad_all = joined(attn_grad, 1).reshape(n * rows, c.width)
    if c.by_heads:
        dys = split_heads(c.z_arr, dy, c.slots)
        dys = yield from exchange_steps(dys, c.n_seq)
        scal = jnp.concatenate([jnp.stack([c.z, c.me]), c.lengths[:, 0]]).astype(jnp.int32)
        grads = attend_back(scal, [f.pieces for f in fwd], [f.kept for f in fwd], dys, c.masks)
        grads = yield from exchange_steps(grads, c.n_seq)
    else:
        grads = [gathered_back(f.kept, dy[m * rows : (m + 1) * rows]) for m, f in enumerate(fwd)]
        grads = [jnp.concatenate(grads, axis=0)]
    tables = (c.cos, c.sin, c.qg, c.kg)
    cross = []
    for m, f in enumerate(fwd):
        e, f.gains = cross_call(c.slots, m, c.z_arr, grads, f.proj, f.inv, *tables)
        cross.append(e.T)
    cross = yield from sum_rows_steps(jnp.concatenate(cross, axis=0), c.n_mp)
    for m, f in enumerate(fwd):
        e = cross[2 * m : 2 * m + 2].T
        f.qkv_grad = raw_call(
            c.slots, c.width, m, c.z_arr, grads, f.proj, f.inv, e, *tables
        )
    yield (), [f.qkv_grad for f in fwd]
    back = jnp.stack([dot_nt(f.qkv_grad, c.qkv_weight).astype(bf16) for f in fwd])
    back = yield from scatter_steps(back, c.n_mp, 1, c.far)
    c.input_grad = jnp.stack(hidden_grad) + back
    return c.input_grad


def turning_task(c):
    yield (), ()
    c.attn_grad_t = []
    for m in range(len(c.fwd)):
        c.attn_grad_t.append(turn(c.line, c.attn_grad, m, len(c.fwd)))
        yield (), ()


def gains_task(c):
    yield (), ()
    gains = sum(f.gains for f in c.fwd)
    gains = lax.dynamic_update_slice(jnp.zeros((2, c.width), f32), gains, (0, c.me * c.local))
    gains = jnp.concatenate(
        [gains, sum(f.attn_gain for f in c.fwd)[None], sum(f.mlp_gain for f in c.fwd)[None]], axis=0
    )
    for name, n in ((MP, c.n_mp), (SEQ, c.n_seq), (DP, c.n_dp)):
        for b in bits_of(n):
            got = lax.ppermute(gains, name, xor_perm(n, b))
            got = yield got, gains
            gains = gains + got
    c.gains = gains
    return gains


def per_device(
    n_dp, n_seq, n_mp,
    tokens, lengths, cotangent, q_weight, k_weight, v_weight, o_weight, q_gain, k_gain,
    attn_gain, gate_weight, up_weight, down_weight, mlp_gain,
):
    c = Layer()
    micros, own_rows, width = tokens.shape
    rows = own_rows * n_mp
    local = q_weight.shape[1]
    heads = local // HEAD_DIM
    ff = gate_weight.shape[1]
    me, z = lax.axis_index(MP), lax.axis_index(SEQ)
    c.tokens, c.lengths, c.cotangent, c.o_weight = tokens, lengths, cotangent, o_weight
    c.gate_weight, c.up_weight, c.down_weight = gate_weight, up_weight, down_weight
    c.attn_gain, c.mlp_gain = attn_gain, mlp_gain
    c.n_dp, c.n_seq, c.n_mp, c.rows, c.width, c.local = n_dp, n_seq, n_mp, rows, width, local
    c.me, c.z, c.masks = me, z, row_masks(n_mp)
    c.by_heads = heads == n_seq
    c.slots = n_seq if c.by_heads else 1
    c.z_arr = z.astype(jnp.int32).reshape(1)
    c.qkv_weight = jnp.concatenate([q_weight, k_weight, v_weight], axis=1)
    c.qg = lax.dynamic_slice_in_dim(q_gain, me * local, local)[None]
    c.kg = lax.dynamic_slice_in_dim(k_gain, me * local, local)[None]
    block = jnp.asarray(c.masks, jnp.int32) ^ me
    steps = jnp.arange(own_rows, dtype=jnp.int32)
    c.pos = z * rows + (block[:, None] * own_rows + steps).reshape(-1)
    c.own_pos = z * rows + me * own_rows + steps
    frequency = rope_base ** (-(jnp.arange(HALF, dtype=f32) * 2.0 / HEAD_DIM))
    angles = c.pos.astype(f32)[:, None] * frequency[None, :]
    cos, sin = jnp.cos(angles), jnp.sin(angles)
    c.cos = jnp.concatenate([cos, cos], axis=1)
    c.sin = jnp.concatenate([-sin, sin], axis=1)
    c.fwd = [Layer() for _ in range(micros)]

    at = Place(n_seq)
    c.rounds = rounds = n_seq == 4
    line = c.line = Line(jnp.zeros((1,), jnp.int32))
    fw = [forward_task(c, m) for m in range(micros)]
    line.add(*fw)
    def turned(m, name):
        f = c.fwd[m]
        rows_ = getattr(f, name)
        setattr(f, name + "_t", turn(line, rows_ if isinstance(rows_, list) else [rows_]))

    extra = {"a": (0, "x"), "b": (1, "x"), "c": (0, "act"), "d": (1, "act"), "e": (0, "mlp_in"), "f": (1, "mlp_in")}
    order = ORDER if (micros, n_mp, c.by_heads) == (2, 4, True) and rounds else ""
    for act in order:
        if act in extra:
            turned(*extra[act])
        else:
            line.step(fw[int(act)])
    while any(t in line.waits for t in fw):
        for t in fw:
            line.step(t)

    c.far = 0
    each = lambda name: [getattr(f, name) for f in c.fwd]
    outs = list(blanks(
        [(ff, width), (width, ff), (width, ff)]
        + [(width, local)] * 3
        + [(width, local) if rounds else (local, width)]
    ))
    back, gains = backward_task(c), gains_task(c)
    side = []
    line.add(back)

    stack = lambda lists: [x for pieces in lists for x in pieces]
    both = lambda name: jnp.concatenate(each(name), axis=0)
    both2 = lambda name: jnp.concatenate(stack(each(name)), axis=0)

    def work(key):
        if rounds:
            return {
                "down": lambda: (each("act_t"), stack(each("mlp_grad"))),
                "gate": lambda: (each("mlp_in_t"), each("gate_grad")),
                "up": lambda: (each("mlp_in_t"), each("up_grad")),
                "o": lambda: (c.attn_grad_t, each("mixed")),
                "qkv": lambda: (each("x_t"), each("qkv_grad")),
            }[key]()
        return {
            "down": lambda: (both("act"), both2("mlp_grad")),
            "gate": lambda: (both2("mlp_in"), both("gate_grad")),
            "up": lambda: (both2("mlp_in"), both("up_grad")),
            "o": lambda: (both("mixed"), c.attn_grad_all),
            "qkv": lambda: (both2("x"), both("qkv_grad")),
        }[key]()

    done, live = {}, []
    if rounds:
        reducer = Rounds(at, outs, line)
        reducer.width = local // 2

    def rows_of(key):
        if key not in done:
            done[key] = work(key)
        return done[key]

    def one_round(new_a, new_b, script=""):
        if rounds:
            for new, table in ((new_a, reducer.a), (new_b, reducer.b)):
                if new is not None:
                    key, which, first, n, col, span = new
                    x, grad = rows_of(key)
                    table[reducer.r] = dict(
                        x=x, grad=grad, cols=(first, n), which=which, col=col, rows=span
                    )
            for act in script:
                if act in "XOM":
                    getattr(reducer, "step_" + act.lower())()
                else:
                    line.step({"c": back, "t": turning, "g": gains}[act])
            reducer.r += 1
            return
        for new, kind in ((new_a, "a"), (new_b, "b")):
            if new is not None:
                key, which, first, n, col, _ = new
                x, grad = rows_of(key)
                if kind == "a":
                    if key + "/" not in done:
                        done[key + "/"] = (take_half(x, at.dp, False), take_half(x, at.dp, True))
                    t = task_a(at, outs, which, *done[key + "/"], grad, slice(first, first + n), col)
                else:
                    t = task_b(at, outs, which, x, grad, slice(first, first + n), col)
                line.add(t)
                live.append(t)
        live[:] = line.step(*live)
        for t in side:
            line.step(t)

    unit = local // 2
    cut = lambda key, which, n, u=unit, first=0, parts=1: [
        (key, which, first + t, u, t, (k * (width // parts), width // parts))
        for t in range(0, n, u)
        for k in range(parts)
    ]
    ready = {
        "down": lambda: True,
        "gate": lambda: all(hasattr(f, "up_grad") for f in c.fwd),
        "o": lambda: len(c.attn_grad_t) == micros if rounds else hasattr(c, "attn_grad_all"),
        "qkv": lambda: all(hasattr(f, "qkv_grad") for f in c.fwd),
    }
    ready["up"] = ready["gate"]
    todo = cut("down", 0, width) + cut("gate", 1, ff) + cut("up", 2, ff)
    todo += cut("o", 6, local) if rounds else cut("o", 6, width, width // 2)
    for t in range(3):
        todo += cut("qkv", 3 + t, local, first=t * local, parts=1)
    c.attn_grad_t = []
    if rounds:
        for m in range(micros):
            for name in ("x", "act", "mlp_in"):
                if not hasattr(c.fwd[m], name + "_t"):
                    turned(m, name)
        turning = turning_task(c)
        line.add(turning)
    else:
        side = [back]
    count_a = (len(todo) * 5) // 8

    def take():
        for i, chunk in enumerate(todo):
            if ready[chunk[0]]():
                return todo.pop(i)
        return None

    gains_on = False
    r = taken_a = 0
    while todo or any(t in line.waits for t in (back, gains)) or (
        reducer.a or reducer.b if rounds else live
    ):
        late = ready["qkv"]()
        if late and not gains_on and not (rounds and todo):
            gains_on = True
            side.append(gains)
            line.add(gains)
        new_a = take() if taken_a < count_a else None
        taken_a += new_a is not None
        script = SCRIPT[r] if r < len(SCRIPT) else "XgOcMg"
        lone = rounds and r < len(SCRIPT) and script[-1:] == "-"
        new_b = None if lone else take()
        one_round(new_a, new_b, script.strip("-") if rounds else "")
        r += 1
    return (
        jnp.stack(each("layer")),
        c.input_grad,
        outs[3],
        outs[4],
        outs[5],
        outs[6].T if rounds else outs[6],
        c.gains[0],
        c.gains[1],
        c.gains[2],
        outs[1],
        outs[2],
        outs[0],
        c.gains[3],
    )


SCRIPT = (
    "XOc",
    "XcOM",
    "XcOM",
    "XcOM",
    "XOcM",
    "XOcM",
    "XOMc",
    "XOtMtc",
    "XOcM",
    "XcOMc",
    "XOMc",
)

ORDER = "00001111ab00010101010ce1101d0f1011"


def solution(mesh):
    n_dp, n_seq, n_mp = (mesh.shape[a] for a in (DP, SEQ, MP))
    assert n_dp == 2
    rows = P(None, (DP, SEQ, MP), None)
    cols, flat, all_ = P(None, MP), P(MP, None), P()
    return jax.shard_map(
        functools.partial(per_device, n_dp, n_seq, n_mp),
        mesh=mesh,
        in_specs=(rows, P(None, DP), rows, cols, cols, cols, flat, all_, all_, all_, cols, cols, flat, all_),
        out_specs=(rows, rows, cols, cols, cols, flat, all_, all_, all_, cols, cols, flat, all_),
        check_vma=False,
    )
```
